256 devices in a mesh: section: 8 (over y, z_hi), expert: 32 (over x, z_lo, core).
Axes of the slice: x: 4, y: 4, z: 8 (z_hi: 2, z_lo: 4; z = z_hi * 4 + z_lo), core: 2. Of those that a mesh axis runs over, the one named last changes fastest.
Arguments:
- embedded: bfloat16 [4096, 3584], P('expert'), may hold values from -6 to 6
- forward_held: bfloat16 [8, 4096, 3584], P('section', 'expert'), may hold values from -6 to 6
- forward_route: int32 [8, 4096, 1], P('section', 'expert'), may hold values from 0 to 7; in each aligned block of 128 rows (0 to 127, 128 to 255, ..., all dimensions but the last counted through in order) at most 24 rows name the same one
- forward_weight: float32 [8, 4096], P('section', 'expert'), may hold values from 0.2 to 1
- loss_cotangent: bfloat16 [4096, 3584], P('expert'), may hold values from -6 to 6
- backward_held: bfloat16 [8, 4096, 3584], P('section', 'expert'), may hold values from -6 to 6
- backward_route: int32 [8, 4096, 1], P('section', 'expert'), may hold values from 0 to 7; in each aligned block of 128 rows (0 to 127, 128 to 255, ..., all dimensions but the last counted through in order) at most 24 rows name the same one
- backward_weight: float32 [8, 4096], P('section', 'expert'), may hold values from 0.2 to 1
- saved_gate: bfloat16 [8, 768, 8192], P('section', None, 'expert'), may hold values from -6 to 6
- saved_up: bfloat16 [8, 768, 8192], P('section', None, 'expert'), may hold values from -6 to 6
- gate_weight: bfloat16 [8, 3584, 8192], P('section', None, 'expert'), may hold values from -0.09375 to 0.09375
- up_weight: bfloat16 [8, 3584, 8192], P('section', None, 'expert'), may hold values from -0.09375 to 0.09375
- down_weight: bfloat16 [8, 8192, 3584], P('section', 'expert'), may hold values from -0.1875 to 0.1875
- steering: float32 [8, 3584], P('section'), may hold values from -6 to 6
Outputs:
- forward_out: bfloat16 [8, 4096, 3584], P('section', 'expert')
- forward_coefficient: float32 [8, 4096], P('section', 'expert')
- backward_out: bfloat16 [8, 4096, 3584], P('section', 'expert')
The draws below stay inside these ranges and needn't reach their ends.
Inputs may be any that keep to these rules, and one draw needn't show every extreme that they name: `forward_route`: in each aligned block of 128 tokens of a layer (the tokens of one device) no expert is chosen more than 24 times, and some expert is chosen exactly 24 times in some block. `backward_route`: in each aligned block of 128 tokens of a layer (the tokens of one device) no expert is chosen more than 24 times, and some expert is chosen exactly 24 times in some block.
All inputs are finite; a program needn't handle non-finite values.
Results may differ from the reference program's by a relative error of at most 0.0058.
Values may be sent and summed in bfloat16 or wider, within the bound.
A program may use at most 64 MiB of HBM per device.

```python
import math
import jax
import jax.numpy as jnp
import numpy as np
from jax import lax

D = 3584
H = 1024
HDEV = 256
TOK_DEV = 128
EXPERTS = 8
CAP = 24
MB_TOK = 4096
N_SECTION = 8
N_EXPERT = 32


def shard_levels(stream_key, dims, cuts, smallest, top_value):
    factor_of, own = 1.0, jax.random.fold_in(stream_key, 6)
    for axis_at, parts in cuts:
        draws = jnp.exp(jax.random.uniform(jax.random.fold_in(own, axis_at), (parts,), jnp.float32, smallest / len(cuts), top_value / len(cuts)))
        factor_of = factor_of * jnp.repeat(draws, dims[axis_at] // parts).reshape([-1 if axis == axis_at else 1 for axis in range(len(dims))])
    return factor_of


def shared_out(stream_key, own, number, rows, count, top, bound, skew):
    ranking = jax.random.permutation(stream_key, count)
    crowded, usual = portions_of(count, rows * top, bound, skew, True), portions_of(count, rows * top, bound, skew, False)
    places = jnp.arange(count)

    def named(tallies, rotation):
        used = int((tallies > 0).sum())
        fixed = max(1, used // 4)
        shifted = fixed + (places - fixed + rotation * (used - fixed)) % max(1, count - fixed)
        return jnp.zeros((count,), jnp.int32).at[ranking[jnp.where(places < fixed, places, shifted)]].set(jnp.asarray(tallies, jnp.int32))

    tallies = jnp.where(number % 4 == 0, named(crowded, number // 4), named(usual, number - number // 4 - 1))
    mixed = jax.random.permutation(jax.random.fold_in(own, 3), count)
    donor, taker = mixed[0:count // 2 * 2:2], mixed[1:count // 2 * 2:2]
    slack = jnp.minimum(tallies[donor] - 1, bound - tallies[taker]) // 2
    slack = jnp.where((donor == ranking[0]) | (taker == ranking[0]) | (tallies[taker] == 0), 0, jnp.maximum(slack, 0))
    shifted = jax.random.randint(jax.random.fold_in(own, 4), (count // 2,), 0, 1 << 20) % (slack + 1)
    tallies = tallies.at[donor].add(-shifted).at[taker].add(shifted)
    items = jnp.searchsorted(jnp.cumsum(tallies), jnp.arange(rows * top), side="right").astype(jnp.int32)
    table = items.reshape(top, rows).T
    table = table[jax.random.permutation(jax.random.fold_in(own, 1), rows)]
    rotation = jax.random.randint(jax.random.fold_in(own, 2), (rows, 1), 0, top)
    return jnp.take_along_axis(table, (jnp.arange(top)[None, :] + rotation) % top, axis=1)


def portions_of(count, total, bound, slope, full):
    portions = [(1 << 20) // math.isqrt(standing ** slope) + 1 for standing in range(1, count + 1)]
    largest = bound if full else min(bound, max(-(-total // count), total * portions[0] // sum(portions)))
    least = 1 if total - largest >= count - 1 else 0
    given, spare = [largest] + [least] * (count - 1), total - largest - least * (count - 1)
    while spare > 0:
        free = [i for i in range(1, count) if given[i] < largest] or [i for i in range(1, count) if given[i] < bound]
        whole, left = sum([portions[i] for i in free]), spare
        for i in free:
            addition = min(bound - given[i], max(1, left * portions[i] // whole), spare)
            given[i] = given[i] + addition
            spare = spare - addition
    return np.array(given)


def scatter_about(own_key, shape, width, most, shards=(), kind=jnp.bfloat16):
    result = width * jax.random.normal(own_key, shape, jnp.float32)
    if shards:
        result = result * shard_levels(own_key, shape, shards, -0.22, 0.18)
    return jnp.clip(result, -most, most).astype(kind)


def setup_inputs(seed: int = 0) -> dict:
    arg_keys = jax.random.split(jax.random.key(seed), 15)
    embedded = scatter_about(arg_keys[0], (MB_TOK, D), 1.0, 6.0, ((0, 32),))
    forward_held = scatter_about(arg_keys[1], (N_SECTION, MB_TOK, D), 1.0, 6.0, ((0, 8), (1, 32)))
    forward_route_keys = jax.random.split(jax.random.fold_in(arg_keys[2], 1), N_SECTION * MB_TOK // TOK_DEV)
    forward_route_turns = jax.random.permutation(jax.random.fold_in(arg_keys[2], 3), N_SECTION * MB_TOK // TOK_DEV)
    forward_route = jax.vmap(lambda own, number: shared_out(jax.random.fold_in(arg_keys[2], 2), own, number, TOK_DEV, EXPERTS, 1, CAP, 2))(forward_route_keys, forward_route_turns).reshape((N_SECTION, MB_TOK, 1))
    forward_weight = jnp.clip(0.2 + 0.8 * jax.random.uniform(arg_keys[3], (N_SECTION, MB_TOK), jnp.float32) ** shard_levels(arg_keys[3], (N_SECTION, MB_TOK), ((0, 8), (1, 32)), -0.2, 0.2), 0.2, 1.0)
    loss_cotangent = scatter_about(arg_keys[4], (MB_TOK, D), 1.0, 6.0, ((0, 32),))
    backward_held = scatter_about(arg_keys[5], (N_SECTION, MB_TOK, D), 1.0, 6.0, ((0, 8), (1, 32)))
    backward_route_keys = jax.random.split(jax.random.fold_in(arg_keys[6], 1), N_SECTION * MB_TOK // TOK_DEV)
    backward_route_turns = jax.random.permutation(jax.random.fold_in(arg_keys[6], 3), N_SECTION * MB_TOK // TOK_DEV)
    backward_route = jax.vmap(lambda own, number: shared_out(jax.random.fold_in(arg_keys[6], 2), own, number, TOK_DEV, EXPERTS, 1, CAP, 2))(backward_route_keys, backward_route_turns).reshape((N_SECTION, MB_TOK, 1))
    backward_weight = jnp.clip(0.2 + 0.8 * jax.random.uniform(arg_keys[7], (N_SECTION, MB_TOK), jnp.float32) ** shard_levels(arg_keys[7], (N_SECTION, MB_TOK), ((0, 8), (1, 32)), -0.2, 0.2), 0.2, 1.0)
    saved_gate = scatter_about(arg_keys[8], (N_SECTION, N_EXPERT * CAP, EXPERTS * H), 1.0, 6.0, ((0, 8), (2, 32)))
    saved_up = scatter_about(arg_keys[9], (N_SECTION, N_EXPERT * CAP, EXPERTS * H), 1.0, 6.0, ((0, 8), (2, 32)))
    gate_weight = scatter_about(arg_keys[10], (N_SECTION, D, EXPERTS * H), D ** -0.5, 0.09375, ((0, 8), (2, 32)))
    up_weight = scatter_about(arg_keys[11], (N_SECTION, D, EXPERTS * H), D ** -0.5, 0.09375, ((0, 8), (2, 32)))
    down_weight = scatter_about(arg_keys[12], (N_SECTION, EXPERTS * H, D), H ** -0.5, 0.1875, ((0, 8), (1, 32)))
    steering = scatter_about(arg_keys[13], (N_SECTION, D), 1.0, 6.0, ((0, 8),), jnp.float32)
    return dict(embedded=embedded, forward_held=forward_held, forward_route=forward_route, forward_weight=forward_weight, loss_cotangent=loss_cotangent, backward_held=backward_held, backward_route=backward_route, backward_weight=backward_weight, saved_gate=saved_gate, saved_up=saved_up, gate_weight=gate_weight, up_weight=up_weight, down_weight=down_weight, steering=steering)


def placement_rows(route_section):
    expert_ids = route_section[:, 0].astype(jnp.int32)
    blocked = expert_ids.reshape(N_EXPERT, TOK_DEV)
    onehot = (blocked[:, :, None] == jnp.arange(EXPERTS, dtype=jnp.int32)[None, None, :]).astype(jnp.int32)
    earlier = jnp.cumsum(onehot, axis=1) - onehot
    position = lax.optimization_barrier(jnp.sum(earlier * onehot, axis=2))
    row_index = jnp.arange(N_EXPERT, dtype=jnp.int32)[:, None] * CAP + position
    return (expert_ids, row_index.reshape(MB_TOK).astype(jnp.int32))

def layout_of(expert_ids, row_index):
    layout = jnp.full((EXPERTS, N_EXPERT * CAP), MB_TOK, jnp.int32)
    return layout.at[expert_ids, row_index].set(jnp.arange(MB_TOK, dtype=jnp.int32))

def forward_expert(slot_rows, gate_cols, up_cols, down_rows):
    summed = jnp.zeros((slot_rows.shape[0], D), jnp.float32)
    for holder in range(H // HDEV):
        first_col = holder * HDEV
        gate_pre = jnp.dot(slot_rows, gate_cols[:, first_col:first_col + HDEV], preferred_element_type=jnp.float32)
        up_pre = jnp.dot(slot_rows, up_cols[:, first_col:first_col + HDEV], preferred_element_type=jnp.float32)
        hidden = (jax.nn.silu(gate_pre) * up_pre).astype(jnp.bfloat16)
        partial_out = jnp.dot(hidden, down_rows[first_col:first_col + HDEV], preferred_element_type=jnp.float32).astype(jnp.bfloat16)
        summed = summed + partial_out.astype(jnp.float32)
    return summed.astype(jnp.bfloat16)

def backward_expert(slot_rows, gate_saved, up_saved, gate_cols, up_cols, down_rows):
    contract = (((1,), (1,)), ((), ()))
    summed = jnp.zeros((slot_rows.shape[0], D), jnp.float32)
    for holder in range(H // HDEV):
        first_col = holder * HDEV
        grad_hidden = lax.dot_general(slot_rows, down_rows[first_col:first_col + HDEV], contract, preferred_element_type=jnp.float32)
        gate_pre = gate_saved[:, first_col:first_col + HDEV].astype(jnp.float32)
        up_pre = up_saved[:, first_col:first_col + HDEV].astype(jnp.float32)
        sigmoid_gate = jax.nn.sigmoid(gate_pre)
        grad_gate = (grad_hidden * up_pre * sigmoid_gate * (1.0 + gate_pre * (1.0 - sigmoid_gate))).astype(jnp.bfloat16)
        grad_up = (grad_hidden * gate_pre * sigmoid_gate).astype(jnp.bfloat16)
        grad_part = lax.dot_general(grad_gate, gate_cols[:, first_col:first_col + HDEV], contract, preferred_element_type=jnp.float32)
        grad_part = grad_part + lax.dot_general(grad_up, up_cols[:, first_col:first_col + HDEV], contract, preferred_element_type=jnp.float32)
        summed = summed + grad_part.astype(jnp.bfloat16).astype(jnp.float32)
    return summed.astype(jnp.bfloat16)

def one_section(operands):
    forward_in, backward_in, forward_route, forward_weight, backward_route, backward_weight, gate_store, up_store, gate_mat, up_mat, down_mat, steer_vec = operands
    unit_dir = steer_vec / jnp.sqrt(jnp.sum(steer_vec * steer_vec) + 1e-06)
    expert_ids, row_index = placement_rows(forward_route)
    layout = layout_of(expert_ids, row_index)
    padded = jnp.concatenate([forward_in, jnp.zeros((1, D), forward_in.dtype)], axis=0)
    forward_slots = padded[layout]

    def expert_forward(packed):
        expert_index, slot_rows = packed
        gate_cols = lax.dynamic_slice_in_dim(gate_mat, expert_index * H, H, 1)
        up_cols = lax.dynamic_slice_in_dim(up_mat, expert_index * H, H, 1)
        down_rows = lax.dynamic_slice_in_dim(down_mat, expert_index * H, H, 0)
        return forward_expert(slot_rows, gate_cols, up_cols, down_rows)
    forward_outs = lax.map(expert_forward, (jnp.arange(EXPERTS, dtype=jnp.int32), forward_slots))
    picked = forward_outs[expert_ids, row_index]
    mixed_rows = forward_weight[:, None] * picked.astype(jnp.float32)
    coefficient = lax.optimization_barrier(jnp.sum(mixed_rows * unit_dir[None, :], axis=1))
    forward_out = (forward_in.astype(jnp.float32) + mixed_rows - coefficient[:, None] * unit_dir[None, :]).astype(jnp.bfloat16)
    backward_dy = backward_in.astype(jnp.float32)
    along_dir = lax.optimization_barrier(jnp.sum(backward_dy * unit_dir[None, :], axis=1))
    sent_rows = (backward_weight[:, None] * (backward_dy - along_dir[:, None] * unit_dir[None, :])).astype(jnp.bfloat16)
    backward_ids, backward_index = placement_rows(backward_route)
    backward_layout = layout_of(backward_ids, backward_index)
    padded_sent = jnp.concatenate([sent_rows, jnp.zeros((1, D), sent_rows.dtype)], axis=0)
    backward_slots = padded_sent[backward_layout]

    def expert_backward(packed):
        expert_index, slot_rows = packed
        gate_cols = lax.dynamic_slice_in_dim(gate_mat, expert_index * H, H, 1)
        up_cols = lax.dynamic_slice_in_dim(up_mat, expert_index * H, H, 1)
        down_rows = lax.dynamic_slice_in_dim(down_mat, expert_index * H, H, 0)
        gate_saved = lax.dynamic_slice_in_dim(gate_store, expert_index * H, H, 1)
        up_saved = lax.dynamic_slice_in_dim(up_store, expert_index * H, H, 1)
        return backward_expert(slot_rows, gate_saved, up_saved, gate_cols, up_cols, down_rows)
    backward_outs = lax.map(expert_backward, (jnp.arange(EXPERTS, dtype=jnp.int32), backward_slots))
    returned = backward_outs[backward_ids, backward_index]
    backward_out = (backward_dy + returned.astype(jnp.float32)).astype(jnp.bfloat16)
    return (forward_out, coefficient, backward_out)

def reference(embedded, forward_held, forward_route, forward_weight, loss_cotangent, backward_held, backward_route, backward_weight, saved_gate, saved_up, gate_weight, up_weight, down_weight, steering):
    forward_inputs = jnp.concatenate([embedded[None], forward_held[:-1]], axis=0)
    backward_inputs = jnp.concatenate([backward_held[1:], loss_cotangent[None]], axis=0)
    results = lax.map(one_section, (forward_inputs, backward_inputs, forward_route, forward_weight, backward_route, backward_weight, saved_gate, saved_up, gate_weight, up_weight, down_weight, steering))
    return (results[0], results[1], results[2])
```

```python
import jax
import jax.numpy as jnp
import numpy as np
from jax import lax
from jax.sharding import Mesh
from jax.sharding import PartitionSpec as P

H = 1024
EXPERT_AXES = ("ex", "em", "ep", "ec")
GROUP = ("ex", "em")
HOLDERS = ("ep", "ec")


def shifted(value, axis, by):
    devices = lax.axis_size(axis)
    pairs = [(i, i + by) for i in range(devices) if 0 <= i + by < devices]
    return lax.ppermute(value, axis, pairs)


def dispatch_layout(expert_ids, expert_count, capacity):
    onehot = (expert_ids[:, None] == jnp.arange(expert_count, dtype=jnp.int32)[None, :]).astype(
        jnp.int32
    )
    earlier = jnp.cumsum(onehot, axis=0) - onehot
    position = jnp.sum(earlier * onehot, axis=1)
    target = expert_ids * capacity + position
    return (
        jnp.arange(expert_count * capacity, dtype=jnp.int32)[:, None] == target[None, :]
    ).astype(jnp.bfloat16)


def expert_forward(slot_rows, weights):
    gate_cols, up_cols, down_rows = weights
    gate_pre = jnp.dot(slot_rows, gate_cols, preferred_element_type=jnp.float32)
    up_pre = jnp.dot(slot_rows, up_cols, preferred_element_type=jnp.float32)
    hidden = (jax.nn.silu(gate_pre) * up_pre).astype(jnp.bfloat16)
    return jnp.dot(hidden, down_rows, preferred_element_type=jnp.float32).astype(jnp.bfloat16)


def expert_backward(slot_rows, gate_saved, up_saved, weights):
    gate_cols, up_cols, down_rows = weights
    contract = (((1,), (1,)), ((), ()))
    grad_hidden = lax.dot_general(
        slot_rows, down_rows, contract, preferred_element_type=jnp.float32
    )
    gate_pre = gate_saved.astype(jnp.float32)
    up_pre = up_saved.astype(jnp.float32)
    sigmoid_gate = jax.nn.sigmoid(gate_pre)
    grad_gate = (
        grad_hidden * up_pre * sigmoid_gate * (1.0 + gate_pre * (1.0 - sigmoid_gate))
    ).astype(jnp.bfloat16)
    grad_up = (grad_hidden * gate_pre * sigmoid_gate).astype(jnp.bfloat16)
    grad_part = lax.dot_general(grad_gate, gate_cols, contract, preferred_element_type=jnp.float32)
    grad_part = grad_part + lax.dot_general(
        grad_up, up_cols, contract, preferred_element_type=jnp.float32
    )
    return grad_part.astype(jnp.bfloat16)


def combine_holders(parts):
    swapped = lax.all_to_all(parts, "ec", split_axis=2, concat_axis=2, tiled=True)
    pair = swapped[:, :, 0].astype(jnp.float32) + swapped[:, :, 1].astype(jnp.float32)
    me = lax.axis_index("ep")
    mine = jnp.where(me == 0, pair[:, 0], pair[:, 1])
    other = jnp.where(me == 0, pair[:, 1], pair[:, 0]).astype(jnp.bfloat16)
    arrived = lax.ppermute(other, "ep", [(0, 1), (1, 0)])
    return (mine + arrived.astype(jnp.float32)).astype(jnp.bfloat16)


def body(
    embedded,
    forward_held,
    forward_route,
    forward_weight,
    loss_cotangent,
    backward_held,
    backward_route,
    backward_weight,
    saved_gate,
    saved_up,
    gate_weight,
    up_weight,
    down_weight,
    steering,
):
    section_count = lax.axis_size("section")
    section_index = lax.axis_index("section")
    group_count = lax.axis_size(GROUP)
    holder_count = lax.axis_size(HOLDERS)
    local_hidden = gate_weight.shape[2]
    expert_count = group_count
    device_count = group_count * holder_count
    capacity = saved_gate.shape[1] // device_count
    feature_count = embedded.shape[1]
    arriving = shifted(forward_held, "section", 1)[0]
    forward_in = jnp.where(section_index == 0, embedded, arriving)
    returning = shifted(backward_held, "section", -1)[0]
    backward_in = jnp.where(section_index == section_count - 1, loss_cotangent, returning)
    direction = steering[0]
    unit_dir = direction / jnp.sqrt(jnp.sum(direction * direction) + 1e-06)
    weights = (gate_weight[0], up_weight[0], down_weight[0])

    forward_layout = dispatch_layout(forward_route[0, :, 0], expert_count, capacity)
    forward_send = jnp.dot(forward_layout, forward_in, preferred_element_type=jnp.float32).astype(
        jnp.bfloat16
    )
    backward_dy = backward_in.astype(jnp.float32)
    along_dir = jnp.sum(backward_dy * unit_dir[None, :], axis=1)
    sent_rows = (
        backward_weight[0][:, None] * (backward_dy - along_dir[:, None] * unit_dir[None, :])
    ).astype(jnp.bfloat16)
    backward_layout = dispatch_layout(backward_route[0, :, 0], expert_count, capacity)
    backward_send = jnp.dot(backward_layout, sent_rows, preferred_element_type=jnp.float32).astype(
        jnp.bfloat16
    )
    send = jnp.stack([forward_send, backward_send]).reshape(2, expert_count, capacity, feature_count)
    by_group = lax.all_to_all(send, GROUP, split_axis=1, concat_axis=1, tiled=True)
    gathered = lax.all_gather(by_group, HOLDERS, axis=1, tiled=False)
    rows = gathered.reshape(2, device_count * capacity, feature_count)

    def reorder(saved):
        return (
            saved[0]
            .reshape(group_count, holder_count, capacity, local_hidden)
            .transpose(1, 0, 2, 3)
            .reshape(device_count * capacity, local_hidden)
        )

    forward_part = expert_forward(rows[0], weights)
    backward_part = expert_backward(rows[1], reorder(saved_gate), reorder(saved_up), weights)
    parts = jnp.stack([forward_part, backward_part]).reshape(
        2, 2, 2, group_count, capacity, feature_count
    )
    summed = combine_holders(parts)
    back = lax.all_to_all(summed, GROUP, split_axis=1, concat_axis=1, tiled=True)
    back = back.reshape(2, expert_count * capacity, feature_count)

    contract = (((0,), (0,)), ((), ()))
    picked = lax.dot_general(forward_layout, back[0], contract, preferred_element_type=jnp.float32)
    mixed_rows = forward_weight[0][:, None] * picked
    coefficient = jnp.sum(mixed_rows * unit_dir[None, :], axis=1)
    forward_out = (
        forward_in.astype(jnp.float32) + mixed_rows - coefficient[:, None] * unit_dir[None, :]
    ).astype(jnp.bfloat16)
    returned = lax.dot_general(
        backward_layout, back[1], contract, preferred_element_type=jnp.float32
    )
    backward_out = (backward_dy + returned).astype(jnp.bfloat16)
    return (forward_out[None], coefficient[None], backward_out[None])


def solution(mesh):
    sections = mesh.shape["section"]
    experts = mesh.shape["expert"]
    fine = Mesh(
        np.asarray(mesh.devices).reshape(sections, experts // 8, 2, 2, 2),
        ("section",) + EXPERT_AXES,
    )
    E = EXPERT_AXES
    in_specs = (
        P(E, None),
        P("section", E, None),
        P("section", E, None),
        P("section", E),
        P(E, None),
        P("section", E, None),
        P("section", E, None),
        P("section", E),
        P("section", None, E),
        P("section", None, E),
        P("section", None, E),
        P("section", None, E),
        P("section", E, None),
        P("section", None),
    )
    out_specs = (P("section", E, None), P("section", E), P("section", E, None))
    return jax.shard_map(body, mesh=fine, in_specs=in_specs, out_specs=out_specs, check_vma=False)
```

```python
import jax
import jax.numpy as jnp
import numpy as np
from jax import lax
from jax.sharding import Mesh
from jax.sharding import PartitionSpec as P

H = 1024
EXPERT_AXES = ("ex", "em", "ep", "ec")
GROUP = ("ex", "em")
HOLDERS = ("ep", "ec")


def shifted(value, axis, by):
    devices = lax.axis_size(axis)
    pairs = [(i, i + by) for i in range(devices) if 0 <= i + by < devices]
    return lax.ppermute(value, axis, pairs)


def dispatch_layout(expert_ids, expert_count, capacity):
    onehot = (expert_ids[:, None] == jnp.arange(expert_count, dtype=jnp.int32)[None, :]).astype(
        jnp.int32
    )
    earlier = jnp.cumsum(onehot, axis=0) - onehot
    position = jnp.sum(earlier * onehot, axis=1)
    target = expert_ids * capacity + position
    return (
        jnp.arange(expert_count * capacity, dtype=jnp.int32)[:, None] == target[None, :]
    ).astype(jnp.bfloat16)


def expert_forward(slot_rows, weights):
    gate_cols, up_cols, down_rows = weights
    gate_pre = jnp.dot(slot_rows, gate_cols, preferred_element_type=jnp.float32)
    up_pre = jnp.dot(slot_rows, up_cols, preferred_element_type=jnp.float32)
    hidden = (jax.nn.silu(gate_pre) * up_pre).astype(jnp.bfloat16)
    return jnp.dot(hidden, down_rows, preferred_element_type=jnp.float32).astype(jnp.bfloat16)


def expert_backward(slot_rows, gate_saved, up_saved, weights):
    gate_cols, up_cols, down_rows = weights
    contract = (((1,), (1,)), ((), ()))
    grad_hidden = lax.dot_general(
        slot_rows, down_rows, contract, preferred_element_type=jnp.float32
    )
    gate_pre = gate_saved.astype(jnp.float32)
    up_pre = up_saved.astype(jnp.float32)
    sigmoid_gate = jax.nn.sigmoid(gate_pre)
    grad_gate = (
        grad_hidden * up_pre * sigmoid_gate * (1.0 + gate_pre * (1.0 - sigmoid_gate))
    ).astype(jnp.bfloat16)
    grad_up = (grad_hidden * gate_pre * sigmoid_gate).astype(jnp.bfloat16)
    grad_part = lax.dot_general(grad_gate, gate_cols, contract, preferred_element_type=jnp.float32)
    grad_part = grad_part + lax.dot_general(
        grad_up, up_cols, contract, preferred_element_type=jnp.float32
    )
    return grad_part.astype(jnp.bfloat16)


def swap_pair(value):
    return lax.ppermute(value, "ep", [(0, 1), (1, 0)])


def spread_to_holders(send):
    own = lax.all_to_all(send, GROUP, split_axis=0, concat_axis=0, tiled=True)
    other = swap_pair(own)
    pair = jnp.stack([own, other])
    return lax.all_gather(pair, "ec", axis=0, tiled=False)


def collect_from_holders(parts):
    swapped = lax.all_to_all(parts, "ec", split_axis=0, concat_axis=0, tiled=True)
    pair = swapped[0].astype(jnp.float32) + swapped[1].astype(jnp.float32)
    arrived = swap_pair(pair[1].astype(jnp.bfloat16))
    summed = (pair[0] + arrived.astype(jnp.float32)).astype(jnp.bfloat16)
    return lax.all_to_all(summed, GROUP, split_axis=0, concat_axis=0, tiled=True)


def body(
    embedded,
    forward_held,
    forward_route,
    forward_weight,
    loss_cotangent,
    backward_held,
    backward_route,
    backward_weight,
    saved_gate,
    saved_up,
    gate_weight,
    up_weight,
    down_weight,
    steering,
):
    section_count = lax.axis_size("section")
    section_index = lax.axis_index("section")
    group_count = lax.axis_size(GROUP)
    holder_count = lax.axis_size(HOLDERS)
    local_hidden = gate_weight.shape[2]
    expert_count = group_count
    device_count = group_count * holder_count
    capacity = saved_gate.shape[1] // device_count
    feature_count = embedded.shape[1]
    rows_shape = (device_count * capacity, feature_count)
    arriving = shifted(forward_held, "section", 1)[0]
    forward_in = jnp.where(section_index == 0, embedded, arriving)
    returning = shifted(backward_held, "section", -1)[0]
    backward_in = jnp.where(section_index == section_count - 1, loss_cotangent, returning)
    direction = steering[0]
    unit_dir = direction / jnp.sqrt(jnp.sum(direction * direction) + 1e-06)
    weights = (gate_weight[0], up_weight[0], down_weight[0])

    forward_layout = dispatch_layout(forward_route[0, :, 0], expert_count, capacity)
    forward_send = jnp.dot(forward_layout, forward_in, preferred_element_type=jnp.float32).astype(
        jnp.bfloat16
    )
    forward_rows = spread_to_holders(forward_send.reshape(expert_count, capacity, feature_count))

    backward_dy = backward_in.astype(jnp.float32)
    along_dir = jnp.sum(backward_dy * unit_dir[None, :], axis=1)
    sent_rows = (
        backward_weight[0][:, None] * (backward_dy - along_dir[:, None] * unit_dir[None, :])
    ).astype(jnp.bfloat16)
    backward_layout = dispatch_layout(backward_route[0, :, 0], expert_count, capacity)
    backward_send = jnp.dot(backward_layout, sent_rows, preferred_element_type=jnp.float32).astype(
        jnp.bfloat16
    )
    backward_rows = spread_to_holders(backward_send.reshape(expert_count, capacity, feature_count))

    flip = lax.axis_index("ep") == 1

    def reorder(saved):
        grouped = saved[0].reshape(group_count, 2, 2, capacity, local_hidden).transpose(2, 1, 0, 3, 4)
        grouped = jnp.where(flip, grouped[:, ::-1], grouped)
        return grouped.reshape(device_count * capacity, local_hidden)

    forward_part = expert_forward(forward_rows.reshape(rows_shape), weights)
    forward_back = collect_from_holders(
        forward_part.reshape(2, 2, group_count, capacity, feature_count)
    ).reshape(expert_count * capacity, feature_count)
    backward_part = expert_backward(
        backward_rows.reshape(rows_shape), reorder(saved_gate), reorder(saved_up), weights
    )
    backward_back = collect_from_holders(
        backward_part.reshape(2, 2, group_count, capacity, feature_count)
    ).reshape(expert_count * capacity, feature_count)

    contract = (((0,), (0,)), ((), ()))
    picked = lax.dot_general(forward_layout, forward_back, contract, preferred_element_type=jnp.float32)
    mixed_rows = forward_weight[0][:, None] * picked
    coefficient = jnp.sum(mixed_rows * unit_dir[None, :], axis=1)
    forward_out = (
        forward_in.astype(jnp.float32) + mixed_rows - coefficient[:, None] * unit_dir[None, :]
    ).astype(jnp.bfloat16)
    returned = lax.dot_general(
        backward_layout, backward_back, contract, preferred_element_type=jnp.float32
    )
    backward_out = (backward_dy + returned).astype(jnp.bfloat16)
    return (forward_out[None], coefficient[None], backward_out[None])


def solution(mesh):
    sections = mesh.shape["section"]
    experts = mesh.shape["expert"]
    fine = Mesh(
        np.asarray(mesh.devices).reshape(sections, experts // 8, 2, 2, 2),
        ("section",) + EXPERT_AXES,
    )
    E = EXPERT_AXES
    in_specs = (
        P(E, None),
        P("section", E, None),
        P("section", E, None),
        P("section", E),
        P(E, None),
        P("section", E, None),
        P("section", E, None),
        P("section", E),
        P("section", None, E),
        P("section", None, E),
        P("section", None, E),
        P("section", None, E),
        P("section", E, None),
        P("section", None),
    )
    out_specs = (P("section", E, None), P("section", E), P("section", E, None))
    return jax.shard_map(body, mesh=fine, in_specs=in_specs, out_specs=out_specs, check_vma=False)
```

```python
import functools

import jax
import jax.numpy as jnp
import numpy as np
from jax import lax
from jax.experimental import pallas as pl
from jax.experimental.pallas import tpu as pltpu
from jax.sharding import Mesh
from jax.sharding import PartitionSpec as P

H = 1024
EXPERT_AXES = ("ex", "em", "ep", "ec")
GROUP = ("ex", "em")
HOLDERS = ("ep", "ec")
MESH_IDS = pl.DeviceIdType.MESH


def shifted(value, axis, by):
    devices = lax.axis_size(axis)
    pairs = [(i, i + by) for i in range(devices) if 0 <= i + by < devices]
    return lax.ppermute(value, axis, pairs)


def dispatch_layout(expert_ids, expert_count, capacity):
    onehot = (expert_ids[:, None] == jnp.arange(expert_count, dtype=jnp.int32)[None, :]).astype(
        jnp.int32
    )
    earlier = jnp.cumsum(onehot, axis=0) - onehot
    position = jnp.sum(earlier * onehot, axis=1)
    target = expert_ids * capacity + position
    return (
        jnp.arange(expert_count * capacity, dtype=jnp.int32)[:, None] == target[None, :]
    ).astype(jnp.bfloat16)


def expert_forward(slot_rows, weights):
    gate_cols, up_cols, down_rows = weights
    gate_pre = jnp.dot(slot_rows, gate_cols, preferred_element_type=jnp.float32)
    up_pre = jnp.dot(slot_rows, up_cols, preferred_element_type=jnp.float32)
    hidden = (jax.nn.silu(gate_pre) * up_pre).astype(jnp.bfloat16)
    return jnp.dot(hidden, down_rows, preferred_element_type=jnp.float32).astype(jnp.bfloat16)


def expert_backward(slot_rows, gate_saved, up_saved, weights):
    gate_cols, up_cols, down_rows = weights
    contract = (((1,), (1,)), ((), ()))
    grad_hidden = lax.dot_general(
        slot_rows, down_rows, contract, preferred_element_type=jnp.float32
    )
    gate_pre = gate_saved.astype(jnp.float32)
    up_pre = up_saved.astype(jnp.float32)
    sigmoid_gate = jax.nn.sigmoid(gate_pre)
    grad_gate = (
        grad_hidden * up_pre * sigmoid_gate * (1.0 + gate_pre * (1.0 - sigmoid_gate))
    ).astype(jnp.bfloat16)
    grad_up = (grad_hidden * gate_pre * sigmoid_gate).astype(jnp.bfloat16)
    grad_part = lax.dot_general(grad_gate, gate_cols, contract, preferred_element_type=jnp.float32)
    grad_part = grad_part + lax.dot_general(
        grad_up, up_cols, contract, preferred_element_type=jnp.float32
    )
    return grad_part.astype(jnp.bfloat16)


def swap_pair(value):
    return lax.ppermute(value, "ep", [(0, 1), (1, 0)])


def spread_kernel(groups, *refs):
    streams = (len(refs) - 6) // 2
    sends = refs[:streams]
    rows = refs[streams : 2 * streams]
    first_recv, first_send, pair_recv, pair_send, near_recv, near_send = refs[2 * streams : 2 * streams + 6]
    section = lax.axis_index("section")
    ex = lax.axis_index("ex")
    em = lax.axis_index("em")
    ep = lax.axis_index("ep")
    ec = lax.axis_index("ec")
    me = ex * 2 + em
    partner = (section, ex, em, 1 - ep, ec)
    sibling = (section, ex, em, ep, 1 - ec)

    def peer(g):
        return (section, g // 2, g % 2, ep, ec)

    barrier = pltpu.get_barrier_semaphore()
    for d in range(1, groups):
        pl.semaphore_signal(barrier, inc=1, device_id=peer((me + d) % groups), device_id_type=MESH_IDS)
    pl.semaphore_signal(barrier, inc=1, device_id=partner, device_id_type=MESH_IDS)
    pl.semaphore_signal(barrier, inc=1, device_id=sibling, device_id_type=MESH_IDS)
    pl.semaphore_wait(barrier, groups + 1)

    def first_copy(s, g, target):
        return pltpu.make_async_remote_copy(
            src_ref=sends[s].at[g],
            dst_ref=rows[s].at[ec, 0, me],
            send_sem=first_send.at[s, g],
            recv_sem=first_recv.at[s, me],
            device_id=target,
            device_id_type=MESH_IDS,
        )

    def arrived(s, g):
        return pltpu.make_async_remote_copy(
            src_ref=sends[s].at[g],
            dst_ref=rows[s].at[ec, 0, g],
            send_sem=first_send.at[s, g],
            recv_sem=first_recv.at[s, g],
            device_id=peer(g),
            device_id_type=MESH_IDS,
        )

    def relay(s, q, g, target, recv, send, slot):
        return pltpu.make_async_remote_copy(
            src_ref=rows[s].at[ec, q, g],
            dst_ref=rows[s].at[ec, slot, g],
            send_sem=send.at[s, q, g],
            recv_sem=recv.at[s, q, g],
            device_id=target,
            device_id_type=MESH_IDS,
        )

    local = []
    for s in range(streams):
        copy = pltpu.make_async_copy(sends[s].at[me], rows[s].at[ec, 0, me], first_recv.at[s, me])
        copy.start()
        local.append(copy)
        for d in range(1, groups):
            g = (me + d) % groups
            first_copy(s, g, peer(g)).start()
    outgoing = []
    for s in range(streams):
        local[s].wait()
        for d in range(groups):
            g = (me + groups - d) % groups
            if d > 0:
                arrived(s, g).wait_recv()
            for target, recv, send, slot in (
                (partner, pair_recv, pair_send, 1),
                (sibling, near_recv, near_send, 0),
            ):
                copy = relay(s, 0, g, target, recv, send, slot)
                copy.start()
                outgoing.append(copy)
    for s in range(streams):
        for d in range(groups):
            g = (me + groups - d) % groups
            relay(s, 0, g, partner, pair_recv, pair_send, 1).wait_recv()
            copy = relay(s, 1, g, sibling, near_recv, near_send, 1)
            copy.start()
            outgoing.append(copy)
    for s in range(streams):
        for q in range(2):
            for g in range(groups):
                pltpu.make_async_remote_copy(
                    src_ref=rows[s].at[1 - ec, q, g],
                    dst_ref=rows[s].at[1 - ec, q, g],
                    send_sem=near_send.at[s, q, g],
                    recv_sem=near_recv.at[s, q, g],
                    device_id=sibling,
                    device_id_type=MESH_IDS,
                ).wait_recv()
    for s in range(streams):
        for d in range(1, groups):
            g = (me + d) % groups
            first_copy(s, g, peer(g)).wait_send()
    for copy in outgoing:
        copy.wait_send()


def spread_to_holders(*sends):
    groups, capacity, features = sends[0].shape
    streams = len(sends)
    rows = jax.ShapeDtypeStruct((2, 2, groups, capacity, features), sends[0].dtype)
    any_spec = pl.BlockSpec(memory_space=pl.ANY)
    return pl.pallas_call(
        functools.partial(spread_kernel, groups),
        out_shape=[rows] * streams,
        in_specs=[any_spec] * streams,
        out_specs=[any_spec] * streams,
        scratch_shapes=[
            pltpu.SemaphoreType.DMA((streams, groups)),
            pltpu.SemaphoreType.DMA((streams, groups)),
            pltpu.SemaphoreType.DMA((streams, 2, groups)),
            pltpu.SemaphoreType.DMA((streams, 2, groups)),
            pltpu.SemaphoreType.DMA((streams, 2, groups)),
            pltpu.SemaphoreType.DMA((streams, 2, groups)),
        ],
        compiler_params=pltpu.CompilerParams(collective_id=0, has_side_effects=True),
    )(*sends)


def collect_from_holders(parts):
    swapped = lax.all_to_all(parts, "ec", split_axis=0, concat_axis=0, tiled=True)
    pair = swapped[0].astype(jnp.float32) + swapped[1].astype(jnp.float32)
    arrived = swap_pair(pair[1].astype(jnp.bfloat16))
    summed = (pair[0] + arrived.astype(jnp.float32)).astype(jnp.bfloat16)
    return lax.all_to_all(summed, GROUP, split_axis=0, concat_axis=0, tiled=True)


def body(
    embedded,
    forward_held,
    forward_route,
    forward_weight,
    loss_cotangent,
    backward_held,
    backward_route,
    backward_weight,
    saved_gate,
    saved_up,
    gate_weight,
    up_weight,
    down_weight,
    steering,
):
    section_count = lax.axis_size("section")
    section_index = lax.axis_index("section")
    group_count = lax.axis_size(GROUP)
    holder_count = lax.axis_size(HOLDERS)
    local_hidden = gate_weight.shape[2]
    expert_count = group_count
    device_count = group_count * holder_count
    capacity = saved_gate.shape[1] // device_count
    feature_count = embedded.shape[1]
    rows_shape = (device_count * capacity, feature_count)
    arriving = shifted(forward_held, "section", 1)[0]
    forward_in = jnp.where(section_index == 0, embedded, arriving)
    returning = shifted(backward_held, "section", -1)[0]
    backward_in = jnp.where(section_index == section_count - 1, loss_cotangent, returning)
    direction = steering[0]
    unit_dir = direction / jnp.sqrt(jnp.sum(direction * direction) + 1e-06)
    weights = (gate_weight[0], up_weight[0], down_weight[0])

    forward_layout = dispatch_layout(forward_route[0, :, 0], expert_count, capacity)
    forward_send = jnp.dot(forward_layout, forward_in, preferred_element_type=jnp.float32).astype(
        jnp.bfloat16
    )

    backward_dy = backward_in.astype(jnp.float32)
    along_dir = jnp.sum(backward_dy * unit_dir[None, :], axis=1)
    sent_rows = (
        backward_weight[0][:, None] * (backward_dy - along_dir[:, None] * unit_dir[None, :])
    ).astype(jnp.bfloat16)
    backward_layout = dispatch_layout(backward_route[0, :, 0], expert_count, capacity)
    backward_send = jnp.dot(backward_layout, sent_rows, preferred_element_type=jnp.float32).astype(
        jnp.bfloat16
    )
    forward_rows, backward_rows = spread_to_holders(
        forward_send.reshape(expert_count, capacity, feature_count),
        backward_send.reshape(expert_count, capacity, feature_count),
    )

    flip = lax.axis_index("ep") == 1

    def reorder(saved):
        grouped = saved[0].reshape(group_count, 2, 2, capacity, local_hidden).transpose(2, 1, 0, 3, 4)
        grouped = jnp.where(flip, grouped[:, ::-1], grouped)
        return grouped.reshape(device_count * capacity, local_hidden)

    forward_part = expert_forward(forward_rows.reshape(rows_shape), weights)
    forward_back = collect_from_holders(
        forward_part.reshape(2, 2, group_count, capacity, feature_count)
    ).reshape(expert_count * capacity, feature_count)
    backward_part = expert_backward(
        backward_rows.reshape(rows_shape), reorder(saved_gate), reorder(saved_up), weights
    )
    backward_back = collect_from_holders(
        backward_part.reshape(2, 2, group_count, capacity, feature_count)
    ).reshape(expert_count * capacity, feature_count)

    contract = (((0,), (0,)), ((), ()))
    picked = lax.dot_general(forward_layout, forward_back, contract, preferred_element_type=jnp.float32)
    mixed_rows = forward_weight[0][:, None] * picked
    coefficient = jnp.sum(mixed_rows * unit_dir[None, :], axis=1)
    forward_out = (
        forward_in.astype(jnp.float32) + mixed_rows - coefficient[:, None] * unit_dir[None, :]
    ).astype(jnp.bfloat16)
    returned = lax.dot_general(
        backward_layout, backward_back, contract, preferred_element_type=jnp.float32
    )
    backward_out = (backward_dy + returned).astype(jnp.bfloat16)
    return (forward_out[None], coefficient[None], backward_out[None])


def solution(mesh):
    sections = mesh.shape["section"]
    experts = mesh.shape["expert"]
    fine = Mesh(
        np.asarray(mesh.devices).reshape(sections, experts // 8, 2, 2, 2),
        ("section",) + EXPERT_AXES,
    )
    E = EXPERT_AXES
    in_specs = (
        P(E, None),
        P("section", E, None),
        P("section", E, None),
        P("section", E),
        P(E, None),
        P("section", E, None),
        P("section", E, None),
        P("section", E),
        P("section", None, E),
        P("section", None, E),
        P("section", None, E),
        P("section", None, E),
        P("section", E, None),
        P("section", None),
    )
    out_specs = (P("section", E, None), P("section", E), P("section", E, None))
    return jax.shard_map(body, mesh=fine, in_specs=in_specs, out_specs=out_specs, check_vma=False)
```

```python
import functools

import jax
import jax.numpy as jnp
import numpy as np
from jax import lax
from jax.experimental import pallas as pl
from jax.experimental.pallas import tpu as pltpu
from jax.sharding import Mesh
from jax.sharding import PartitionSpec as P

H = 1024
EXPERT_AXES = ("ex", "em", "ep", "ec")
GROUP = ("ex", "em")
HOLDERS = ("ep", "ec")
MESH_IDS = pl.DeviceIdType.MESH


def shifted(value, axis, by):
    devices = lax.axis_size(axis)
    pairs = [(i, i + by) for i in range(devices) if 0 <= i + by < devices]
    return lax.ppermute(value, axis, pairs)


def dispatch_layout(expert_ids, expert_count, capacity):
    onehot = (expert_ids[:, None] == jnp.arange(expert_count, dtype=jnp.int32)[None, :]).astype(
        jnp.int32
    )
    earlier = jnp.cumsum(onehot, axis=0) - onehot
    position = jnp.sum(earlier * onehot, axis=1)
    target = expert_ids * capacity + position
    return (
        jnp.arange(expert_count * capacity, dtype=jnp.int32)[:, None] == target[None, :]
    ).astype(jnp.bfloat16)


def expert_forward(slot_rows, weights):
    gate_cols, up_cols, down_rows = weights
    gate_pre = jnp.dot(slot_rows, gate_cols, preferred_element_type=jnp.float32)
    up_pre = jnp.dot(slot_rows, up_cols, preferred_element_type=jnp.float32)
    hidden = (jax.nn.silu(gate_pre) * up_pre).astype(jnp.bfloat16)
    return jnp.dot(hidden, down_rows, preferred_element_type=jnp.float32).astype(jnp.bfloat16)


def expert_backward(slot_rows, gate_saved, up_saved, weights):
    gate_cols, up_cols, down_rows = weights
    contract = (((1,), (1,)), ((), ()))
    grad_hidden = lax.dot_general(
        slot_rows, down_rows, contract, preferred_element_type=jnp.float32
    )
    gate_pre = gate_saved.astype(jnp.float32)
    up_pre = up_saved.astype(jnp.float32)
    sigmoid_gate = jax.nn.sigmoid(gate_pre)
    grad_gate = (
        grad_hidden * up_pre * sigmoid_gate * (1.0 + gate_pre * (1.0 - sigmoid_gate))
    ).astype(jnp.bfloat16)
    grad_up = (grad_hidden * gate_pre * sigmoid_gate).astype(jnp.bfloat16)
    grad_part = lax.dot_general(grad_gate, gate_cols, contract, preferred_element_type=jnp.float32)
    grad_part = grad_part + lax.dot_general(
        grad_up, up_cols, contract, preferred_element_type=jnp.float32
    )
    return grad_part.astype(jnp.bfloat16)


def swap_pair(value):
    return lax.ppermute(value, "ep", [(0, 1), (1, 0)])


def spread_kernel(groups, *refs):
    streams = (len(refs) - 6) // 2
    sends = refs[:streams]
    rows = refs[streams : 2 * streams]
    first_recv, first_send, pair_recv, pair_send, near_recv, near_send = refs[2 * streams : 2 * streams + 6]
    section = lax.axis_index("section")
    ex = lax.axis_index("ex")
    em = lax.axis_index("em")
    ep = lax.axis_index("ep")
    ec = lax.axis_index("ec")
    me = ex * 2 + em
    partner = (section, ex, em, 1 - ep, ec)
    sibling = (section, ex, em, ep, 1 - ec)

    def peer(g):
        return (section, g // 2, g % 2, ep, ec)

    barrier = pltpu.get_barrier_semaphore()
    for d in range(1, groups):
        pl.semaphore_signal(barrier, inc=1, device_id=peer((me + d) % groups), device_id_type=MESH_IDS)
    pl.semaphore_signal(barrier, inc=1, device_id=partner, device_id_type=MESH_IDS)
    pl.semaphore_signal(barrier, inc=1, device_id=sibling, device_id_type=MESH_IDS)
    pl.semaphore_wait(barrier, groups + 1)

    def first_copy(s, g, target):
        return pltpu.make_async_remote_copy(
            src_ref=sends[s].at[g],
            dst_ref=rows[s].at[ec, 0, me],
            send_sem=first_send.at[s, g],
            recv_sem=first_recv.at[s, me],
            device_id=target,
            device_id_type=MESH_IDS,
        )

    def arrived(s, g):
        return pltpu.make_async_remote_copy(
            src_ref=sends[s].at[g],
            dst_ref=rows[s].at[ec, 0, g],
            send_sem=first_send.at[s, g],
            recv_sem=first_recv.at[s, g],
            device_id=peer(g),
            device_id_type=MESH_IDS,
        )

    def relay(s, q, g, target, recv, send, slot):
        return pltpu.make_async_remote_copy(
            src_ref=rows[s].at[ec, q, g],
            dst_ref=rows[s].at[ec, slot, g],
            send_sem=send.at[s, q, g],
            recv_sem=recv.at[s, q, g],
            device_id=target,
            device_id_type=MESH_IDS,
        )

    local = []
    for s in range(streams):
        copy = pltpu.make_async_copy(sends[s].at[me], rows[s].at[ec, 0, me], first_recv.at[s, me])
        copy.start()
        local.append(copy)
        for d in range(1, groups):
            g = (me + d) % groups
            first_copy(s, g, peer(g)).start()
    outgoing = []
    for s in range(streams):
        local[s].wait()
        for d in range(groups):
            g = (me + groups - d) % groups
            if d > 0:
                arrived(s, g).wait_recv()
            for target, recv, send, slot in (
                (partner, pair_recv, pair_send, 1),
                (sibling, near_recv, near_send, 0),
            ):
                copy = relay(s, 0, g, target, recv, send, slot)
                copy.start()
                outgoing.append(copy)
    for s in range(streams):
        for d in range(groups):
            g = (me + groups - d) % groups
            relay(s, 0, g, partner, pair_recv, pair_send, 1).wait_recv()
            copy = relay(s, 1, g, sibling, near_recv, near_send, 1)
            copy.start()
            outgoing.append(copy)
    for s in range(streams):
        for q in range(2):
            for g in range(groups):
                pltpu.make_async_remote_copy(
                    src_ref=rows[s].at[1 - ec, q, g],
                    dst_ref=rows[s].at[1 - ec, q, g],
                    send_sem=near_send.at[s, q, g],
                    recv_sem=near_recv.at[s, q, g],
                    device_id=sibling,
                    device_id_type=MESH_IDS,
                ).wait_recv()
    for s in range(streams):
        for d in range(1, groups):
            g = (me + d) % groups
            first_copy(s, g, peer(g)).wait_send()
    for copy in outgoing:
        copy.wait_send()


def spread_to_holders(*sends):
    groups, capacity, features = sends[0].shape
    streams = len(sends)
    rows = jax.ShapeDtypeStruct((2, 2, groups, capacity, features), sends[0].dtype)
    any_spec = pl.BlockSpec(memory_space=pl.ANY)
    return pl.pallas_call(
        functools.partial(spread_kernel, groups),
        out_shape=[rows] * streams,
        in_specs=[any_spec] * streams,
        out_specs=[any_spec] * streams,
        scratch_shapes=[
            pltpu.SemaphoreType.DMA((streams, groups)),
            pltpu.SemaphoreType.DMA((streams, groups)),
            pltpu.SemaphoreType.DMA((streams, 2, groups)),
            pltpu.SemaphoreType.DMA((streams, 2, groups)),
            pltpu.SemaphoreType.DMA((streams, 2, groups)),
            pltpu.SemaphoreType.DMA((streams, 2, groups)),
        ],
        compiler_params=pltpu.CompilerParams(collective_id=0, has_side_effects=True),
    )(*sends)


def collect_kernel(groups, mine, other, back, landed, summed, swap_recv, swap_send, back_recv, back_send):
    streams = mine.shape[0]
    section = lax.axis_index("section")
    ex = lax.axis_index("ex")
    em = lax.axis_index("em")
    ep = lax.axis_index("ep")
    ec = lax.axis_index("ec")
    me = ex * 2 + em
    partner = (section, ex, em, 1 - ep, ec)

    def peer(g):
        return (section, g // 2, g % 2, ep, ec)

    barrier = pltpu.get_barrier_semaphore()
    for d in range(1, groups):
        pl.semaphore_signal(barrier, inc=1, device_id=peer((me + d) % groups), device_id_type=MESH_IDS)
    pl.semaphore_signal(barrier, inc=1, device_id=partner, device_id_type=MESH_IDS)
    pl.semaphore_wait(barrier, groups)

    def swap(s, g):
        return pltpu.make_async_remote_copy(
            src_ref=other.at[s, g],
            dst_ref=landed.at[s, g],
            send_sem=swap_send.at[s, g],
            recv_sem=swap_recv.at[s, g],
            device_id=partner,
            device_id_type=MESH_IDS,
        )

    def reply(s, g):
        return pltpu.make_async_remote_copy(
            src_ref=summed.at[s, g],
            dst_ref=back.at[s, me],
            send_sem=back_send.at[s, g],
            recv_sem=back_recv.at[s, me],
            device_id=peer(g),
            device_id_type=MESH_IDS,
        )

    def incoming(s, g):
        return pltpu.make_async_remote_copy(
            src_ref=summed.at[s, g],
            dst_ref=back.at[s, g],
            send_sem=back_send.at[s, g],
            recv_sem=back_recv.at[s, g],
            device_id=peer(g),
            device_id_type=MESH_IDS,
        )

    for s in range(streams):
        for d in range(1, groups + 1):
            swap(s, (me + d) % groups).start()
    local = []
    for s in range(streams):
        for d in range(1, groups + 1):
            g = (me + d) % groups
            swap(s, g).wait_recv()
            summed[s, g] = (mine[s, g] + landed[s, g].astype(jnp.float32)).astype(summed.dtype)
            if d < groups:
                reply(s, g).start()
            else:
                copy = pltpu.make_async_copy(summed.at[s, g], back.at[s, me], back_recv.at[s, me])
                copy.start()
                local.append(copy)
    for s in range(streams):
        local[s].wait()
        for d in range(1, groups):
            incoming(s, (me + d) % groups).wait_recv()
    for s in range(streams):
        for d in range(1, groups + 1):
            swap(s, (me + d) % groups).wait_send()
        for d in range(1, groups):
            reply(s, (me + d) % groups).wait_send()


def collect_from_holders(*parts):
    mine, other = [], []
    for part in parts:
        swapped = lax.all_to_all(part, "ec", split_axis=0, concat_axis=0, tiled=True)
        pair = swapped[0].astype(jnp.float32) + swapped[1].astype(jnp.float32)
        mine.append(pair[0])
        other.append(pair[1].astype(jnp.bfloat16))
    mine = jnp.stack(mine)
    other = jnp.stack(other)
    streams, groups = mine.shape[:2]
    any_spec = pl.BlockSpec(memory_space=pl.ANY)
    back = pl.pallas_call(
        functools.partial(collect_kernel, groups),
        out_shape=jax.ShapeDtypeStruct(other.shape, jnp.bfloat16),
        in_specs=[pl.BlockSpec(memory_space=pltpu.VMEM), any_spec],
        out_specs=any_spec,
        scratch_shapes=[
            pltpu.VMEM(other.shape, jnp.bfloat16),
            pltpu.VMEM(other.shape, jnp.bfloat16),
            pltpu.SemaphoreType.DMA((streams, groups)),
            pltpu.SemaphoreType.DMA((streams, groups)),
            pltpu.SemaphoreType.DMA((streams, groups)),
            pltpu.SemaphoreType.DMA((streams, groups)),
        ],
        compiler_params=pltpu.CompilerParams(collective_id=1, has_side_effects=True),
    )(mine, other)
    return [back[s] for s in range(streams)]


def body(
    embedded,
    forward_held,
    forward_route,
    forward_weight,
    loss_cotangent,
    backward_held,
    backward_route,
    backward_weight,
    saved_gate,
    saved_up,
    gate_weight,
    up_weight,
    down_weight,
    steering,
):
    section_count = lax.axis_size("section")
    section_index = lax.axis_index("section")
    group_count = lax.axis_size(GROUP)
    holder_count = lax.axis_size(HOLDERS)
    local_hidden = gate_weight.shape[2]
    expert_count = group_count
    device_count = group_count * holder_count
    capacity = saved_gate.shape[1] // device_count
    feature_count = embedded.shape[1]
    rows_shape = (device_count * capacity, feature_count)
    arriving = shifted(forward_held, "section", 1)[0]
    forward_in = jnp.where(section_index == 0, embedded, arriving)
    returning = shifted(backward_held, "section", -1)[0]
    backward_in = jnp.where(section_index == section_count - 1, loss_cotangent, returning)
    direction = steering[0]
    unit_dir = direction / jnp.sqrt(jnp.sum(direction * direction) + 1e-06)
    weights = (gate_weight[0], up_weight[0], down_weight[0])

    forward_layout = dispatch_layout(forward_route[0, :, 0], expert_count, capacity)
    forward_send = jnp.dot(forward_layout, forward_in, preferred_element_type=jnp.float32).astype(
        jnp.bfloat16
    )

    backward_dy = backward_in.astype(jnp.float32)
    along_dir = jnp.sum(backward_dy * unit_dir[None, :], axis=1)
    sent_rows = (
        backward_weight[0][:, None] * (backward_dy - along_dir[:, None] * unit_dir[None, :])
    ).astype(jnp.bfloat16)
    backward_layout = dispatch_layout(backward_route[0, :, 0], expert_count, capacity)
    backward_send = jnp.dot(backward_layout, sent_rows, preferred_element_type=jnp.float32).astype(
        jnp.bfloat16
    )
    forward_rows, backward_rows = spread_to_holders(
        forward_send.reshape(expert_count, capacity, feature_count),
        backward_send.reshape(expert_count, capacity, feature_count),
    )

    flip = lax.axis_index("ep") == 1

    def reorder(saved):
        grouped = saved[0].reshape(group_count, 2, 2, capacity, local_hidden).transpose(2, 1, 0, 3, 4)
        grouped = jnp.where(flip, grouped[:, ::-1], grouped)
        return grouped.reshape(device_count * capacity, local_hidden)

    forward_part = expert_forward(forward_rows.reshape(rows_shape), weights)
    backward_part = expert_backward(
        backward_rows.reshape(rows_shape), reorder(saved_gate), reorder(saved_up), weights
    )
    forward_back, backward_back = collect_from_holders(
        forward_part.reshape(2, 2, group_count, capacity, feature_count),
        backward_part.reshape(2, 2, group_count, capacity, feature_count),
    )
    forward_back = forward_back.reshape(expert_count * capacity, feature_count)
    backward_back = backward_back.reshape(expert_count * capacity, feature_count)

    contract = (((0,), (0,)), ((), ()))
    picked = lax.dot_general(forward_layout, forward_back, contract, preferred_element_type=jnp.float32)
    mixed_rows = forward_weight[0][:, None] * picked
    coefficient = jnp.sum(mixed_rows * unit_dir[None, :], axis=1)
    forward_out = (
        forward_in.astype(jnp.float32) + mixed_rows - coefficient[:, None] * unit_dir[None, :]
    ).astype(jnp.bfloat16)
    returned = lax.dot_general(
        backward_layout, backward_back, contract, preferred_element_type=jnp.float32
    )
    backward_out = (backward_dy + returned).astype(jnp.bfloat16)
    return (forward_out[None], coefficient[None], backward_out[None])


def solution(mesh):
    sections = mesh.shape["section"]
    experts = mesh.shape["expert"]
    fine = Mesh(
        np.asarray(mesh.devices).reshape(sections, experts // 8, 2, 2, 2),
        ("section",) + EXPERT_AXES,
    )
    E = EXPERT_AXES
    in_specs = (
        P(E, None),
        P("section", E, None),
        P("section", E, None),
        P("section", E),
        P(E, None),
        P("section", E, None),
        P("section", E, None),
        P("section", E),
        P("section", None, E),
        P("section", None, E),
        P("section", None, E),
        P("section", None, E),
        P("section", E, None),
        P("section", None),
    )
    out_specs = (P("section", E, None), P("section", E), P("section", E, None))
    return jax.shard_map(body, mesh=fine, in_specs=in_specs, out_specs=out_specs, check_vma=False)
```

```python
import functools

import jax
import jax.numpy as jnp
import numpy as np
from jax import lax
from jax.experimental import pallas as pl
from jax.experimental.pallas import tpu as pltpu
from jax.sharding import Mesh
from jax.sharding import PartitionSpec as P

H = 1024
EXPERT_AXES = ("ex", "em", "ep", "ec")
GROUP = ("ex", "em")
HOLDERS = ("ep", "ec")
MESH_IDS = pl.DeviceIdType.MESH


def shifted(value, axis, by):
    devices = lax.axis_size(axis)
    pairs = [(i, i + by) for i in range(devices) if 0 <= i + by < devices]
    return lax.ppermute(value, axis, pairs)


def dispatch_layout(expert_ids, expert_count, capacity):
    onehot = (expert_ids[:, None] == jnp.arange(expert_count, dtype=jnp.int32)[None, :]).astype(
        jnp.int32
    )
    earlier = jnp.cumsum(onehot, axis=0) - onehot
    position = jnp.sum(earlier * onehot, axis=1)
    target = expert_ids * capacity + position
    return (
        jnp.arange(expert_count * capacity, dtype=jnp.int32)[:, None] == target[None, :]
    ).astype(jnp.bfloat16)


def expert_forward(slot_rows, weights):
    gate_cols, up_cols, down_rows = weights
    gate_pre = jnp.dot(slot_rows, gate_cols, preferred_element_type=jnp.float32)
    up_pre = jnp.dot(slot_rows, up_cols, preferred_element_type=jnp.float32)
    hidden = (jax.nn.silu(gate_pre) * up_pre).astype(jnp.bfloat16)
    return jnp.dot(hidden, down_rows, preferred_element_type=jnp.float32).astype(jnp.bfloat16)


def expert_backward(slot_rows, gate_saved, up_saved, weights):
    gate_cols, up_cols, down_rows = weights
    contract = (((1,), (1,)), ((), ()))
    grad_hidden = lax.dot_general(
        slot_rows, down_rows, contract, preferred_element_type=jnp.float32
    )
    gate_pre = gate_saved.astype(jnp.float32)
    up_pre = up_saved.astype(jnp.float32)
    sigmoid_gate = jax.nn.sigmoid(gate_pre)
    grad_gate = (
        grad_hidden * up_pre * sigmoid_gate * (1.0 + gate_pre * (1.0 - sigmoid_gate))
    ).astype(jnp.bfloat16)
    grad_up = (grad_hidden * gate_pre * sigmoid_gate).astype(jnp.bfloat16)
    grad_part = lax.dot_general(grad_gate, gate_cols, contract, preferred_element_type=jnp.float32)
    grad_part = grad_part + lax.dot_general(
        grad_up, up_cols, contract, preferred_element_type=jnp.float32
    )
    return grad_part.astype(jnp.bfloat16)


def swap_pair(value):
    return lax.ppermute(value, "ep", [(0, 1), (1, 0)])


def spread_kernel(groups, *refs):
    streams = (len(refs) - 6) // 2
    sends = refs[:streams]
    rows = refs[streams : 2 * streams]
    first_recv, first_send, pair_recv, pair_send, near_recv, near_send = refs[2 * streams : 2 * streams + 6]
    section = lax.axis_index("section")
    ex = lax.axis_index("ex")
    em = lax.axis_index("em")
    ep = lax.axis_index("ep")
    ec = lax.axis_index("ec")
    me = ex * 2 + em
    partner = (section, ex, em, 1 - ep, ec)
    sibling = (section, ex, em, ep, 1 - ec)

    def peer(g):
        return (section, g // 2, g % 2, ep, ec)

    barrier = pltpu.get_barrier_semaphore()
    for d in range(1, groups):
        pl.semaphore_signal(barrier, inc=1, device_id=peer((me + d) % groups), device_id_type=MESH_IDS)
    pl.semaphore_signal(barrier, inc=1, device_id=partner, device_id_type=MESH_IDS)
    pl.semaphore_signal(barrier, inc=1, device_id=sibling, device_id_type=MESH_IDS)
    pl.semaphore_wait(barrier, groups + 1)

    def first_copy(s, g, target):
        return pltpu.make_async_remote_copy(
            src_ref=sends[s].at[g],
            dst_ref=rows[s].at[ec, 0, me],
            send_sem=first_send.at[s, g],
            recv_sem=first_recv.at[s, me],
            device_id=target,
            device_id_type=MESH_IDS,
        )

    def arrived(s, g):
        return pltpu.make_async_remote_copy(
            src_ref=sends[s].at[g],
            dst_ref=rows[s].at[ec, 0, g],
            send_sem=first_send.at[s, g],
            recv_sem=first_recv.at[s, g],
            device_id=peer(g),
            device_id_type=MESH_IDS,
        )

    def relay(s, q, g, target, recv, send, slot):
        return pltpu.make_async_remote_copy(
            src_ref=rows[s].at[ec, q, g],
            dst_ref=rows[s].at[ec, slot, g],
            send_sem=send.at[s, q, g],
            recv_sem=recv.at[s, q, g],
            device_id=target,
            device_id_type=MESH_IDS,
        )

    local = []
    for s in range(streams):
        copy = pltpu.make_async_copy(sends[s].at[me], rows[s].at[ec, 0, me], first_recv.at[s, me])
        copy.start()
        local.append(copy)
    for d in range(1, groups):
        for s in range(streams):
            g = (me + d) % groups
            first_copy(s, g, peer(g)).start()
    outgoing = []
    for d in range(groups):
        for s in range(streams):
            g = (me + groups - d) % groups
            if d > 0:
                arrived(s, g).wait_recv()
            else:
                local[s].wait()
            for target, recv, send, slot in (
                (partner, pair_recv, pair_send, 1),
                (sibling, near_recv, near_send, 0),
            ):
                copy = relay(s, 0, g, target, recv, send, slot)
                copy.start()
                outgoing.append(copy)
    for d in range(groups):
        for s in range(streams):
            g = (me + groups - d) % groups
            relay(s, 0, g, partner, pair_recv, pair_send, 1).wait_recv()
            copy = relay(s, 1, g, sibling, near_recv, near_send, 1)
            copy.start()
            outgoing.append(copy)
    for s in range(streams):
        for q in range(2):
            for g in range(groups):
                pltpu.make_async_remote_copy(
                    src_ref=rows[s].at[1 - ec, q, g],
                    dst_ref=rows[s].at[1 - ec, q, g],
                    send_sem=near_send.at[s, q, g],
                    recv_sem=near_recv.at[s, q, g],
                    device_id=sibling,
                    device_id_type=MESH_IDS,
                ).wait_recv()
    for s in range(streams):
        for d in range(1, groups):
            g = (me + d) % groups
            first_copy(s, g, peer(g)).wait_send()
    for copy in outgoing:
        copy.wait_send()


def spread_to_holders(*sends):
    groups, capacity, features = sends[0].shape
    streams = len(sends)
    rows = jax.ShapeDtypeStruct((2, 2, groups, capacity, features), sends[0].dtype)
    any_spec = pl.BlockSpec(memory_space=pl.ANY)
    return pl.pallas_call(
        functools.partial(spread_kernel, groups),
        out_shape=[rows] * streams,
        in_specs=[any_spec] * streams,
        out_specs=[any_spec] * streams,
        scratch_shapes=[
            pltpu.SemaphoreType.DMA((streams, groups)),
            pltpu.SemaphoreType.DMA((streams, groups)),
            pltpu.SemaphoreType.DMA((streams, 2, groups)),
            pltpu.SemaphoreType.DMA((streams, 2, groups)),
            pltpu.SemaphoreType.DMA((streams, 2, groups)),
            pltpu.SemaphoreType.DMA((streams, 2, groups)),
        ],
        compiler_params=pltpu.CompilerParams(collective_id=0, has_side_effects=True),
    )(*sends)


def collect_kernel(groups, mine, other, back, landed, summed, swap_recv, swap_send, back_recv, back_send):
    streams = mine.shape[0]
    section = lax.axis_index("section")
    ex = lax.axis_index("ex")
    em = lax.axis_index("em")
    ep = lax.axis_index("ep")
    ec = lax.axis_index("ec")
    me = ex * 2 + em
    partner = (section, ex, em, 1 - ep, ec)

    def peer(g):
        return (section, g // 2, g % 2, ep, ec)

    barrier = pltpu.get_barrier_semaphore()
    for d in range(1, groups):
        pl.semaphore_signal(barrier, inc=1, device_id=peer((me + d) % groups), device_id_type=MESH_IDS)
    pl.semaphore_signal(barrier, inc=1, device_id=partner, device_id_type=MESH_IDS)
    pl.semaphore_wait(barrier, groups)

    def swap(s, g):
        return pltpu.make_async_remote_copy(
            src_ref=other.at[s, g],
            dst_ref=landed.at[s, g],
            send_sem=swap_send.at[s, g],
            recv_sem=swap_recv.at[s, g],
            device_id=partner,
            device_id_type=MESH_IDS,
        )

    def reply(s, g):
        return pltpu.make_async_remote_copy(
            src_ref=summed.at[s, g],
            dst_ref=back.at[s, me],
            send_sem=back_send.at[s, g],
            recv_sem=back_recv.at[s, me],
            device_id=peer(g),
            device_id_type=MESH_IDS,
        )

    def incoming(s, g):
        return pltpu.make_async_remote_copy(
            src_ref=summed.at[s, g],
            dst_ref=back.at[s, g],
            send_sem=back_send.at[s, g],
            recv_sem=back_recv.at[s, g],
            device_id=peer(g),
            device_id_type=MESH_IDS,
        )

    for d in range(1, groups + 1):
        for s in range(streams):
            swap(s, (me + d) % groups).start()
    local = []
    for d in range(1, groups + 1):
        for s in range(streams):
            g = (me + d) % groups
            swap(s, g).wait_recv()
            summed[s, g] = (mine[s, g] + landed[s, g].astype(jnp.float32)).astype(summed.dtype)
            if d < groups:
                reply(s, g).start()
            else:
                copy = pltpu.make_async_copy(summed.at[s, g], back.at[s, me], back_recv.at[s, me])
                copy.start()
                local.append(copy)
    for s in range(streams):
        local[s].wait()
        for d in range(1, groups):
            incoming(s, (me + d) % groups).wait_recv()
    for s in range(streams):
        for d in range(1, groups + 1):
            swap(s, (me + d) % groups).wait_send()
        for d in range(1, groups):
            reply(s, (me + d) % groups).wait_send()


def collect_from_holders(*parts):
    mine, other = [], []
    for part in parts:
        swapped = lax.all_to_all(part, "ec", split_axis=0, concat_axis=0, tiled=True)
        pair = swapped[0].astype(jnp.float32) + swapped[1].astype(jnp.float32)
        mine.append(pair[0])
        other.append(pair[1].astype(jnp.bfloat16))
    mine = jnp.stack(mine)
    other = jnp.stack(other)
    streams, groups = mine.shape[:2]
    any_spec = pl.BlockSpec(memory_space=pl.ANY)
    back = pl.pallas_call(
        functools.partial(collect_kernel, groups),
        out_shape=jax.ShapeDtypeStruct(other.shape, jnp.bfloat16),
        in_specs=[pl.BlockSpec(memory_space=pltpu.VMEM), any_spec],
        out_specs=any_spec,
        scratch_shapes=[
            pltpu.VMEM(other.shape, jnp.bfloat16),
            pltpu.VMEM(other.shape, jnp.bfloat16),
            pltpu.SemaphoreType.DMA((streams, groups)),
            pltpu.SemaphoreType.DMA((streams, groups)),
            pltpu.SemaphoreType.DMA((streams, groups)),
            pltpu.SemaphoreType.DMA((streams, groups)),
        ],
        compiler_params=pltpu.CompilerParams(collective_id=1, has_side_effects=True),
    )(mine, other)
    return [back[s] for s in range(streams)]


def body(
    embedded,
    forward_held,
    forward_route,
    forward_weight,
    loss_cotangent,
    backward_held,
    backward_route,
    backward_weight,
    saved_gate,
    saved_up,
    gate_weight,
    up_weight,
    down_weight,
    steering,
):
    section_count = lax.axis_size("section")
    section_index = lax.axis_index("section")
    group_count = lax.axis_size(GROUP)
    holder_count = lax.axis_size(HOLDERS)
    local_hidden = gate_weight.shape[2]
    expert_count = group_count
    device_count = group_count * holder_count
    capacity = saved_gate.shape[1] // device_count
    feature_count = embedded.shape[1]
    rows_shape = (device_count * capacity, feature_count)
    arriving = shifted(forward_held, "section", 1)[0]
    forward_in = jnp.where(section_index == 0, embedded, arriving)
    returning = shifted(backward_held, "section", -1)[0]
    backward_in = jnp.where(section_index == section_count - 1, loss_cotangent, returning)
    direction = steering[0]
    unit_dir = direction / jnp.sqrt(jnp.sum(direction * direction) + 1e-06)
    weights = (gate_weight[0], up_weight[0], down_weight[0])

    forward_layout = dispatch_layout(forward_route[0, :, 0], expert_count, capacity)
    forward_send = jnp.dot(forward_layout, forward_in, preferred_element_type=jnp.float32).astype(
        jnp.bfloat16
    )

    backward_dy = backward_in.astype(jnp.float32)
    along_dir = jnp.sum(backward_dy * unit_dir[None, :], axis=1)
    sent_rows = (
        backward_weight[0][:, None] * (backward_dy - along_dir[:, None] * unit_dir[None, :])
    ).astype(jnp.bfloat16)
    backward_layout = dispatch_layout(backward_route[0, :, 0], expert_count, capacity)
    backward_send = jnp.dot(backward_layout, sent_rows, preferred_element_type=jnp.float32).astype(
        jnp.bfloat16
    )
    forward_rows, backward_rows = spread_to_holders(
        forward_send.reshape(expert_count, capacity, feature_count),
        backward_send.reshape(expert_count, capacity, feature_count),
    )

    flip = lax.axis_index("ep") == 1

    def reorder(saved):
        grouped = saved[0].reshape(group_count, 2, 2, capacity, local_hidden).transpose(2, 1, 0, 3, 4)
        grouped = jnp.where(flip, grouped[:, ::-1], grouped)
        return grouped.reshape(device_count * capacity, local_hidden)

    forward_part = expert_forward(forward_rows.reshape(rows_shape), weights)
    backward_part = expert_backward(
        backward_rows.reshape(rows_shape), reorder(saved_gate), reorder(saved_up), weights
    )
    forward_back, backward_back = collect_from_holders(
        forward_part.reshape(2, 2, group_count, capacity, feature_count),
        backward_part.reshape(2, 2, group_count, capacity, feature_count),
    )
    forward_back = forward_back.reshape(expert_count * capacity, feature_count)
    backward_back = backward_back.reshape(expert_count * capacity, feature_count)

    contract = (((0,), (0,)), ((), ()))
    picked = lax.dot_general(forward_layout, forward_back, contract, preferred_element_type=jnp.float32)
    mixed_rows = forward_weight[0][:, None] * picked
    coefficient = jnp.sum(mixed_rows * unit_dir[None, :], axis=1)
    forward_out = (
        forward_in.astype(jnp.float32) + mixed_rows - coefficient[:, None] * unit_dir[None, :]
    ).astype(jnp.bfloat16)
    returned = lax.dot_general(
        backward_layout, backward_back, contract, preferred_element_type=jnp.float32
    )
    backward_out = (backward_dy + returned).astype(jnp.bfloat16)
    return (forward_out[None], coefficient[None], backward_out[None])


def solution(mesh):
    sections = mesh.shape["section"]
    experts = mesh.shape["expert"]
    fine = Mesh(
        np.asarray(mesh.devices).reshape(sections, experts // 8, 2, 2, 2),
        ("section",) + EXPERT_AXES,
    )
    E = EXPERT_AXES
    in_specs = (
        P(E, None),
        P("section", E, None),
        P("section", E, None),
        P("section", E),
        P(E, None),
        P("section", E, None),
        P("section", E, None),
        P("section", E),
        P("section", None, E),
        P("section", None, E),
        P("section", None, E),
        P("section", None, E),
        P("section", E, None),
        P("section", None),
    )
    out_specs = (P("section", E, None), P("section", E), P("section", E, None))
    return jax.shard_map(body, mesh=fine, in_specs=in_specs, out_specs=out_specs, check_vma=False)
```

```python
import functools

import jax
import jax.numpy as jnp
import numpy as np
from jax import lax
from jax.experimental import pallas as pl
from jax.experimental.pallas import tpu as pltpu
from jax.sharding import Mesh
from jax.sharding import PartitionSpec as P

H = 1024
EXPERT_AXES = ("ex", "em", "ep", "ec")
GROUP = ("ex", "em")
HOLDERS = ("ep", "ec")
MESH_IDS = pl.DeviceIdType.MESH


def shifted(value, axis, by):
    devices = lax.axis_size(axis)
    pairs = [(i, i + by) for i in range(devices) if 0 <= i + by < devices]
    return lax.ppermute(value, axis, pairs)


def dispatch_layout(expert_ids, expert_count, capacity):
    onehot = (expert_ids[:, None] == jnp.arange(expert_count, dtype=jnp.int32)[None, :]).astype(
        jnp.int32
    )
    earlier = jnp.cumsum(onehot, axis=0) - onehot
    position = jnp.sum(earlier * onehot, axis=1)
    target = expert_ids * capacity + position
    return (
        jnp.arange(expert_count * capacity, dtype=jnp.int32)[:, None] == target[None, :]
    ).astype(jnp.bfloat16)


def expert_forward(slot_rows, weights):
    gate_cols, up_cols, down_rows = weights
    gate_pre = jnp.dot(slot_rows, gate_cols, preferred_element_type=jnp.float32)
    up_pre = jnp.dot(slot_rows, up_cols, preferred_element_type=jnp.float32)
    hidden = (jax.nn.silu(gate_pre) * up_pre).astype(jnp.bfloat16)
    return jnp.dot(hidden, down_rows, preferred_element_type=jnp.float32).astype(jnp.bfloat16)


def expert_backward(slot_rows, gate_saved, up_saved, weights):
    gate_cols, up_cols, down_rows = weights
    contract = (((1,), (1,)), ((), ()))
    grad_hidden = lax.dot_general(
        slot_rows, down_rows, contract, preferred_element_type=jnp.float32
    )
    gate_pre = gate_saved.astype(jnp.float32)
    up_pre = up_saved.astype(jnp.float32)
    sigmoid_gate = jax.nn.sigmoid(gate_pre)
    grad_gate = (
        grad_hidden * up_pre * sigmoid_gate * (1.0 + gate_pre * (1.0 - sigmoid_gate))
    ).astype(jnp.bfloat16)
    grad_up = (grad_hidden * gate_pre * sigmoid_gate).astype(jnp.bfloat16)
    grad_part = lax.dot_general(grad_gate, gate_cols, contract, preferred_element_type=jnp.float32)
    grad_part = grad_part + lax.dot_general(
        grad_up, up_cols, contract, preferred_element_type=jnp.float32
    )
    return grad_part.astype(jnp.bfloat16)


def swap_pair(value):
    return lax.ppermute(value, "ep", [(0, 1), (1, 0)])


def spread_kernel(groups, *refs):
    streams = (len(refs) - 6) // 2
    sends = refs[:streams]
    rows = refs[streams : 2 * streams]
    first_recv, first_send, pair_recv, pair_send, near_recv, near_send = refs[2 * streams : 2 * streams + 6]
    section = lax.axis_index("section")
    ex = lax.axis_index("ex")
    em = lax.axis_index("em")
    ep = lax.axis_index("ep")
    ec = lax.axis_index("ec")
    me = ex * 2 + em
    partner = (section, ex, em, 1 - ep, ec)
    sibling = (section, ex, em, ep, 1 - ec)

    def peer(g):
        return (section, g // 2, g % 2, ep, ec)

    barrier = pltpu.get_barrier_semaphore()
    for d in range(1, groups):
        pl.semaphore_signal(barrier, inc=1, device_id=peer((me + d) % groups), device_id_type=MESH_IDS)
    pl.semaphore_signal(barrier, inc=1, device_id=partner, device_id_type=MESH_IDS)
    pl.semaphore_signal(barrier, inc=1, device_id=sibling, device_id_type=MESH_IDS)
    pl.semaphore_wait(barrier, groups + 1)

    def first_copy(s, g, target):
        return pltpu.make_async_remote_copy(
            src_ref=sends[s].at[g],
            dst_ref=rows[s].at[ec, 0, me],
            send_sem=first_send.at[s, g],
            recv_sem=first_recv.at[s, me],
            device_id=target,
            device_id_type=MESH_IDS,
        )

    def arrived(s, g):
        return pltpu.make_async_remote_copy(
            src_ref=sends[s].at[g],
            dst_ref=rows[s].at[ec, 0, g],
            send_sem=first_send.at[s, g],
            recv_sem=first_recv.at[s, g],
            device_id=peer(g),
            device_id_type=MESH_IDS,
        )

    def relay(s, q, g, target, recv, send, slot):
        return pltpu.make_async_remote_copy(
            src_ref=rows[s].at[ec, q, g],
            dst_ref=rows[s].at[ec, slot, g],
            send_sem=send.at[s, q, g],
            recv_sem=recv.at[s, q, g],
            device_id=target,
            device_id_type=MESH_IDS,
        )

    local = []
    for s in range(streams):
        copy = pltpu.make_async_copy(sends[s].at[me], rows[s].at[ec, 0, me], first_recv.at[s, me])
        copy.start()
        local.append(copy)
    for d in range(1, groups):
        for s in range(streams):
            g = (me + d) % groups
            first_copy(s, g, peer(g)).start()
    outgoing = []
    for d in range(groups):
        for s in range(streams):
            g = (me + groups - d) % groups
            if d > 0:
                arrived(s, g).wait_recv()
            else:
                local[s].wait()
            for target, recv, send, slot in (
                (partner, pair_recv, pair_send, 1),
                (sibling, near_recv, near_send, 0),
            ):
                copy = relay(s, 0, g, target, recv, send, slot)
                copy.start()
                outgoing.append(copy)
    for d in range(groups):
        for s in range(streams):
            g = (me + groups - d) % groups
            relay(s, 0, g, partner, pair_recv, pair_send, 1).wait_recv()
            copy = relay(s, 1, g, sibling, near_recv, near_send, 1)
            copy.start()
            outgoing.append(copy)
    for s in range(streams):
        for q in range(2):
            for g in range(groups):
                pltpu.make_async_remote_copy(
                    src_ref=rows[s].at[1 - ec, q, g],
                    dst_ref=rows[s].at[1 - ec, q, g],
                    send_sem=near_send.at[s, q, g],
                    recv_sem=near_recv.at[s, q, g],
                    device_id=sibling,
                    device_id_type=MESH_IDS,
                ).wait_recv()
    for s in range(streams):
        for d in range(1, groups):
            g = (me + d) % groups
            first_copy(s, g, peer(g)).wait_send()
    for copy in outgoing:
        copy.wait_send()


def spread_to_holders(*sends):
    groups, capacity, features = sends[0].shape
    streams = len(sends)
    rows = jax.ShapeDtypeStruct((2, 2, groups, capacity, features), sends[0].dtype)
    any_spec = pl.BlockSpec(memory_space=pl.ANY)
    return pl.pallas_call(
        functools.partial(spread_kernel, groups),
        out_shape=[rows] * streams,
        in_specs=[any_spec] * streams,
        out_specs=[any_spec] * streams,
        scratch_shapes=[
            pltpu.SemaphoreType.DMA((streams, groups)),
            pltpu.SemaphoreType.DMA((streams, groups)),
            pltpu.SemaphoreType.DMA((streams, 2, groups)),
            pltpu.SemaphoreType.DMA((streams, 2, groups)),
            pltpu.SemaphoreType.DMA((streams, 2, groups)),
            pltpu.SemaphoreType.DMA((streams, 2, groups)),
        ],
        compiler_params=pltpu.CompilerParams(collective_id=0, has_side_effects=True),
    )(*sends)


def collect_kernel(
    groups, parts, back, near_land, other_buf, pair_land, summed,
    near_recv, near_send, swap_recv, swap_send, back_recv, back_send,
):
    streams = parts.shape[0]
    section = lax.axis_index("section")
    ex = lax.axis_index("ex")
    em = lax.axis_index("em")
    ep = lax.axis_index("ep")
    ec = lax.axis_index("ec")
    me = ex * 2 + em
    partner = (section, ex, em, 1 - ep, ec)
    sibling = (section, ex, em, ep, 1 - ec)

    def peer(g):
        return (section, g // 2, g % 2, ep, ec)

    barrier = pltpu.get_barrier_semaphore()
    for d in range(1, groups):
        pl.semaphore_signal(barrier, inc=1, device_id=peer((me + d) % groups), device_id_type=MESH_IDS)
    pl.semaphore_signal(barrier, inc=1, device_id=partner, device_id_type=MESH_IDS)
    pl.semaphore_signal(barrier, inc=1, device_id=sibling, device_id_type=MESH_IDS)
    pl.semaphore_wait(barrier, groups + 1)

    def near(s, q, g):
        return pltpu.make_async_remote_copy(
            src_ref=parts.at[s, 1 - ec, q, g],
            dst_ref=near_land.at[s, q, g],
            send_sem=near_send.at[s, q, g],
            recv_sem=near_recv.at[s, q, g],
            device_id=sibling,
            device_id_type=MESH_IDS,
        )

    def swap(s, g):
        return pltpu.make_async_remote_copy(
            src_ref=other_buf.at[s, g],
            dst_ref=pair_land.at[s, g],
            send_sem=swap_send.at[s, g],
            recv_sem=swap_recv.at[s, g],
            device_id=partner,
            device_id_type=MESH_IDS,
        )

    def reply(s, g):
        return pltpu.make_async_remote_copy(
            src_ref=summed.at[s, g],
            dst_ref=back.at[s, me],
            send_sem=back_send.at[s, g],
            recv_sem=back_recv.at[s, me],
            device_id=peer(g),
            device_id_type=MESH_IDS,
        )

    def incoming(s, g):
        return pltpu.make_async_remote_copy(
            src_ref=summed.at[s, g],
            dst_ref=back.at[s, g],
            send_sem=back_send.at[s, g],
            recv_sem=back_recv.at[s, g],
            device_id=peer(g),
            device_id_type=MESH_IDS,
        )

    for q in (1, 0):
        for d in range(1, groups + 1):
            for s in range(streams):
                near(s, q, (me + d) % groups).start()
    for d in range(1, groups + 1):
        for s in range(streams):
            g = (me + d) % groups
            near(s, 1, g).wait_recv()
            other_buf[s, g] = (
                parts[s, ec, 1, g].astype(jnp.float32) + near_land[s, 1, g].astype(jnp.float32)
            ).astype(other_buf.dtype)
            swap(s, g).start()
    local = []
    for d in range(1, groups + 1):
        for s in range(streams):
            g = (me + d) % groups
            near(s, 0, g).wait_recv()
            swap(s, g).wait_recv()
            pair = parts[s, ec, 0, g].astype(jnp.float32) + near_land[s, 0, g].astype(jnp.float32)
            summed[s, g] = (pair + pair_land[s, g].astype(jnp.float32)).astype(summed.dtype)
            if d < groups:
                reply(s, g).start()
            else:
                copy = pltpu.make_async_copy(summed.at[s, g], back.at[s, me], back_recv.at[s, me])
                copy.start()
                local.append(copy)
    for s in range(streams):
        local[s].wait()
        for d in range(1, groups):
            incoming(s, (me + d) % groups).wait_recv()
    for s in range(streams):
        for d in range(1, groups + 1):
            g = (me + d) % groups
            swap(s, g).wait_send()
            near(s, 0, g).wait_send()
            near(s, 1, g).wait_send()
        for d in range(1, groups):
            reply(s, (me + d) % groups).wait_send()


def collect_from_holders(*parts):
    parts = jnp.stack(parts)
    streams, _, _, groups, capacity, features = parts.shape
    block = (streams, groups, capacity, features)
    any_spec = pl.BlockSpec(memory_space=pl.ANY)
    back = pl.pallas_call(
        functools.partial(collect_kernel, groups),
        out_shape=jax.ShapeDtypeStruct(block, jnp.bfloat16),
        in_specs=[pl.BlockSpec(memory_space=pltpu.VMEM)],
        out_specs=any_spec,
        scratch_shapes=[
            pltpu.VMEM((streams, 2, groups, capacity, features), jnp.bfloat16),
            pltpu.VMEM(block, jnp.bfloat16),
            pltpu.VMEM(block, jnp.bfloat16),
            pltpu.VMEM(block, jnp.bfloat16),
            pltpu.SemaphoreType.DMA((streams, 2, groups)),
            pltpu.SemaphoreType.DMA((streams, 2, groups)),
            pltpu.SemaphoreType.DMA((streams, groups)),
            pltpu.SemaphoreType.DMA((streams, groups)),
            pltpu.SemaphoreType.DMA((streams, groups)),
            pltpu.SemaphoreType.DMA((streams, groups)),
        ],
        compiler_params=pltpu.CompilerParams(
            collective_id=1, has_side_effects=True, vmem_limit_bytes=60 * 1024 * 1024
        ),
    )(parts)
    return [back[s] for s in range(streams)]


def body(
    embedded,
    forward_held,
    forward_route,
    forward_weight,
    loss_cotangent,
    backward_held,
    backward_route,
    backward_weight,
    saved_gate,
    saved_up,
    gate_weight,
    up_weight,
    down_weight,
    steering,
):
    section_count = lax.axis_size("section")
    section_index = lax.axis_index("section")
    group_count = lax.axis_size(GROUP)
    holder_count = lax.axis_size(HOLDERS)
    local_hidden = gate_weight.shape[2]
    expert_count = group_count
    device_count = group_count * holder_count
    capacity = saved_gate.shape[1] // device_count
    feature_count = embedded.shape[1]
    rows_shape = (device_count * capacity, feature_count)
    arriving = shifted(forward_held, "section", 1)[0]
    forward_in = jnp.where(section_index == 0, embedded, arriving)
    returning = shifted(backward_held, "section", -1)[0]
    backward_in = jnp.where(section_index == section_count - 1, loss_cotangent, returning)
    direction = steering[0]
    unit_dir = direction / jnp.sqrt(jnp.sum(direction * direction) + 1e-06)
    weights = (gate_weight[0], up_weight[0], down_weight[0])

    forward_layout = dispatch_layout(forward_route[0, :, 0], expert_count, capacity)
    forward_send = jnp.dot(forward_layout, forward_in, preferred_element_type=jnp.float32).astype(
        jnp.bfloat16
    )

    backward_dy = backward_in.astype(jnp.float32)
    along_dir = jnp.sum(backward_dy * unit_dir[None, :], axis=1)
    sent_rows = (
        backward_weight[0][:, None] * (backward_dy - along_dir[:, None] * unit_dir[None, :])
    ).astype(jnp.bfloat16)
    backward_layout = dispatch_layout(backward_route[0, :, 0], expert_count, capacity)
    backward_send = jnp.dot(backward_layout, sent_rows, preferred_element_type=jnp.float32).astype(
        jnp.bfloat16
    )
    forward_rows, backward_rows = spread_to_holders(
        forward_send.reshape(expert_count, capacity, feature_count),
        backward_send.reshape(expert_count, capacity, feature_count),
    )

    flip = lax.axis_index("ep") == 1

    def reorder(saved):
        grouped = saved[0].reshape(group_count, 2, 2, capacity, local_hidden).transpose(2, 1, 0, 3, 4)
        grouped = jnp.where(flip, grouped[:, ::-1], grouped)
        return grouped.reshape(device_count * capacity, local_hidden)

    forward_part = expert_forward(forward_rows.reshape(rows_shape), weights)
    backward_part = expert_backward(
        backward_rows.reshape(rows_shape), reorder(saved_gate), reorder(saved_up), weights
    )
    forward_back, backward_back = collect_from_holders(
        forward_part.reshape(2, 2, group_count, capacity, feature_count),
        backward_part.reshape(2, 2, group_count, capacity, feature_count),
    )
    forward_back = forward_back.reshape(expert_count * capacity, feature_count)
    backward_back = backward_back.reshape(expert_count * capacity, feature_count)

    contract = (((0,), (0,)), ((), ()))
    picked = lax.dot_general(forward_layout, forward_back, contract, preferred_element_type=jnp.float32)
    mixed_rows = forward_weight[0][:, None] * picked
    coefficient = jnp.sum(mixed_rows * unit_dir[None, :], axis=1)
    forward_out = (
        forward_in.astype(jnp.float32) + mixed_rows - coefficient[:, None] * unit_dir[None, :]
    ).astype(jnp.bfloat16)
    returned = lax.dot_general(
        backward_layout, backward_back, contract, preferred_element_type=jnp.float32
    )
    backward_out = (backward_dy + returned).astype(jnp.bfloat16)
    return (forward_out[None], coefficient[None], backward_out[None])


def solution(mesh):
    sections = mesh.shape["section"]
    experts = mesh.shape["expert"]
    fine = Mesh(
        np.asarray(mesh.devices).reshape(sections, experts // 8, 2, 2, 2),
        ("section",) + EXPERT_AXES,
    )
    E = EXPERT_AXES
    in_specs = (
        P(E, None),
        P("section", E, None),
        P("section", E, None),
        P("section", E),
        P(E, None),
        P("section", E, None),
        P("section", E, None),
        P("section", E),
        P("section", None, E),
        P("section", None, E),
        P("section", None, E),
        P("section", None, E),
        P("section", E, None),
        P("section", None),
    )
    out_specs = (P("section", E, None), P("section", E), P("section", E, None))
    return jax.shard_map(body, mesh=fine, in_specs=in_specs, out_specs=out_specs, check_vma=False)
```

```python
import functools

import jax
import jax.numpy as jnp
import numpy as np
from jax import lax
from jax.experimental import pallas as pl
from jax.experimental.pallas import tpu as pltpu
from jax.sharding import Mesh
from jax.sharding import PartitionSpec as P

H = 1024
EXPERT_AXES = ("ex", "em", "ep", "ec")
GROUP = ("ex", "em")
HOLDERS = ("ep", "ec")
MESH_IDS = pl.DeviceIdType.MESH


def shifted(value, axis, by):
    devices = lax.axis_size(axis)
    pairs = [(i, i + by) for i in range(devices) if 0 <= i + by < devices]
    return lax.ppermute(value, axis, pairs)


def dispatch_layout(expert_ids, expert_count, capacity):
    onehot = (expert_ids[:, None] == jnp.arange(expert_count, dtype=jnp.int32)[None, :]).astype(
        jnp.int32
    )
    earlier = jnp.cumsum(onehot, axis=0) - onehot
    position = jnp.sum(earlier * onehot, axis=1)
    target = expert_ids * capacity + position
    return (
        jnp.arange(expert_count * capacity, dtype=jnp.int32)[:, None] == target[None, :]
    ).astype(jnp.bfloat16)


def expert_forward(slot_rows, weights):
    gate_cols, up_cols, down_rows = weights
    gate_pre = jnp.dot(slot_rows, gate_cols, preferred_element_type=jnp.float32)
    up_pre = jnp.dot(slot_rows, up_cols, preferred_element_type=jnp.float32)
    hidden = (jax.nn.silu(gate_pre) * up_pre).astype(jnp.bfloat16)
    return jnp.dot(hidden, down_rows, preferred_element_type=jnp.float32).astype(jnp.bfloat16)


def expert_backward(slot_rows, gate_saved, up_saved, weights):
    gate_cols, up_cols, down_rows = weights
    contract = (((1,), (1,)), ((), ()))
    grad_hidden = lax.dot_general(
        slot_rows, down_rows, contract, preferred_element_type=jnp.float32
    )
    gate_pre = gate_saved.astype(jnp.float32)
    up_pre = up_saved.astype(jnp.float32)
    sigmoid_gate = jax.nn.sigmoid(gate_pre)
    grad_gate = (
        grad_hidden * up_pre * sigmoid_gate * (1.0 + gate_pre * (1.0 - sigmoid_gate))
    ).astype(jnp.bfloat16)
    grad_up = (grad_hidden * gate_pre * sigmoid_gate).astype(jnp.bfloat16)
    grad_part = lax.dot_general(grad_gate, gate_cols, contract, preferred_element_type=jnp.float32)
    grad_part = grad_part + lax.dot_general(
        grad_up, up_cols, contract, preferred_element_type=jnp.float32
    )
    return grad_part.astype(jnp.bfloat16)


def swap_pair(value):
    return lax.ppermute(value, "ep", [(0, 1), (1, 0)])


def spread_kernel(groups, *refs):
    streams = (len(refs) - 6) // 2
    sends = refs[:streams]
    rows = refs[streams : 2 * streams]
    first_recv, first_send, pair_recv, pair_send, near_recv, near_send = refs[2 * streams : 2 * streams + 6]
    section = lax.axis_index("section")
    ex = lax.axis_index("ex")
    em = lax.axis_index("em")
    ep = lax.axis_index("ep")
    ec = lax.axis_index("ec")
    me = ex * 2 + em
    partner = (section, ex, em, 1 - ep, ec)
    sibling = (section, ex, em, ep, 1 - ec)

    def peer(g):
        return (section, g // 2, g % 2, ep, ec)

    barrier = pltpu.get_barrier_semaphore()
    for d in range(1, groups):
        pl.semaphore_signal(barrier, inc=1, device_id=peer((me + d) % groups), device_id_type=MESH_IDS)
    pl.semaphore_signal(barrier, inc=1, device_id=partner, device_id_type=MESH_IDS)
    pl.semaphore_signal(barrier, inc=1, device_id=sibling, device_id_type=MESH_IDS)
    pl.semaphore_wait(barrier, groups + 1)

    def first_copy(s, g, target):
        return pltpu.make_async_remote_copy(
            src_ref=sends[s].at[g],
            dst_ref=rows[s].at[ec, 0, me],
            send_sem=first_send.at[s, g],
            recv_sem=first_recv.at[s, me],
            device_id=target,
            device_id_type=MESH_IDS,
        )

    def arrived(s, g):
        return pltpu.make_async_remote_copy(
            src_ref=sends[s].at[g],
            dst_ref=rows[s].at[ec, 0, g],
            send_sem=first_send.at[s, g],
            recv_sem=first_recv.at[s, g],
            device_id=peer(g),
            device_id_type=MESH_IDS,
        )

    def relay(s, q, g, target, recv, send, slot):
        return pltpu.make_async_remote_copy(
            src_ref=rows[s].at[ec, q, g],
            dst_ref=rows[s].at[ec, slot, g],
            send_sem=send.at[s, q, g],
            recv_sem=recv.at[s, q, g],
            device_id=target,
            device_id_type=MESH_IDS,
        )

    local = []
    for s in range(streams):
        copy = pltpu.make_async_copy(sends[s].at[me], rows[s].at[ec, 0, me], first_recv.at[s, me])
        copy.start()
        local.append(copy)
    for d in range(1, groups):
        for s in range(streams):
            g = (me + d) % groups
            first_copy(s, g, peer(g)).start()
    outgoing = []
    for d in range(groups):
        for s in range(streams):
            g = (me + groups - d) % groups
            if d > 0:
                arrived(s, g).wait_recv()
            else:
                local[s].wait()
            for target, recv, send, slot in (
                (partner, pair_recv, pair_send, 1),
                (sibling, near_recv, near_send, 0),
            ):
                copy = relay(s, 0, g, target, recv, send, slot)
                copy.start()
                outgoing.append(copy)
    for d in range(groups):
        for s in range(streams):
            g = (me + groups - d) % groups
            relay(s, 0, g, partner, pair_recv, pair_send, 1).wait_recv()
            copy = relay(s, 1, g, sibling, near_recv, near_send, 1)
            copy.start()
            outgoing.append(copy)
    for s in range(streams):
        for q in range(2):
            for g in range(groups):
                pltpu.make_async_remote_copy(
                    src_ref=rows[s].at[1 - ec, q, g],
                    dst_ref=rows[s].at[1 - ec, q, g],
                    send_sem=near_send.at[s, q, g],
                    recv_sem=near_recv.at[s, q, g],
                    device_id=sibling,
                    device_id_type=MESH_IDS,
                ).wait_recv()
    for s in range(streams):
        for d in range(1, groups):
            g = (me + d) % groups
            first_copy(s, g, peer(g)).wait_send()
    for copy in outgoing:
        copy.wait_send()


def spread_to_holders(*sends):
    groups, capacity, features = sends[0].shape
    streams = len(sends)
    rows = jax.ShapeDtypeStruct((2, 2, groups, capacity, features), sends[0].dtype)
    any_spec = pl.BlockSpec(memory_space=pl.ANY)
    return pl.pallas_call(
        functools.partial(spread_kernel, groups),
        out_shape=[rows] * streams,
        in_specs=[any_spec] * streams,
        out_specs=[any_spec] * streams,
        scratch_shapes=[
            pltpu.SemaphoreType.DMA((streams, groups)),
            pltpu.SemaphoreType.DMA((streams, groups)),
            pltpu.SemaphoreType.DMA((streams, 2, groups)),
            pltpu.SemaphoreType.DMA((streams, 2, groups)),
            pltpu.SemaphoreType.DMA((streams, 2, groups)),
            pltpu.SemaphoreType.DMA((streams, 2, groups)),
        ],
        compiler_params=pltpu.CompilerParams(collective_id=0, has_side_effects=True),
    )(*sends)


def collect_kernel(groups, *refs):
    streams = len(refs) - 11
    parts = refs[:streams]
    back, near_land, other_buf, pair_land, summed = refs[streams : streams + 5]
    near_recv, near_send, swap_recv, swap_send, back_recv, back_send = refs[streams + 5 :]
    section = lax.axis_index("section")
    ex = lax.axis_index("ex")
    em = lax.axis_index("em")
    ep = lax.axis_index("ep")
    ec = lax.axis_index("ec")
    me = ex * 2 + em
    partner = (section, ex, em, 1 - ep, ec)
    sibling = (section, ex, em, ep, 1 - ec)

    def peer(g):
        return (section, g // 2, g % 2, ep, ec)

    barrier = pltpu.get_barrier_semaphore()
    for d in range(1, groups):
        pl.semaphore_signal(barrier, inc=1, device_id=peer((me + d) % groups), device_id_type=MESH_IDS)
    pl.semaphore_signal(barrier, inc=1, device_id=partner, device_id_type=MESH_IDS)
    pl.semaphore_signal(barrier, inc=1, device_id=sibling, device_id_type=MESH_IDS)
    pl.semaphore_wait(barrier, groups + 1)

    def near(s, q, g):
        return pltpu.make_async_remote_copy(
            src_ref=parts[s].at[1 - ec, q, g],
            dst_ref=near_land.at[s, q, g],
            send_sem=near_send.at[s, q, g],
            recv_sem=near_recv.at[s, q, g],
            device_id=sibling,
            device_id_type=MESH_IDS,
        )

    def swap(s, g):
        return pltpu.make_async_remote_copy(
            src_ref=other_buf.at[s, g],
            dst_ref=pair_land.at[s, g],
            send_sem=swap_send.at[s, g],
            recv_sem=swap_recv.at[s, g],
            device_id=partner,
            device_id_type=MESH_IDS,
        )

    def reply(s, g):
        return pltpu.make_async_remote_copy(
            src_ref=summed.at[s, g],
            dst_ref=back.at[s, me],
            send_sem=back_send.at[s, g],
            recv_sem=back_recv.at[s, me],
            device_id=peer(g),
            device_id_type=MESH_IDS,
        )

    def incoming(s, g):
        return pltpu.make_async_remote_copy(
            src_ref=summed.at[s, g],
            dst_ref=back.at[s, g],
            send_sem=back_send.at[s, g],
            recv_sem=back_recv.at[s, g],
            device_id=peer(g),
            device_id_type=MESH_IDS,
        )

    for q in (1, 0):
        for d in range(1, groups + 1):
            for s in range(streams):
                near(s, q, (me + d) % groups).start()
    for d in range(1, groups + 1):
        for s in range(streams):
            g = (me + d) % groups
            near(s, 1, g).wait_recv()
            other_buf[s, g] = (
                parts[s][ec, 1, g].astype(jnp.float32) + near_land[s, 1, g].astype(jnp.float32)
            ).astype(other_buf.dtype)
            swap(s, g).start()
    local = []
    for d in range(1, groups + 1):
        for s in range(streams):
            g = (me + d) % groups
            near(s, 0, g).wait_recv()
            swap(s, g).wait_recv()
            pair = parts[s][ec, 0, g].astype(jnp.float32) + near_land[s, 0, g].astype(jnp.float32)
            summed[s, g] = (pair + pair_land[s, g].astype(jnp.float32)).astype(summed.dtype)
            if d < groups:
                reply(s, g).start()
            else:
                copy = pltpu.make_async_copy(summed.at[s, g], back.at[s, me], back_recv.at[s, me])
                copy.start()
                local.append(copy)
    for s in range(streams):
        local[s].wait()
        for d in range(1, groups):
            incoming(s, (me + d) % groups).wait_recv()
    for s in range(streams):
        for d in range(1, groups + 1):
            g = (me + d) % groups
            swap(s, g).wait_send()
            near(s, 0, g).wait_send()
            near(s, 1, g).wait_send()
        for d in range(1, groups):
            reply(s, (me + d) % groups).wait_send()


def collect_from_holders(*parts):
    streams = len(parts)
    _, _, groups, capacity, features = parts[0].shape
    block = (streams, groups, capacity, features)
    any_spec = pl.BlockSpec(memory_space=pl.ANY)
    back = pl.pallas_call(
        functools.partial(collect_kernel, groups),
        out_shape=jax.ShapeDtypeStruct(block, jnp.bfloat16),
        in_specs=[pl.BlockSpec(memory_space=pltpu.VMEM)] * streams,
        out_specs=any_spec,
        scratch_shapes=[
            pltpu.VMEM((streams, 2, groups, capacity, features), jnp.bfloat16),
            pltpu.VMEM(block, jnp.bfloat16),
            pltpu.VMEM(block, jnp.bfloat16),
            pltpu.VMEM(block, jnp.bfloat16),
            pltpu.SemaphoreType.DMA((streams, 2, groups)),
            pltpu.SemaphoreType.DMA((streams, 2, groups)),
            pltpu.SemaphoreType.DMA((streams, groups)),
            pltpu.SemaphoreType.DMA((streams, groups)),
            pltpu.SemaphoreType.DMA((streams, groups)),
            pltpu.SemaphoreType.DMA((streams, groups)),
        ],
        compiler_params=pltpu.CompilerParams(
            collective_id=1, has_side_effects=True, vmem_limit_bytes=60 * 1024 * 1024
        ),
    )(*parts)
    return [back[s] for s in range(streams)]


def body(
    embedded,
    forward_held,
    forward_route,
    forward_weight,
    loss_cotangent,
    backward_held,
    backward_route,
    backward_weight,
    saved_gate,
    saved_up,
    gate_weight,
    up_weight,
    down_weight,
    steering,
):
    section_count = lax.axis_size("section")
    section_index = lax.axis_index("section")
    group_count = lax.axis_size(GROUP)
    holder_count = lax.axis_size(HOLDERS)
    local_hidden = gate_weight.shape[2]
    expert_count = group_count
    device_count = group_count * holder_count
    capacity = saved_gate.shape[1] // device_count
    feature_count = embedded.shape[1]
    rows_shape = (device_count * capacity, feature_count)
    arriving = shifted(forward_held, "section", 1)[0]
    forward_in = jnp.where(section_index == 0, embedded, arriving)
    returning = shifted(backward_held, "section", -1)[0]
    backward_in = jnp.where(section_index == section_count - 1, loss_cotangent, returning)
    direction = steering[0]
    unit_dir = direction / jnp.sqrt(jnp.sum(direction * direction) + 1e-06)
    weights = (gate_weight[0], up_weight[0], down_weight[0])

    forward_layout = dispatch_layout(forward_route[0, :, 0], expert_count, capacity)
    forward_send = jnp.dot(forward_layout, forward_in, preferred_element_type=jnp.float32).astype(
        jnp.bfloat16
    )

    backward_dy = backward_in.astype(jnp.float32)
    along_dir = jnp.sum(backward_dy * unit_dir[None, :], axis=1)
    sent_rows = (
        backward_weight[0][:, None] * (backward_dy - along_dir[:, None] * unit_dir[None, :])
    ).astype(jnp.bfloat16)
    backward_layout = dispatch_layout(backward_route[0, :, 0], expert_count, capacity)
    backward_send = jnp.dot(backward_layout, sent_rows, preferred_element_type=jnp.float32).astype(
        jnp.bfloat16
    )
    forward_rows, backward_rows = spread_to_holders(
        forward_send.reshape(expert_count, capacity, feature_count),
        backward_send.reshape(expert_count, capacity, feature_count),
    )

    flip = lax.axis_index("ep") == 1

    def reorder(saved):
        grouped = saved[0].reshape(group_count, 2, 2, capacity, local_hidden).transpose(2, 1, 0, 3, 4)
        grouped = jnp.where(flip, grouped[:, ::-1], grouped)
        return grouped.reshape(device_count * capacity, local_hidden)

    forward_part = expert_forward(forward_rows.reshape(rows_shape), weights)
    backward_part = expert_backward(
        backward_rows.reshape(rows_shape), reorder(saved_gate), reorder(saved_up), weights
    )
    forward_back, backward_back = collect_from_holders(
        forward_part.reshape(2, 2, group_count, capacity, feature_count),
        backward_part.reshape(2, 2, group_count, capacity, feature_count),
    )
    forward_back = forward_back.reshape(expert_count * capacity, feature_count)
    backward_back = backward_back.reshape(expert_count * capacity, feature_count)

    contract = (((0,), (0,)), ((), ()))
    picked = lax.dot_general(forward_layout, forward_back, contract, preferred_element_type=jnp.float32)
    mixed_rows = forward_weight[0][:, None] * picked
    coefficient = jnp.sum(mixed_rows * unit_dir[None, :], axis=1)
    forward_out = (
        forward_in.astype(jnp.float32) + mixed_rows - coefficient[:, None] * unit_dir[None, :]
    ).astype(jnp.bfloat16)
    returned = lax.dot_general(
        backward_layout, backward_back, contract, preferred_element_type=jnp.float32
    )
    backward_out = (backward_dy + returned).astype(jnp.bfloat16)
    return (forward_out[None], coefficient[None], backward_out[None])


def solution(mesh):
    sections = mesh.shape["section"]
    experts = mesh.shape["expert"]
    fine = Mesh(
        np.asarray(mesh.devices).reshape(sections, experts // 8, 2, 2, 2),
        ("section",) + EXPERT_AXES,
    )
    E = EXPERT_AXES
    in_specs = (
        P(E, None),
        P("section", E, None),
        P("section", E, None),
        P("section", E),
        P(E, None),
        P("section", E, None),
        P("section", E, None),
        P("section", E),
        P("section", None, E),
        P("section", None, E),
        P("section", None, E),
        P("section", None, E),
        P("section", E, None),
        P("section", None),
    )
    out_specs = (P("section", E, None), P("section", E), P("section", E, None))
    return jax.shard_map(body, mesh=fine, in_specs=in_specs, out_specs=out_specs, check_vma=False)
```

```python
import functools

import jax
import jax.numpy as jnp
import numpy as np
from jax import lax
from jax.experimental import pallas as pl
from jax.experimental.pallas import tpu as pltpu
from jax.sharding import Mesh
from jax.sharding import PartitionSpec as P

H = 1024
EXPERT_AXES = ("ex", "em", "ep", "ec")
GROUP = ("ex", "em")
HOLDERS = ("ep", "ec")
MESH_IDS = pl.DeviceIdType.MESH


def shifted(value, axis, by):
    devices = lax.axis_size(axis)
    pairs = [(i, i + by) for i in range(devices) if 0 <= i + by < devices]
    return lax.ppermute(value, axis, pairs)


def dispatch_layout(expert_ids, expert_count, capacity):
    onehot = (expert_ids[:, None] == jnp.arange(expert_count, dtype=jnp.int32)[None, :]).astype(
        jnp.int32
    )
    earlier = jnp.cumsum(onehot, axis=0) - onehot
    position = jnp.sum(earlier * onehot, axis=1)
    target = expert_ids * capacity + position
    return (
        jnp.arange(expert_count * capacity, dtype=jnp.int32)[:, None] == target[None, :]
    ).astype(jnp.bfloat16)


def expert_forward(slot_rows, weights):
    gate_cols, up_cols, down_rows = weights
    gate_pre = jnp.dot(slot_rows, gate_cols, preferred_element_type=jnp.float32)
    up_pre = jnp.dot(slot_rows, up_cols, preferred_element_type=jnp.float32)
    hidden = (jax.nn.silu(gate_pre) * up_pre).astype(jnp.bfloat16)
    return jnp.dot(hidden, down_rows, preferred_element_type=jnp.float32).astype(jnp.bfloat16)


def expert_backward(slot_rows, gate_saved, up_saved, weights):
    gate_cols, up_cols, down_rows = weights
    contract = (((1,), (1,)), ((), ()))
    grad_hidden = lax.dot_general(
        slot_rows, down_rows, contract, preferred_element_type=jnp.float32
    )
    gate_pre = gate_saved.astype(jnp.float32)
    up_pre = up_saved.astype(jnp.float32)
    sigmoid_gate = jax.nn.sigmoid(gate_pre)
    grad_gate = (
        grad_hidden * up_pre * sigmoid_gate * (1.0 + gate_pre * (1.0 - sigmoid_gate))
    ).astype(jnp.bfloat16)
    grad_up = (grad_hidden * gate_pre * sigmoid_gate).astype(jnp.bfloat16)
    grad_part = lax.dot_general(grad_gate, gate_cols, contract, preferred_element_type=jnp.float32)
    grad_part = grad_part + lax.dot_general(
        grad_up, up_cols, contract, preferred_element_type=jnp.float32
    )
    return grad_part.astype(jnp.bfloat16)


def swap_pair(value):
    return lax.ppermute(value, "ep", [(0, 1), (1, 0)])


def spread_kernel(groups, *refs):
    streams = (len(refs) - 4) // 2
    sends = refs[:streams]
    rows = refs[streams : 2 * streams]
    first_recv, first_send, pair_recv, pair_send = refs[2 * streams :]
    section = lax.axis_index("section")
    ex = lax.axis_index("ex")
    em = lax.axis_index("em")
    ep = lax.axis_index("ep")
    ec = lax.axis_index("ec")
    me = ex * 2 + em
    partner = (section, ex, em, 1 - ep, ec)

    def peer(g):
        return (section, g // 2, g % 2, ep, ec)

    barrier = pltpu.get_barrier_semaphore()
    for d in range(1, groups):
        pl.semaphore_signal(barrier, inc=1, device_id=peer((me + d) % groups), device_id_type=MESH_IDS)
    pl.semaphore_signal(barrier, inc=1, device_id=partner, device_id_type=MESH_IDS)
    pl.semaphore_wait(barrier, groups)

    def first_copy(s, g):
        return pltpu.make_async_remote_copy(
            src_ref=sends[s].at[g],
            dst_ref=rows[s].at[0, me],
            send_sem=first_send.at[s, g],
            recv_sem=first_recv.at[s, me],
            device_id=peer(g),
            device_id_type=MESH_IDS,
        )

    def arrived(s, g):
        return pltpu.make_async_remote_copy(
            src_ref=sends[s].at[g],
            dst_ref=rows[s].at[0, g],
            send_sem=first_send.at[s, g],
            recv_sem=first_recv.at[s, g],
            device_id=peer(g),
            device_id_type=MESH_IDS,
        )

    def relay(s, g):
        return pltpu.make_async_remote_copy(
            src_ref=rows[s].at[0, g],
            dst_ref=rows[s].at[1, g],
            send_sem=pair_send.at[s, g],
            recv_sem=pair_recv.at[s, g],
            device_id=partner,
            device_id_type=MESH_IDS,
        )

    local = []
    for s in range(streams):
        copy = pltpu.make_async_copy(sends[s].at[me], rows[s].at[0, me], first_recv.at[s, me])
        copy.start()
        local.append(copy)
    for d in range(1, groups):
        for s in range(streams):
            first_copy(s, (me + d) % groups).start()
    for d in range(groups):
        for s in range(streams):
            g = (me + groups - d) % groups
            if d > 0:
                arrived(s, g).wait_recv()
            else:
                local[s].wait()
            relay(s, g).start()
    for d in range(groups):
        for s in range(streams):
            relay(s, (me + groups - d) % groups).wait_recv()
    for s in range(streams):
        for d in range(1, groups):
            first_copy(s, (me + d) % groups).wait_send()
        for g in range(groups):
            relay(s, g).wait_send()


def spread_to_holders(*sends):
    groups, capacity, features = sends[0].shape
    streams = len(sends)
    rows = jax.ShapeDtypeStruct((2, groups, capacity, features), sends[0].dtype)
    any_spec = pl.BlockSpec(memory_space=pl.ANY)
    return pl.pallas_call(
        functools.partial(spread_kernel, groups),
        out_shape=[rows] * streams,
        in_specs=[any_spec] * streams,
        out_specs=[any_spec] * streams,
        scratch_shapes=[
            pltpu.SemaphoreType.DMA((streams, groups)),
            pltpu.SemaphoreType.DMA((streams, groups)),
            pltpu.SemaphoreType.DMA((streams, groups)),
            pltpu.SemaphoreType.DMA((streams, groups)),
        ],
        compiler_params=pltpu.CompilerParams(collective_id=0, has_side_effects=True),
    )(*sends)


def collect_kernel(groups, mine, other, back, landed, summed, swap_recv, swap_send, back_recv, back_send):
    streams = mine.shape[0]
    section = lax.axis_index("section")
    ex = lax.axis_index("ex")
    em = lax.axis_index("em")
    ep = lax.axis_index("ep")
    ec = lax.axis_index("ec")
    me = ex * 2 + em
    partner = (section, ex, em, 1 - ep, ec)

    def peer(g):
        return (section, g // 2, g % 2, ep, ec)

    barrier = pltpu.get_barrier_semaphore()
    for d in range(1, groups):
        pl.semaphore_signal(barrier, inc=1, device_id=peer((me + d) % groups), device_id_type=MESH_IDS)
    pl.semaphore_signal(barrier, inc=1, device_id=partner, device_id_type=MESH_IDS)
    pl.semaphore_wait(barrier, groups)

    def swap(s, g):
        return pltpu.make_async_remote_copy(
            src_ref=other.at[s, g],
            dst_ref=landed.at[s, g],
            send_sem=swap_send.at[s, g],
            recv_sem=swap_recv.at[s, g],
            device_id=partner,
            device_id_type=MESH_IDS,
        )

    def reply(s, g):
        return pltpu.make_async_remote_copy(
            src_ref=summed.at[s, g],
            dst_ref=back.at[s, me],
            send_sem=back_send.at[s, g],
            recv_sem=back_recv.at[s, me],
            device_id=peer(g),
            device_id_type=MESH_IDS,
        )

    def incoming(s, g):
        return pltpu.make_async_remote_copy(
            src_ref=summed.at[s, g],
            dst_ref=back.at[s, g],
            send_sem=back_send.at[s, g],
            recv_sem=back_recv.at[s, g],
            device_id=peer(g),
            device_id_type=MESH_IDS,
        )

    for s in range(streams):
        for d in range(1, groups + 1):
            swap(s, (me + d) % groups).start()
    local = []
    for s in range(streams):
        for d in range(1, groups + 1):
            g = (me + d) % groups
            swap(s, g).wait_recv()
            summed[s, g] = (mine[s, g] + landed[s, g].astype(jnp.float32)).astype(summed.dtype)
            if d < groups:
                reply(s, g).start()
            else:
                copy = pltpu.make_async_copy(summed.at[s, g], back.at[s, me], back_recv.at[s, me])
                copy.start()
                local.append(copy)
    for s in range(streams):
        local[s].wait()
        for d in range(1, groups):
            incoming(s, (me + d) % groups).wait_recv()
    for s in range(streams):
        for d in range(1, groups + 1):
            swap(s, (me + d) % groups).wait_send()
        for d in range(1, groups):
            reply(s, (me + d) % groups).wait_send()


def collect_from_holders(mine, other):
    streams, groups = mine.shape[:2]
    any_spec = pl.BlockSpec(memory_space=pl.ANY)
    return pl.pallas_call(
        functools.partial(collect_kernel, groups),
        out_shape=jax.ShapeDtypeStruct(other.shape, jnp.bfloat16),
        in_specs=[pl.BlockSpec(memory_space=pltpu.VMEM), any_spec],
        out_specs=any_spec,
        scratch_shapes=[
            pltpu.VMEM(other.shape, jnp.bfloat16),
            pltpu.VMEM(other.shape, jnp.bfloat16),
            pltpu.SemaphoreType.DMA((streams, groups)),
            pltpu.SemaphoreType.DMA((streams, groups)),
            pltpu.SemaphoreType.DMA((streams, groups)),
            pltpu.SemaphoreType.DMA((streams, groups)),
        ],
        compiler_params=pltpu.CompilerParams(collective_id=1, has_side_effects=True),
    )(mine, other)


def body(
    embedded,
    forward_held,
    forward_route,
    forward_weight,
    loss_cotangent,
    backward_held,
    backward_route,
    backward_weight,
    saved_gate,
    saved_up,
    gate_weight,
    up_weight,
    down_weight,
    steering,
):
    section_count = lax.axis_size("section")
    section_index = lax.axis_index("section")
    group_count = lax.axis_size(GROUP)
    holder_count = lax.axis_size(HOLDERS)
    local_hidden = gate_weight.shape[2]
    expert_count = group_count
    device_count = group_count * holder_count
    capacity = saved_gate.shape[1] // device_count
    feature_count = embedded.shape[1]
    rows_shape = (device_count * capacity, feature_count)
    arriving = shifted(forward_held, "section", 1)[0]
    forward_in = jnp.where(section_index == 0, embedded, arriving)
    returning = shifted(backward_held, "section", -1)[0]
    backward_in = jnp.where(section_index == section_count - 1, loss_cotangent, returning)
    direction = steering[0]
    unit_dir = direction / jnp.sqrt(jnp.sum(direction * direction) + 1e-06)
    both = [lax.all_gather(w[0], "ec", axis=0, tiled=False) for w in (gate_weight, up_weight, down_weight)]
    slices = [tuple(w[k] for w in both) for k in range(2)]

    forward_layout = dispatch_layout(forward_route[0, :, 0], expert_count, capacity)
    forward_send = jnp.dot(forward_layout, forward_in, preferred_element_type=jnp.float32).astype(
        jnp.bfloat16
    )

    backward_dy = backward_in.astype(jnp.float32)
    along_dir = jnp.sum(backward_dy * unit_dir[None, :], axis=1)
    sent_rows = (
        backward_weight[0][:, None] * (backward_dy - along_dir[:, None] * unit_dir[None, :])
    ).astype(jnp.bfloat16)
    backward_layout = dispatch_layout(backward_route[0, :, 0], expert_count, capacity)
    backward_send = jnp.dot(backward_layout, sent_rows, preferred_element_type=jnp.float32).astype(
        jnp.bfloat16
    )
    forward_rows, backward_rows = spread_to_holders(
        forward_send.reshape(expert_count, capacity, feature_count),
        backward_send.reshape(expert_count, capacity, feature_count),
    )

    flip = lax.axis_index("ep") == 1

    def reorder(saved):
        grouped = saved[0].reshape(group_count, 2, 2, capacity, local_hidden).transpose(2, 1, 0, 3, 4)
        mine = lax.all_to_all(grouped, "ec", split_axis=0, concat_axis=0, tiled=True)
        mine = jnp.where(flip, mine[:, ::-1], mine)
        return mine.reshape(2, device_count * capacity // 2, local_hidden)

    gate_rows = reorder(saved_gate)
    up_rows = reorder(saved_up)
    half_rows = (device_count * capacity // 2, feature_count)
    forward_rows = forward_rows.reshape(half_rows)
    backward_rows = backward_rows.reshape(half_rows)
    forward_pair = sum(
        expert_forward(forward_rows, slices[k]).astype(jnp.float32) for k in range(2)
    )
    backward_pair = sum(
        expert_backward(backward_rows, gate_rows[k], up_rows[k], slices[k]).astype(jnp.float32)
        for k in range(2)
    )
    pairs = jnp.stack([forward_pair, backward_pair]).reshape(
        2, 2, group_count, capacity, feature_count
    )
    forward_back, backward_back = collect_from_holders(pairs[:, 0], pairs[:, 1].astype(jnp.bfloat16))
    forward_back = forward_back.reshape(expert_count * capacity, feature_count)
    backward_back = backward_back.reshape(expert_count * capacity, feature_count)

    contract = (((0,), (0,)), ((), ()))
    picked = lax.dot_general(forward_layout, forward_back, contract, preferred_element_type=jnp.float32)
    mixed_rows = forward_weight[0][:, None] * picked
    coefficient = jnp.sum(mixed_rows * unit_dir[None, :], axis=1)
    forward_out = (
        forward_in.astype(jnp.float32) + mixed_rows - coefficient[:, None] * unit_dir[None, :]
    ).astype(jnp.bfloat16)
    returned = lax.dot_general(
        backward_layout, backward_back, contract, preferred_element_type=jnp.float32
    )
    backward_out = (backward_dy + returned).astype(jnp.bfloat16)
    return (forward_out[None], coefficient[None], backward_out[None])


def solution(mesh):
    sections = mesh.shape["section"]
    experts = mesh.shape["expert"]
    fine = Mesh(
        np.asarray(mesh.devices).reshape(sections, experts // 8, 2, 2, 2),
        ("section",) + EXPERT_AXES,
    )
    E = EXPERT_AXES
    in_specs = (
        P(E, None),
        P("section", E, None),
        P("section", E, None),
        P("section", E),
        P(E, None),
        P("section", E, None),
        P("section", E, None),
        P("section", E),
        P("section", None, E),
        P("section", None, E),
        P("section", None, E),
        P("section", None, E),
        P("section", E, None),
        P("section", None),
    )
    out_specs = (P("section", E, None), P("section", E), P("section", E, None))
    return jax.shard_map(body, mesh=fine, in_specs=in_specs, out_specs=out_specs, check_vma=False)
```

```python
import functools

import jax
import jax.numpy as jnp
import numpy as np
from jax import lax
from jax.experimental import pallas as pl
from jax.experimental.pallas import tpu as pltpu
from jax.sharding import Mesh
from jax.sharding import PartitionSpec as P

H = 1024
EXPERT_AXES = ("ex", "em", "ep", "ec")
GROUP = ("ex", "em")
HOLDERS = ("ep", "ec")
MESH_IDS = pl.DeviceIdType.MESH


def shifted(value, axis, by):
    devices = lax.axis_size(axis)
    pairs = [(i, i + by) for i in range(devices) if 0 <= i + by < devices]
    return lax.ppermute(value, axis, pairs)


def dispatch_layout(expert_ids, expert_count, capacity):
    onehot = (expert_ids[:, None] == jnp.arange(expert_count, dtype=jnp.int32)[None, :]).astype(
        jnp.int32
    )
    earlier = jnp.cumsum(onehot, axis=0) - onehot
    position = jnp.sum(earlier * onehot, axis=1)
    target = expert_ids * capacity + position
    return (
        jnp.arange(expert_count * capacity, dtype=jnp.int32)[:, None] == target[None, :]
    ).astype(jnp.bfloat16)


def expert_forward(slot_rows, weights):
    gate_cols, up_cols, down_rows = weights
    gate_pre = jnp.dot(slot_rows, gate_cols, preferred_element_type=jnp.float32)
    up_pre = jnp.dot(slot_rows, up_cols, preferred_element_type=jnp.float32)
    hidden = lax.optimization_barrier((jax.nn.silu(gate_pre) * up_pre).astype(jnp.bfloat16))
    return jnp.dot(hidden, down_rows, preferred_element_type=jnp.float32).astype(jnp.bfloat16)


def expert_backward(slot_rows, gate_saved, up_saved, weights):
    gate_cols, up_cols, down_rows = weights
    contract = (((1,), (1,)), ((), ()))
    grad_hidden = lax.dot_general(
        slot_rows, down_rows, contract, preferred_element_type=jnp.float32
    )
    gate_pre = gate_saved.astype(jnp.float32)
    up_pre = up_saved.astype(jnp.float32)
    sigmoid_gate = jax.nn.sigmoid(gate_pre)
    grad_gate = (
        grad_hidden * up_pre * sigmoid_gate * (1.0 + gate_pre * (1.0 - sigmoid_gate))
    ).astype(jnp.bfloat16)
    grad_up = (grad_hidden * gate_pre * sigmoid_gate).astype(jnp.bfloat16)
    grad_gate, grad_up = lax.optimization_barrier((grad_gate, grad_up))
    grad_part = lax.dot_general(grad_gate, gate_cols, contract, preferred_element_type=jnp.float32)
    grad_part = grad_part + lax.dot_general(
        grad_up, up_cols, contract, preferred_element_type=jnp.float32
    )
    return grad_part.astype(jnp.bfloat16)


def swap_pair(value):
    return lax.ppermute(value, "ep", [(0, 1), (1, 0)])


def spread_kernel(groups, *refs):
    streams = (len(refs) - 6) // 2
    sends = refs[:streams]
    rows = refs[streams : 2 * streams]
    first_recv, first_send, pair_recv, pair_send, near_recv, near_send = refs[2 * streams : 2 * streams + 6]
    section = lax.axis_index("section")
    ex = lax.axis_index("ex")
    em = lax.axis_index("em")
    ep = lax.axis_index("ep")
    ec = lax.axis_index("ec")
    me = ex * 2 + em
    partner = (section, ex, em, 1 - ep, ec)
    sibling = (section, ex, em, ep, 1 - ec)

    def peer(g):
        return (section, g // 2, g % 2, ep, ec)

    barrier = pltpu.get_barrier_semaphore()
    for d in range(1, groups):
        pl.semaphore_signal(barrier, inc=1, device_id=peer((me + d) % groups), device_id_type=MESH_IDS)
    pl.semaphore_signal(barrier, inc=1, device_id=partner, device_id_type=MESH_IDS)
    pl.semaphore_signal(barrier, inc=1, device_id=sibling, device_id_type=MESH_IDS)
    pl.semaphore_wait(barrier, groups + 1)

    def first_copy(s, g, target):
        return pltpu.make_async_remote_copy(
            src_ref=sends[s].at[g],
            dst_ref=rows[s].at[ec, 0, me],
            send_sem=first_send.at[s, g],
            recv_sem=first_recv.at[s, me],
            device_id=target,
            device_id_type=MESH_IDS,
        )

    def arrived(s, g):
        return pltpu.make_async_remote_copy(
            src_ref=sends[s].at[g],
            dst_ref=rows[s].at[ec, 0, g],
            send_sem=first_send.at[s, g],
            recv_sem=first_recv.at[s, g],
            device_id=peer(g),
            device_id_type=MESH_IDS,
        )

    def relay(s, q, g, target, recv, send, slot):
        return pltpu.make_async_remote_copy(
            src_ref=rows[s].at[ec, q, g],
            dst_ref=rows[s].at[ec, slot, g],
            send_sem=send.at[s, q, g],
            recv_sem=recv.at[s, q, g],
            device_id=target,
            device_id_type=MESH_IDS,
        )

    local = []
    for s in range(streams):
        copy = pltpu.make_async_copy(sends[s].at[me], rows[s].at[ec, 0, me], first_recv.at[s, me])
        copy.start()
        local.append(copy)
    for d in range(1, groups):
        for s in range(streams):
            g = (me + d) % groups
            first_copy(s, g, peer(g)).start()
    outgoing = []
    for d in range(groups):
        for s in range(streams):
            g = (me + groups - d) % groups
            if d > 0:
                arrived(s, g).wait_recv()
            else:
                local[s].wait()
            for target, recv, send, slot in (
                (partner, pair_recv, pair_send, 1),
                (sibling, near_recv, near_send, 0),
            ):
                copy = relay(s, 0, g, target, recv, send, slot)
                copy.start()
                outgoing.append(copy)
    for d in range(groups):
        for s in range(streams):
            g = (me + groups - d) % groups
            relay(s, 0, g, partner, pair_recv, pair_send, 1).wait_recv()
            copy = relay(s, 1, g, sibling, near_recv, near_send, 1)
            copy.start()
            outgoing.append(copy)
    for s in range(streams):
        for q in range(2):
            for g in range(groups):
                pltpu.make_async_remote_copy(
                    src_ref=rows[s].at[1 - ec, q, g],
                    dst_ref=rows[s].at[1 - ec, q, g],
                    send_sem=near_send.at[s, q, g],
                    recv_sem=near_recv.at[s, q, g],
                    device_id=sibling,
                    device_id_type=MESH_IDS,
                ).wait_recv()
    for s in range(streams):
        for d in range(1, groups):
            g = (me + d) % groups
            first_copy(s, g, peer(g)).wait_send()
    for copy in outgoing:
        copy.wait_send()


def spread_to_holders(*sends):
    groups, capacity, features = sends[0].shape
    streams = len(sends)
    rows = jax.ShapeDtypeStruct((2, 2, groups, capacity, features), sends[0].dtype)
    any_spec = pl.BlockSpec(memory_space=pl.ANY)
    return pl.pallas_call(
        functools.partial(spread_kernel, groups),
        out_shape=[rows] * streams,
        in_specs=[any_spec] * streams,
        out_specs=[any_spec] * streams,
        scratch_shapes=[
            pltpu.SemaphoreType.DMA((streams, groups)),
            pltpu.SemaphoreType.DMA((streams, groups)),
            pltpu.SemaphoreType.DMA((streams, 2, groups)),
            pltpu.SemaphoreType.DMA((streams, 2, groups)),
            pltpu.SemaphoreType.DMA((streams, 2, groups)),
            pltpu.SemaphoreType.DMA((streams, 2, groups)),
        ],
        compiler_params=pltpu.CompilerParams(collective_id=0, has_side_effects=True),
    )(*sends)


def collect_kernel(groups, *refs):
    streams = len(refs) - 11
    parts = refs[:streams]
    back, near_land, other_buf, pair_land, summed = refs[streams : streams + 5]
    near_recv, near_send, swap_recv, swap_send, back_recv, back_send = refs[streams + 5 :]
    section = lax.axis_index("section")
    ex = lax.axis_index("ex")
    em = lax.axis_index("em")
    ep = lax.axis_index("ep")
    ec = lax.axis_index("ec")
    me = ex * 2 + em
    partner = (section, ex, em, 1 - ep, ec)
    sibling = (section, ex, em, ep, 1 - ec)

    def peer(g):
        return (section, g // 2, g % 2, ep, ec)

    barrier = pltpu.get_barrier_semaphore()
    for d in range(1, groups):
        pl.semaphore_signal(barrier, inc=1, device_id=peer((me + d) % groups), device_id_type=MESH_IDS)
    pl.semaphore_signal(barrier, inc=1, device_id=partner, device_id_type=MESH_IDS)
    pl.semaphore_signal(barrier, inc=1, device_id=sibling, device_id_type=MESH_IDS)
    pl.semaphore_wait(barrier, groups + 1)

    def near(s, q, g):
        return pltpu.make_async_remote_copy(
            src_ref=parts[s].at[1 - ec, q, g],
            dst_ref=near_land.at[s, q, g],
            send_sem=near_send.at[s, q, g],
            recv_sem=near_recv.at[s, q, g],
            device_id=sibling,
            device_id_type=MESH_IDS,
        )

    def swap(s, g):
        return pltpu.make_async_remote_copy(
            src_ref=other_buf.at[s, g],
            dst_ref=pair_land.at[s, g],
            send_sem=swap_send.at[s, g],
            recv_sem=swap_recv.at[s, g],
            device_id=partner,
            device_id_type=MESH_IDS,
        )

    def reply(s, g):
        return pltpu.make_async_remote_copy(
            src_ref=summed.at[s, g],
            dst_ref=back.at[s, me],
            send_sem=back_send.at[s, g],
            recv_sem=back_recv.at[s, me],
            device_id=peer(g),
            device_id_type=MESH_IDS,
        )

    def incoming(s, g):
        return pltpu.make_async_remote_copy(
            src_ref=summed.at[s, g],
            dst_ref=back.at[s, g],
            send_sem=back_send.at[s, g],
            recv_sem=back_recv.at[s, g],
            device_id=peer(g),
            device_id_type=MESH_IDS,
        )

    for q in (1, 0):
        for d in range(1, groups + 1):
            for s in range(streams):
                near(s, q, (me + d) % groups).start()
    for d in range(1, groups + 1):
        for s in range(streams):
            g = (me + d) % groups
            near(s, 1, g).wait_recv()
            other_buf[s, g] = (
                parts[s][ec, 1, g].astype(jnp.float32) + near_land[s, 1, g].astype(jnp.float32)
            ).astype(other_buf.dtype)
            swap(s, g).start()
    local = []
    for d in range(1, groups + 1):
        for s in range(streams):
            g = (me + d) % groups
            near(s, 0, g).wait_recv()
            swap(s, g).wait_recv()
            pair = parts[s][ec, 0, g].astype(jnp.float32) + near_land[s, 0, g].astype(jnp.float32)
            summed[s, g] = (pair + pair_land[s, g].astype(jnp.float32)).astype(summed.dtype)
            if d < groups:
                reply(s, g).start()
            else:
                copy = pltpu.make_async_copy(summed.at[s, g], back.at[s, me], back_recv.at[s, me])
                copy.start()
                local.append(copy)
    for s in range(streams):
        local[s].wait()
        for d in range(1, groups):
            incoming(s, (me + d) % groups).wait_recv()
    for s in range(streams):
        for d in range(1, groups + 1):
            g = (me + d) % groups
            swap(s, g).wait_send()
            near(s, 0, g).wait_send()
            near(s, 1, g).wait_send()
        for d in range(1, groups):
            reply(s, (me + d) % groups).wait_send()


def collect_from_holders(*parts):
    streams = len(parts)
    _, _, groups, capacity, features = parts[0].shape
    block = (streams, groups, capacity, features)
    any_spec = pl.BlockSpec(memory_space=pl.ANY)
    back = pl.pallas_call(
        functools.partial(collect_kernel, groups),
        out_shape=jax.ShapeDtypeStruct(block, jnp.bfloat16),
        in_specs=[pl.BlockSpec(memory_space=pltpu.VMEM)] * streams,
        out_specs=any_spec,
        scratch_shapes=[
            pltpu.VMEM((streams, 2, groups, capacity, features), jnp.bfloat16),
            pltpu.VMEM(block, jnp.bfloat16),
            pltpu.VMEM(block, jnp.bfloat16),
            pltpu.VMEM(block, jnp.bfloat16),
            pltpu.SemaphoreType.DMA((streams, 2, groups)),
            pltpu.SemaphoreType.DMA((streams, 2, groups)),
            pltpu.SemaphoreType.DMA((streams, groups)),
            pltpu.SemaphoreType.DMA((streams, groups)),
            pltpu.SemaphoreType.DMA((streams, groups)),
            pltpu.SemaphoreType.DMA((streams, groups)),
        ],
        compiler_params=pltpu.CompilerParams(
            collective_id=1, has_side_effects=True, vmem_limit_bytes=60 * 1024 * 1024
        ),
    )(*parts)
    return [back[s] for s in range(streams)]


def body(
    embedded,
    forward_held,
    forward_route,
    forward_weight,
    loss_cotangent,
    backward_held,
    backward_route,
    backward_weight,
    saved_gate,
    saved_up,
    gate_weight,
    up_weight,
    down_weight,
    steering,
):
    section_count = lax.axis_size("section")
    section_index = lax.axis_index("section")
    group_count = lax.axis_size(GROUP)
    holder_count = lax.axis_size(HOLDERS)
    local_hidden = gate_weight.shape[2]
    expert_count = group_count
    device_count = group_count * holder_count
    capacity = saved_gate.shape[1] // device_count
    feature_count = embedded.shape[1]
    rows_shape = (device_count * capacity, feature_count)
    arriving = shifted(forward_held, "section", 1)[0]
    forward_in = jnp.where(section_index == 0, embedded, arriving)
    returning = shifted(backward_held, "section", -1)[0]
    backward_in = jnp.where(section_index == section_count - 1, loss_cotangent, returning)
    direction = steering[0]
    unit_dir = direction / jnp.sqrt(jnp.sum(direction * direction) + 1e-06)
    weights = (gate_weight[0], up_weight[0], down_weight[0])

    forward_layout = dispatch_layout(forward_route[0, :, 0], expert_count, capacity)
    forward_send = jnp.dot(forward_layout, forward_in, preferred_element_type=jnp.float32).astype(
        jnp.bfloat16
    )

    backward_dy = backward_in.astype(jnp.float32)
    along_dir = jnp.sum(backward_dy * unit_dir[None, :], axis=1)
    sent_rows = (
        backward_weight[0][:, None] * (backward_dy - along_dir[:, None] * unit_dir[None, :])
    ).astype(jnp.bfloat16)
    backward_layout = dispatch_layout(backward_route[0, :, 0], expert_count, capacity)
    backward_send = jnp.dot(backward_layout, sent_rows, preferred_element_type=jnp.float32).astype(
        jnp.bfloat16
    )
    forward_rows, backward_rows = spread_to_holders(
        forward_send.reshape(expert_count, capacity, feature_count),
        backward_send.reshape(expert_count, capacity, feature_count),
    )

    flip = lax.axis_index("ep") == 1

    def reorder(saved):
        grouped = saved[0].reshape(group_count, 2, 2, capacity, local_hidden).transpose(2, 1, 0, 3, 4)
        grouped = jnp.where(flip, grouped[:, ::-1], grouped)
        return grouped.reshape(device_count * capacity, local_hidden)

    forward_part = expert_forward(forward_rows.reshape(rows_shape), weights)
    backward_part = expert_backward(
        backward_rows.reshape(rows_shape), reorder(saved_gate), reorder(saved_up), weights
    )
    forward_back, backward_back = collect_from_holders(
        forward_part.reshape(2, 2, group_count, capacity, feature_count),
        backward_part.reshape(2, 2, group_count, capacity, feature_count),
    )
    forward_back = forward_back.reshape(expert_count * capacity, feature_count)
    backward_back = backward_back.reshape(expert_count * capacity, feature_count)

    contract = (((0,), (0,)), ((), ()))
    picked = lax.dot_general(forward_layout, forward_back, contract, preferred_element_type=jnp.float32)
    mixed_rows = forward_weight[0][:, None] * picked
    coefficient = jnp.sum(mixed_rows * unit_dir[None, :], axis=1)
    forward_out = (
        forward_in.astype(jnp.float32) + mixed_rows - coefficient[:, None] * unit_dir[None, :]
    ).astype(jnp.bfloat16)
    returned = lax.dot_general(
        backward_layout, backward_back, contract, preferred_element_type=jnp.float32
    )
    backward_out = (backward_dy + returned).astype(jnp.bfloat16)
    return (forward_out[None], coefficient[None], backward_out[None])


def solution(mesh):
    sections = mesh.shape["section"]
    experts = mesh.shape["expert"]
    fine = Mesh(
        np.asarray(mesh.devices).reshape(sections, experts // 8, 2, 2, 2),
        ("section",) + EXPERT_AXES,
    )
    E = EXPERT_AXES
    in_specs = (
        P(E, None),
        P("section", E, None),
        P("section", E, None),
        P("section", E),
        P(E, None),
        P("section", E, None),
        P("section", E, None),
        P("section", E),
        P("section", None, E),
        P("section", None, E),
        P("section", None, E),
        P("section", None, E),
        P("section", E, None),
        P("section", None),
    )
    out_specs = (P("section", E, None), P("section", E), P("section", E, None))
    return jax.shard_map(body, mesh=fine, in_specs=in_specs, out_specs=out_specs, check_vma=False)
```

```python
import functools

import jax
import jax.numpy as jnp
import numpy as np
from jax import lax
from jax.experimental import pallas as pl
from jax.experimental.pallas import tpu as pltpu
from jax.sharding import Mesh
from jax.sharding import PartitionSpec as P

H = 1024
EXPERT_AXES = ("ex", "em", "ep", "ec")
GROUP = ("ex", "em")
HOLDERS = ("ep", "ec")
MESH_IDS = pl.DeviceIdType.MESH


def shifted(value, axis, by):
    devices = lax.axis_size(axis)
    pairs = [(i, i + by) for i in range(devices) if 0 <= i + by < devices]
    return lax.ppermute(value, axis, pairs)


def section_shift(value, by):
    axes = ("section",) + EXPERT_AXES
    sections = lax.axis_size("section")
    experts = lax.axis_size(EXPERT_AXES)
    ring = 8
    first = {2: [], -2: []}
    second = {2: [], -2: []}
    for s in range(sections):
        t = s + by
        if not 0 <= t < sections:
            continue
        y, high = divmod(s, 2)
        for e in range(experts):
            x, rest = divmod(e, 8)
            low, core = divmod(rest, 2)
            z = high * 4 + low
            for dz in (2, -2):
                hop = (z + dz) % ring
                middle = (y * 2 + hop // 4) * experts + (x * 4 + hop % 4) * 2 + core
                first[dz].append((s * experts + e, middle))
                second[dz].append((middle, t * experts + e))
    half = value.shape[1] // 2
    up = lax.ppermute(value[:, :half], axes, first[2])
    down = lax.ppermute(value[:, half:], axes, first[-2])
    up = lax.ppermute(up, axes, second[2])
    down = lax.ppermute(down, axes, second[-2])
    return jnp.concatenate([up, down], axis=1)


def dispatch_layout(expert_ids, expert_count, capacity):
    onehot = (expert_ids[:, None] == jnp.arange(expert_count, dtype=jnp.int32)[None, :]).astype(
        jnp.int32
    )
    earlier = jnp.cumsum(onehot, axis=0) - onehot
    position = jnp.sum(earlier * onehot, axis=1)
    target = expert_ids * capacity + position
    return (
        jnp.arange(expert_count * capacity, dtype=jnp.int32)[:, None] == target[None, :]
    ).astype(jnp.bfloat16)


def expert_forward(slot_rows, weights):
    gate_cols, up_cols, down_rows = weights
    gate_pre = jnp.dot(slot_rows, gate_cols, preferred_element_type=jnp.float32)
    up_pre = jnp.dot(slot_rows, up_cols, preferred_element_type=jnp.float32)
    hidden = lax.optimization_barrier((jax.nn.silu(gate_pre) * up_pre).astype(jnp.bfloat16))
    return jnp.dot(hidden, down_rows, preferred_element_type=jnp.float32).astype(jnp.bfloat16)


def expert_backward(slot_rows, gate_saved, up_saved, weights):
    gate_cols, up_cols, down_rows = weights
    contract = (((1,), (1,)), ((), ()))
    grad_hidden = lax.dot_general(
        slot_rows, down_rows, contract, preferred_element_type=jnp.float32
    )
    gate_pre = gate_saved.astype(jnp.float32)
    up_pre = up_saved.astype(jnp.float32)
    sigmoid_gate = jax.nn.sigmoid(gate_pre)
    grad_gate = (
        grad_hidden * up_pre * sigmoid_gate * (1.0 + gate_pre * (1.0 - sigmoid_gate))
    ).astype(jnp.bfloat16)
    grad_up = (grad_hidden * gate_pre * sigmoid_gate).astype(jnp.bfloat16)
    grad_gate, grad_up = lax.optimization_barrier((grad_gate, grad_up))
    grad_part = lax.dot_general(grad_gate, gate_cols, contract, preferred_element_type=jnp.float32)
    grad_part = grad_part + lax.dot_general(
        grad_up, up_cols, contract, preferred_element_type=jnp.float32
    )
    return grad_part.astype(jnp.bfloat16)


def swap_pair(value):
    return lax.ppermute(value, "ep", [(0, 1), (1, 0)])


def spread_kernel(groups, *refs):
    streams = (len(refs) - 6) // 2
    sends = refs[:streams]
    rows = refs[streams : 2 * streams]
    first_recv, first_send, pair_recv, pair_send, near_recv, near_send = refs[2 * streams : 2 * streams + 6]
    section = lax.axis_index("section")
    ex = lax.axis_index("ex")
    em = lax.axis_index("em")
    ep = lax.axis_index("ep")
    ec = lax.axis_index("ec")
    me = ex * 2 + em
    partner = (section, ex, em, 1 - ep, ec)
    sibling = (section, ex, em, ep, 1 - ec)

    def peer(g):
        return (section, g // 2, g % 2, ep, ec)

    barrier = pltpu.get_barrier_semaphore()
    for d in range(1, groups):
        pl.semaphore_signal(barrier, inc=1, device_id=peer((me + d) % groups), device_id_type=MESH_IDS)
    pl.semaphore_signal(barrier, inc=1, device_id=partner, device_id_type=MESH_IDS)
    pl.semaphore_signal(barrier, inc=1, device_id=sibling, device_id_type=MESH_IDS)
    pl.semaphore_wait(barrier, groups + 1)

    def first_copy(s, g, target):
        return pltpu.make_async_remote_copy(
            src_ref=sends[s].at[g],
            dst_ref=rows[s].at[ec, 0, me],
            send_sem=first_send.at[s, g],
            recv_sem=first_recv.at[s, me],
            device_id=target,
            device_id_type=MESH_IDS,
        )

    def arrived(s, g):
        return pltpu.make_async_remote_copy(
            src_ref=sends[s].at[g],
            dst_ref=rows[s].at[ec, 0, g],
            send_sem=first_send.at[s, g],
            recv_sem=first_recv.at[s, g],
            device_id=peer(g),
            device_id_type=MESH_IDS,
        )

    def relay(s, q, g, target, recv, send, slot):
        return pltpu.make_async_remote_copy(
            src_ref=rows[s].at[ec, q, g],
            dst_ref=rows[s].at[ec, slot, g],
            send_sem=send.at[s, q, g],
            recv_sem=recv.at[s, q, g],
            device_id=target,
            device_id_type=MESH_IDS,
        )

    local = []
    for s in range(streams):
        copy = pltpu.make_async_copy(sends[s].at[me], rows[s].at[ec, 0, me], first_recv.at[s, me])
        copy.start()
        local.append(copy)
    for d in range(1, groups):
        for s in range(streams):
            g = (me + d) % groups
            first_copy(s, g, peer(g)).start()
    outgoing = []
    for d in range(groups):
        for s in range(streams):
            g = (me + groups - d) % groups
            if d > 0:
                arrived(s, g).wait_recv()
            else:
                local[s].wait()
            for target, recv, send, slot in (
                (partner, pair_recv, pair_send, 1),
                (sibling, near_recv, near_send, 0),
            ):
                copy = relay(s, 0, g, target, recv, send, slot)
                copy.start()
                outgoing.append(copy)
    for d in range(groups):
        for s in range(streams):
            g = (me + groups - d) % groups
            relay(s, 0, g, partner, pair_recv, pair_send, 1).wait_recv()
            copy = relay(s, 1, g, sibling, near_recv, near_send, 1)
            copy.start()
            outgoing.append(copy)
    for s in range(streams):
        for q in range(2):
            for g in range(groups):
                pltpu.make_async_remote_copy(
                    src_ref=rows[s].at[1 - ec, q, g],
                    dst_ref=rows[s].at[1 - ec, q, g],
                    send_sem=near_send.at[s, q, g],
                    recv_sem=near_recv.at[s, q, g],
                    device_id=sibling,
                    device_id_type=MESH_IDS,
                ).wait_recv()
    for s in range(streams):
        for d in range(1, groups):
            g = (me + d) % groups
            first_copy(s, g, peer(g)).wait_send()
    for copy in outgoing:
        copy.wait_send()


def spread_to_holders(*sends):
    groups, capacity, features = sends[0].shape
    streams = len(sends)
    rows = jax.ShapeDtypeStruct((2, 2, groups, capacity, features), sends[0].dtype)
    any_spec = pl.BlockSpec(memory_space=pl.ANY)
    return pl.pallas_call(
        functools.partial(spread_kernel, groups),
        out_shape=[rows] * streams,
        in_specs=[any_spec] * streams,
        out_specs=[any_spec] * streams,
        scratch_shapes=[
            pltpu.SemaphoreType.DMA((streams, groups)),
            pltpu.SemaphoreType.DMA((streams, groups)),
            pltpu.SemaphoreType.DMA((streams, 2, groups)),
            pltpu.SemaphoreType.DMA((streams, 2, groups)),
            pltpu.SemaphoreType.DMA((streams, 2, groups)),
            pltpu.SemaphoreType.DMA((streams, 2, groups)),
        ],
        compiler_params=pltpu.CompilerParams(collective_id=0, has_side_effects=True),
    )(*sends)


def collect_kernel(groups, *refs):
    streams = len(refs) - 11
    parts = refs[:streams]
    back, near_land, other_buf, pair_land, summed = refs[streams : streams + 5]
    near_recv, near_send, swap_recv, swap_send, back_recv, back_send = refs[streams + 5 :]
    section = lax.axis_index("section")
    ex = lax.axis_index("ex")
    em = lax.axis_index("em")
    ep = lax.axis_index("ep")
    ec = lax.axis_index("ec")
    me = ex * 2 + em
    partner = (section, ex, em, 1 - ep, ec)
    sibling = (section, ex, em, ep, 1 - ec)

    def peer(g):
        return (section, g // 2, g % 2, ep, ec)

    barrier = pltpu.get_barrier_semaphore()
    for d in range(1, groups):
        pl.semaphore_signal(barrier, inc=1, device_id=peer((me + d) % groups), device_id_type=MESH_IDS)
    pl.semaphore_signal(barrier, inc=1, device_id=partner, device_id_type=MESH_IDS)
    pl.semaphore_signal(barrier, inc=1, device_id=sibling, device_id_type=MESH_IDS)
    pl.semaphore_wait(barrier, groups + 1)

    def near(s, q, g):
        return pltpu.make_async_remote_copy(
            src_ref=parts[s].at[1 - ec, q, g],
            dst_ref=near_land.at[s, q, g],
            send_sem=near_send.at[s, q, g],
            recv_sem=near_recv.at[s, q, g],
            device_id=sibling,
            device_id_type=MESH_IDS,
        )

    def swap(s, g):
        return pltpu.make_async_remote_copy(
            src_ref=other_buf.at[s, g],
            dst_ref=pair_land.at[s, g],
            send_sem=swap_send.at[s, g],
            recv_sem=swap_recv.at[s, g],
            device_id=partner,
            device_id_type=MESH_IDS,
        )

    def reply(s, g):
        return pltpu.make_async_remote_copy(
            src_ref=summed.at[s, g],
            dst_ref=back.at[s, me],
            send_sem=back_send.at[s, g],
            recv_sem=back_recv.at[s, me],
            device_id=peer(g),
            device_id_type=MESH_IDS,
        )

    def incoming(s, g):
        return pltpu.make_async_remote_copy(
            src_ref=summed.at[s, g],
            dst_ref=back.at[s, g],
            send_sem=back_send.at[s, g],
            recv_sem=back_recv.at[s, g],
            device_id=peer(g),
            device_id_type=MESH_IDS,
        )

    for q in (1, 0):
        for d in range(1, groups + 1):
            for s in range(streams):
                near(s, q, (me + d) % groups).start()
    for d in range(1, groups + 1):
        for s in range(streams):
            g = (me + d) % groups
            near(s, 1, g).wait_recv()
            other_buf[s, g] = (
                parts[s][ec, 1, g].astype(jnp.float32) + near_land[s, 1, g].astype(jnp.float32)
            ).astype(other_buf.dtype)
            swap(s, g).start()
    local = []
    for d in range(1, groups + 1):
        for s in range(streams):
            g = (me + d) % groups
            near(s, 0, g).wait_recv()
            swap(s, g).wait_recv()
            pair = parts[s][ec, 0, g].astype(jnp.float32) + near_land[s, 0, g].astype(jnp.float32)
            summed[s, g] = (pair + pair_land[s, g].astype(jnp.float32)).astype(summed.dtype)
            if d < groups:
                reply(s, g).start()
            else:
                copy = pltpu.make_async_copy(summed.at[s, g], back.at[s, me], back_recv.at[s, me])
                copy.start()
                local.append(copy)
    for s in range(streams):
        local[s].wait()
        for d in range(1, groups):
            incoming(s, (me + d) % groups).wait_recv()
    for s in range(streams):
        for d in range(1, groups + 1):
            g = (me + d) % groups
            swap(s, g).wait_send()
            near(s, 0, g).wait_send()
            near(s, 1, g).wait_send()
        for d in range(1, groups):
            reply(s, (me + d) % groups).wait_send()


def collect_from_holders(*parts):
    streams = len(parts)
    _, _, groups, capacity, features = parts[0].shape
    block = (streams, groups, capacity, features)
    any_spec = pl.BlockSpec(memory_space=pl.ANY)
    back = pl.pallas_call(
        functools.partial(collect_kernel, groups),
        out_shape=jax.ShapeDtypeStruct(block, jnp.bfloat16),
        in_specs=[pl.BlockSpec(memory_space=pltpu.VMEM)] * streams,
        out_specs=any_spec,
        scratch_shapes=[
            pltpu.VMEM((streams, 2, groups, capacity, features), jnp.bfloat16),
            pltpu.VMEM(block, jnp.bfloat16),
            pltpu.VMEM(block, jnp.bfloat16),
            pltpu.VMEM(block, jnp.bfloat16),
            pltpu.SemaphoreType.DMA((streams, 2, groups)),
            pltpu.SemaphoreType.DMA((streams, 2, groups)),
            pltpu.SemaphoreType.DMA((streams, groups)),
            pltpu.SemaphoreType.DMA((streams, groups)),
            pltpu.SemaphoreType.DMA((streams, groups)),
            pltpu.SemaphoreType.DMA((streams, groups)),
        ],
        compiler_params=pltpu.CompilerParams(
            collective_id=1, has_side_effects=True, vmem_limit_bytes=60 * 1024 * 1024
        ),
    )(*parts)
    return [back[s] for s in range(streams)]


def body(
    embedded,
    forward_held,
    forward_route,
    forward_weight,
    loss_cotangent,
    backward_held,
    backward_route,
    backward_weight,
    saved_gate,
    saved_up,
    gate_weight,
    up_weight,
    down_weight,
    steering,
):
    section_count = lax.axis_size("section")
    section_index = lax.axis_index("section")
    group_count = lax.axis_size(GROUP)
    holder_count = lax.axis_size(HOLDERS)
    local_hidden = gate_weight.shape[2]
    expert_count = group_count
    device_count = group_count * holder_count
    capacity = saved_gate.shape[1] // device_count
    feature_count = embedded.shape[1]
    rows_shape = (device_count * capacity, feature_count)
    arriving = section_shift(forward_held, 1)[0]
    forward_in = jnp.where(section_index == 0, embedded, arriving)
    returning = section_shift(backward_held, -1)[0]
    backward_in = jnp.where(section_index == section_count - 1, loss_cotangent, returning)
    direction = steering[0]
    unit_dir = direction / jnp.sqrt(jnp.sum(direction * direction) + 1e-06)
    weights = (gate_weight[0], up_weight[0], down_weight[0])

    forward_layout = dispatch_layout(forward_route[0, :, 0], expert_count, capacity)
    forward_send = jnp.dot(forward_layout, forward_in, preferred_element_type=jnp.float32).astype(
        jnp.bfloat16
    )

    backward_dy = backward_in.astype(jnp.float32)
    along_dir = jnp.sum(backward_dy * unit_dir[None, :], axis=1)
    sent_rows = (
        backward_weight[0][:, None] * (backward_dy - along_dir[:, None] * unit_dir[None, :])
    ).astype(jnp.bfloat16)
    backward_layout = dispatch_layout(backward_route[0, :, 0], expert_count, capacity)
    backward_send = jnp.dot(backward_layout, sent_rows, preferred_element_type=jnp.float32).astype(
        jnp.bfloat16
    )
    forward_rows, backward_rows = spread_to_holders(
        forward_send.reshape(expert_count, capacity, feature_count),
        backward_send.reshape(expert_count, capacity, feature_count),
    )

    flip = lax.axis_index("ep") == 1

    def reorder(saved):
        grouped = saved[0].reshape(group_count, 2, 2, capacity, local_hidden).transpose(2, 1, 0, 3, 4)
        grouped = jnp.where(flip, grouped[:, ::-1], grouped)
        return grouped.reshape(device_count * capacity, local_hidden)

    forward_part = expert_forward(forward_rows.reshape(rows_shape), weights)
    backward_part = expert_backward(
        backward_rows.reshape(rows_shape), reorder(saved_gate), reorder(saved_up), weights
    )
    forward_back, backward_back = collect_from_holders(
        forward_part.reshape(2, 2, group_count, capacity, feature_count),
        backward_part.reshape(2, 2, group_count, capacity, feature_count),
    )
    forward_back = forward_back.reshape(expert_count * capacity, feature_count)
    backward_back = backward_back.reshape(expert_count * capacity, feature_count)

    contract = (((0,), (0,)), ((), ()))
    picked = lax.dot_general(forward_layout, forward_back, contract, preferred_element_type=jnp.float32)
    mixed_rows = forward_weight[0][:, None] * picked
    coefficient = jnp.sum(mixed_rows * unit_dir[None, :], axis=1)
    forward_out = (
        forward_in.astype(jnp.float32) + mixed_rows - coefficient[:, None] * unit_dir[None, :]
    ).astype(jnp.bfloat16)
    returned = lax.dot_general(
        backward_layout, backward_back, contract, preferred_element_type=jnp.float32
    )
    backward_out = (backward_dy + returned).astype(jnp.bfloat16)
    return (forward_out[None], coefficient[None], backward_out[None])


def solution(mesh):
    sections = mesh.shape["section"]
    experts = mesh.shape["expert"]
    fine = Mesh(
        np.asarray(mesh.devices).reshape(sections, experts // 8, 2, 2, 2),
        ("section",) + EXPERT_AXES,
    )
    E = EXPERT_AXES
    in_specs = (
        P(E, None),
        P("section", E, None),
        P("section", E, None),
        P("section", E),
        P(E, None),
        P("section", E, None),
        P("section", E, None),
        P("section", E),
        P("section", None, E),
        P("section", None, E),
        P("section", None, E),
        P("section", None, E),
        P("section", E, None),
        P("section", None),
    )
    out_specs = (P("section", E, None), P("section", E), P("section", E, None))
    return jax.shard_map(body, mesh=fine, in_specs=in_specs, out_specs=out_specs, check_vma=False)
```

```python
import functools

import jax
import jax.numpy as jnp
import numpy as np
from jax import lax
from jax.experimental import pallas as pl
from jax.experimental.pallas import tpu as pltpu
from jax.sharding import Mesh
from jax.sharding import PartitionSpec as P

H = 1024
EXPERT_AXES = ("ex", "em", "ep", "ec")
GROUP = ("ex", "em")
HOLDERS = ("ep", "ec")
MESH_IDS = pl.DeviceIdType.MESH


def shifted(value, axis, by):
    devices = lax.axis_size(axis)
    pairs = [(i, i + by) for i in range(devices) if 0 <= i + by < devices]
    return lax.ppermute(value, axis, pairs)


def dispatch_layout(expert_ids, expert_count, capacity):
    onehot = (expert_ids[:, None] == jnp.arange(expert_count, dtype=jnp.int32)[None, :]).astype(
        jnp.int32
    )
    earlier = jnp.cumsum(onehot, axis=0) - onehot
    position = jnp.sum(earlier * onehot, axis=1)
    target = expert_ids * capacity + position
    return (
        jnp.arange(expert_count * capacity, dtype=jnp.int32)[:, None] == target[None, :]
    ).astype(jnp.bfloat16)


def expert_forward(slot_rows, weights):
    gate_cols, up_cols, down_rows = weights
    gate_pre = jnp.dot(slot_rows, gate_cols, preferred_element_type=jnp.float32)
    up_pre = jnp.dot(slot_rows, up_cols, preferred_element_type=jnp.float32)
    hidden = lax.optimization_barrier((jax.nn.silu(gate_pre) * up_pre).astype(jnp.bfloat16))
    return jnp.dot(hidden, down_rows, preferred_element_type=jnp.float32).astype(jnp.bfloat16)


def expert_backward(slot_rows, gate_saved, up_saved, weights):
    gate_cols, up_cols, down_rows = weights
    contract = (((1,), (1,)), ((), ()))
    grad_hidden = lax.dot_general(
        slot_rows, down_rows, contract, preferred_element_type=jnp.float32
    )
    gate_pre = gate_saved.astype(jnp.float32)
    up_pre = up_saved.astype(jnp.float32)
    sigmoid_gate = jax.nn.sigmoid(gate_pre)
    grad_gate = (
        grad_hidden * up_pre * sigmoid_gate * (1.0 + gate_pre * (1.0 - sigmoid_gate))
    ).astype(jnp.bfloat16)
    grad_up = (grad_hidden * gate_pre * sigmoid_gate).astype(jnp.bfloat16)
    grad_gate, grad_up = lax.optimization_barrier((grad_gate, grad_up))
    grad_part = lax.dot_general(grad_gate, gate_cols, contract, preferred_element_type=jnp.float32)
    grad_part = grad_part + lax.dot_general(
        grad_up, up_cols, contract, preferred_element_type=jnp.float32
    )
    return grad_part.astype(jnp.bfloat16)


def swap_pair(value):
    return lax.ppermute(value, "ep", [(0, 1), (1, 0)])


def spread_kernel(groups, *refs):
    streams = (len(refs) - 6) // 2
    sends = refs[:streams]
    rows = refs[streams : 2 * streams]
    first_recv, first_send, pair_recv, pair_send, near_recv, near_send = refs[2 * streams : 2 * streams + 6]
    section = lax.axis_index("section")
    ex = lax.axis_index("ex")
    em = lax.axis_index("em")
    ep = lax.axis_index("ep")
    ec = lax.axis_index("ec")
    me = ex * 2 + em
    partner = (section, ex, em, 1 - ep, ec)
    sibling = (section, ex, em, ep, 1 - ec)

    def peer(g):
        return (section, g // 2, g % 2, ep, ec)

    barrier = pltpu.get_barrier_semaphore()
    for d in range(1, groups):
        pl.semaphore_signal(barrier, inc=1, device_id=peer((me + d) % groups), device_id_type=MESH_IDS)
    pl.semaphore_signal(barrier, inc=1, device_id=partner, device_id_type=MESH_IDS)
    pl.semaphore_signal(barrier, inc=1, device_id=sibling, device_id_type=MESH_IDS)
    pl.semaphore_wait(barrier, groups + 1)

    def first_copy(s, g, target):
        return pltpu.make_async_remote_copy(
            src_ref=sends[s].at[g],
            dst_ref=rows[s].at[ec, 0, me],
            send_sem=first_send.at[s, g],
            recv_sem=first_recv.at[s, me],
            device_id=target,
            device_id_type=MESH_IDS,
        )

    def arrived(s, g):
        return pltpu.make_async_remote_copy(
            src_ref=sends[s].at[g],
            dst_ref=rows[s].at[ec, 0, g],
            send_sem=first_send.at[s, g],
            recv_sem=first_recv.at[s, g],
            device_id=peer(g),
            device_id_type=MESH_IDS,
        )

    def relay(s, q, g, target, recv, send, slot):
        return pltpu.make_async_remote_copy(
            src_ref=rows[s].at[ec, q, g],
            dst_ref=rows[s].at[ec, slot, g],
            send_sem=send.at[s, q, g],
            recv_sem=recv.at[s, q, g],
            device_id=target,
            device_id_type=MESH_IDS,
        )

    local = []
    for s in range(streams):
        copy = pltpu.make_async_copy(sends[s].at[me], rows[s].at[ec, 0, me], first_recv.at[s, me])
        copy.start()
        local.append(copy)
    for d in range(1, groups):
        for s in range(streams):
            g = (me + d) % groups
            first_copy(s, g, peer(g)).start()
    outgoing = []
    for d in range(groups):
        for s in range(streams):
            g = (me + groups - d) % groups
            if d > 0:
                arrived(s, g).wait_recv()
            else:
                local[s].wait()
            for target, recv, send, slot in (
                (partner, pair_recv, pair_send, 1),
                (sibling, near_recv, near_send, 0),
            ):
                copy = relay(s, 0, g, target, recv, send, slot)
                copy.start()
                outgoing.append(copy)
    for d in range(groups):
        for s in range(streams):
            g = (me + groups - d) % groups
            relay(s, 0, g, partner, pair_recv, pair_send, 1).wait_recv()
            copy = relay(s, 1, g, sibling, near_recv, near_send, 1)
            copy.start()
            outgoing.append(copy)
    for s in range(streams):
        for q in range(2):
            for g in range(groups):
                pltpu.make_async_remote_copy(
                    src_ref=rows[s].at[1 - ec, q, g],
                    dst_ref=rows[s].at[1 - ec, q, g],
                    send_sem=near_send.at[s, q, g],
                    recv_sem=near_recv.at[s, q, g],
                    device_id=sibling,
                    device_id_type=MESH_IDS,
                ).wait_recv()
    for s in range(streams):
        for d in range(1, groups):
            g = (me + d) % groups
            first_copy(s, g, peer(g)).wait_send()
    for copy in outgoing:
        copy.wait_send()


def spread_to_holders(*sends, collective_id=0):
    groups, capacity, features = sends[0].shape
    streams = len(sends)
    rows = jax.ShapeDtypeStruct((2, 2, groups, capacity, features), sends[0].dtype)
    any_spec = pl.BlockSpec(memory_space=pl.ANY)
    return pl.pallas_call(
        functools.partial(spread_kernel, groups),
        out_shape=[rows] * streams,
        in_specs=[any_spec] * streams,
        out_specs=[any_spec] * streams,
        scratch_shapes=[
            pltpu.SemaphoreType.DMA((streams, groups)),
            pltpu.SemaphoreType.DMA((streams, groups)),
            pltpu.SemaphoreType.DMA((streams, 2, groups)),
            pltpu.SemaphoreType.DMA((streams, 2, groups)),
            pltpu.SemaphoreType.DMA((streams, 2, groups)),
            pltpu.SemaphoreType.DMA((streams, 2, groups)),
        ],
        compiler_params=pltpu.CompilerParams(collective_id=collective_id, has_side_effects=True),
    )(*sends)


def collect_kernel(groups, *refs):
    streams = len(refs) - 11
    parts = refs[:streams]
    back, near_land, other_buf, pair_land, summed = refs[streams : streams + 5]
    near_recv, near_send, swap_recv, swap_send, back_recv, back_send = refs[streams + 5 :]
    section = lax.axis_index("section")
    ex = lax.axis_index("ex")
    em = lax.axis_index("em")
    ep = lax.axis_index("ep")
    ec = lax.axis_index("ec")
    me = ex * 2 + em
    partner = (section, ex, em, 1 - ep, ec)
    sibling = (section, ex, em, ep, 1 - ec)

    def peer(g):
        return (section, g // 2, g % 2, ep, ec)

    barrier = pltpu.get_barrier_semaphore()
    for d in range(1, groups):
        pl.semaphore_signal(barrier, inc=1, device_id=peer((me + d) % groups), device_id_type=MESH_IDS)
    pl.semaphore_signal(barrier, inc=1, device_id=partner, device_id_type=MESH_IDS)
    pl.semaphore_signal(barrier, inc=1, device_id=sibling, device_id_type=MESH_IDS)
    pl.semaphore_wait(barrier, groups + 1)

    def near(s, q, g):
        return pltpu.make_async_remote_copy(
            src_ref=parts[s].at[1 - ec, q, g],
            dst_ref=near_land.at[s, q, g],
            send_sem=near_send.at[s, q, g],
            recv_sem=near_recv.at[s, q, g],
            device_id=sibling,
            device_id_type=MESH_IDS,
        )

    def swap(s, g):
        return pltpu.make_async_remote_copy(
            src_ref=other_buf.at[s, g],
            dst_ref=pair_land.at[s, g],
            send_sem=swap_send.at[s, g],
            recv_sem=swap_recv.at[s, g],
            device_id=partner,
            device_id_type=MESH_IDS,
        )

    def reply(s, g):
        return pltpu.make_async_remote_copy(
            src_ref=summed.at[s, g],
            dst_ref=back.at[s, me],
            send_sem=back_send.at[s, g],
            recv_sem=back_recv.at[s, me],
            device_id=peer(g),
            device_id_type=MESH_IDS,
        )

    def incoming(s, g):
        return pltpu.make_async_remote_copy(
            src_ref=summed.at[s, g],
            dst_ref=back.at[s, g],
            send_sem=back_send.at[s, g],
            recv_sem=back_recv.at[s, g],
            device_id=peer(g),
            device_id_type=MESH_IDS,
        )

    for q in (1, 0):
        for d in range(1, groups + 1):
            for s in range(streams):
                near(s, q, (me + d) % groups).start()
    for d in range(1, groups + 1):
        for s in range(streams):
            g = (me + d) % groups
            near(s, 1, g).wait_recv()
            other_buf[s, g] = (
                parts[s][ec, 1, g].astype(jnp.float32) + near_land[s, 1, g].astype(jnp.float32)
            ).astype(other_buf.dtype)
            swap(s, g).start()
    local = []
    for d in range(1, groups + 1):
        for s in range(streams):
            g = (me + d) % groups
            near(s, 0, g).wait_recv()
            swap(s, g).wait_recv()
            pair = parts[s][ec, 0, g].astype(jnp.float32) + near_land[s, 0, g].astype(jnp.float32)
            summed[s, g] = (pair + pair_land[s, g].astype(jnp.float32)).astype(summed.dtype)
            if d < groups:
                reply(s, g).start()
            else:
                copy = pltpu.make_async_copy(summed.at[s, g], back.at[s, me], back_recv.at[s, me])
                copy.start()
                local.append(copy)
    for s in range(streams):
        local[s].wait()
        for d in range(1, groups):
            incoming(s, (me + d) % groups).wait_recv()
    for s in range(streams):
        for d in range(1, groups + 1):
            g = (me + d) % groups
            swap(s, g).wait_send()
            near(s, 0, g).wait_send()
            near(s, 1, g).wait_send()
        for d in range(1, groups):
            reply(s, (me + d) % groups).wait_send()


def collect_from_holders(*parts):
    streams = len(parts)
    _, _, groups, capacity, features = parts[0].shape
    block = (streams, groups, capacity, features)
    any_spec = pl.BlockSpec(memory_space=pl.ANY)
    back = pl.pallas_call(
        functools.partial(collect_kernel, groups),
        out_shape=jax.ShapeDtypeStruct(block, jnp.bfloat16),
        in_specs=[pl.BlockSpec(memory_space=pltpu.VMEM)] * streams,
        out_specs=any_spec,
        scratch_shapes=[
            pltpu.VMEM((streams, 2, groups, capacity, features), jnp.bfloat16),
            pltpu.VMEM(block, jnp.bfloat16),
            pltpu.VMEM(block, jnp.bfloat16),
            pltpu.VMEM(block, jnp.bfloat16),
            pltpu.SemaphoreType.DMA((streams, 2, groups)),
            pltpu.SemaphoreType.DMA((streams, 2, groups)),
            pltpu.SemaphoreType.DMA((streams, groups)),
            pltpu.SemaphoreType.DMA((streams, groups)),
            pltpu.SemaphoreType.DMA((streams, groups)),
            pltpu.SemaphoreType.DMA((streams, groups)),
        ],
        compiler_params=pltpu.CompilerParams(
            collective_id=1, has_side_effects=True, vmem_limit_bytes=60 * 1024 * 1024
        ),
    )(*parts)
    return [back[s] for s in range(streams)]


def body(
    embedded,
    forward_held,
    forward_route,
    forward_weight,
    loss_cotangent,
    backward_held,
    backward_route,
    backward_weight,
    saved_gate,
    saved_up,
    gate_weight,
    up_weight,
    down_weight,
    steering,
):
    section_count = lax.axis_size("section")
    section_index = lax.axis_index("section")
    group_count = lax.axis_size(GROUP)
    holder_count = lax.axis_size(HOLDERS)
    local_hidden = gate_weight.shape[2]
    expert_count = group_count
    device_count = group_count * holder_count
    capacity = saved_gate.shape[1] // device_count
    feature_count = embedded.shape[1]
    rows_shape = (device_count * capacity, feature_count)
    arriving = shifted(forward_held, "section", 1)[0]
    forward_in = jnp.where(section_index == 0, embedded, arriving)
    returning = shifted(backward_held, "section", -1)[0]
    backward_in = jnp.where(section_index == section_count - 1, loss_cotangent, returning)
    direction = steering[0]
    unit_dir = direction / jnp.sqrt(jnp.sum(direction * direction) + 1e-06)
    weights = (gate_weight[0], up_weight[0], down_weight[0])

    forward_layout = dispatch_layout(forward_route[0, :, 0], expert_count, capacity)
    forward_send = jnp.dot(forward_layout, forward_in, preferred_element_type=jnp.float32).astype(
        jnp.bfloat16
    )

    (forward_rows,) = spread_to_holders(
        forward_send.reshape(expert_count, capacity, feature_count), collective_id=0
    )

    backward_dy = backward_in.astype(jnp.float32)
    along_dir = jnp.sum(backward_dy * unit_dir[None, :], axis=1)
    sent_rows = (
        backward_weight[0][:, None] * (backward_dy - along_dir[:, None] * unit_dir[None, :])
    ).astype(jnp.bfloat16)
    backward_layout = dispatch_layout(backward_route[0, :, 0], expert_count, capacity)
    backward_send = jnp.dot(backward_layout, sent_rows, preferred_element_type=jnp.float32).astype(
        jnp.bfloat16
    )
    (backward_rows,) = spread_to_holders(
        backward_send.reshape(expert_count, capacity, feature_count), collective_id=2
    )

    flip = lax.axis_index("ep") == 1

    def reorder(saved):
        grouped = saved[0].reshape(group_count, 2, 2, capacity, local_hidden).transpose(2, 1, 0, 3, 4)
        grouped = jnp.where(flip, grouped[:, ::-1], grouped)
        return grouped.reshape(device_count * capacity, local_hidden)

    forward_part = expert_forward(forward_rows.reshape(rows_shape), weights)
    backward_part = expert_backward(
        backward_rows.reshape(rows_shape), reorder(saved_gate), reorder(saved_up), weights
    )
    forward_back, backward_back = collect_from_holders(
        forward_part.reshape(2, 2, group_count, capacity, feature_count),
        backward_part.reshape(2, 2, group_count, capacity, feature_count),
    )
    forward_back = forward_back.reshape(expert_count * capacity, feature_count)
    backward_back = backward_back.reshape(expert_count * capacity, feature_count)

    contract = (((0,), (0,)), ((), ()))
    picked = lax.dot_general(forward_layout, forward_back, contract, preferred_element_type=jnp.float32)
    mixed_rows = forward_weight[0][:, None] * picked
    coefficient = jnp.sum(mixed_rows * unit_dir[None, :], axis=1)
    forward_out = (
        forward_in.astype(jnp.float32) + mixed_rows - coefficient[:, None] * unit_dir[None, :]
    ).astype(jnp.bfloat16)
    returned = lax.dot_general(
        backward_layout, backward_back, contract, preferred_element_type=jnp.float32
    )
    backward_out = (backward_dy + returned).astype(jnp.bfloat16)
    return (forward_out[None], coefficient[None], backward_out[None])


def solution(mesh):
    sections = mesh.shape["section"]
    experts = mesh.shape["expert"]
    fine = Mesh(
        np.asarray(mesh.devices).reshape(sections, experts // 8, 2, 2, 2),
        ("section",) + EXPERT_AXES,
    )
    E = EXPERT_AXES
    in_specs = (
        P(E, None),
        P("section", E, None),
        P("section", E, None),
        P("section", E),
        P(E, None),
        P("section", E, None),
        P("section", E, None),
        P("section", E),
        P("section", None, E),
        P("section", None, E),
        P("section", None, E),
        P("section", None, E),
        P("section", E, None),
        P("section", None),
    )
    out_specs = (P("section", E, None), P("section", E), P("section", E, None))
    return jax.shard_map(body, mesh=fine, in_specs=in_specs, out_specs=out_specs, check_vma=False)
```

```python
import functools

import jax
import jax.numpy as jnp
import numpy as np
from jax import lax
from jax.experimental import pallas as pl
from jax.experimental.pallas import tpu as pltpu
from jax.sharding import Mesh
from jax.sharding import PartitionSpec as P

H = 1024
EXPERT_AXES = ("ex", "em", "ep", "ec")
GROUP = ("ex", "em")
HOLDERS = ("ep", "ec")
MESH_IDS = pl.DeviceIdType.MESH


def shifted(value, axis, by):
    devices = lax.axis_size(axis)
    pairs = [(i, i + by) for i in range(devices) if 0 <= i + by < devices]
    return lax.ppermute(value, axis, pairs)


def dispatch_layout(expert_ids, expert_count, capacity):
    onehot = (expert_ids[:, None] == jnp.arange(expert_count, dtype=jnp.int32)[None, :]).astype(
        jnp.int32
    )
    earlier = jnp.cumsum(onehot, axis=0) - onehot
    position = jnp.sum(earlier * onehot, axis=1)
    target = expert_ids * capacity + position
    return (
        jnp.arange(expert_count * capacity, dtype=jnp.int32)[:, None] == target[None, :]
    ).astype(jnp.bfloat16)


def expert_forward(slot_rows, weights):
    gate_cols, up_cols, down_rows = weights
    gate_pre = jnp.dot(slot_rows, gate_cols, preferred_element_type=jnp.float32)
    up_pre = jnp.dot(slot_rows, up_cols, preferred_element_type=jnp.float32)
    hidden = lax.optimization_barrier((jax.nn.silu(gate_pre) * up_pre).astype(jnp.bfloat16))
    return jnp.dot(hidden, down_rows, preferred_element_type=jnp.float32).astype(jnp.bfloat16)


def expert_backward(slot_rows, gate_saved, up_saved, weights):
    gate_cols, up_cols, down_rows = weights
    contract = (((1,), (1,)), ((), ()))
    grad_hidden = lax.dot_general(
        slot_rows, down_rows, contract, preferred_element_type=jnp.float32
    )
    gate_pre = gate_saved.astype(jnp.float32)
    up_pre = up_saved.astype(jnp.float32)
    sigmoid_gate = jax.nn.sigmoid(gate_pre)
    grad_gate = (
        grad_hidden * up_pre * sigmoid_gate * (1.0 + gate_pre * (1.0 - sigmoid_gate))
    ).astype(jnp.bfloat16)
    grad_up = (grad_hidden * gate_pre * sigmoid_gate).astype(jnp.bfloat16)
    grad_gate, grad_up = lax.optimization_barrier((grad_gate, grad_up))
    grads = jnp.concatenate([grad_gate, grad_up], axis=1)
    both_cols = jnp.concatenate([gate_cols, up_cols], axis=1)
    grad_part = lax.dot_general(grads, both_cols, contract, preferred_element_type=jnp.float32)
    return grad_part.astype(jnp.bfloat16)


def swap_pair(value):
    return lax.ppermute(value, "ep", [(0, 1), (1, 0)])


def spread_kernel(groups, *refs):
    streams = (len(refs) - 6) // 2
    sends = refs[:streams]
    rows = refs[streams : 2 * streams]
    first_recv, first_send, pair_recv, pair_send, near_recv, near_send = refs[2 * streams : 2 * streams + 6]
    section = lax.axis_index("section")
    ex = lax.axis_index("ex")
    em = lax.axis_index("em")
    ep = lax.axis_index("ep")
    ec = lax.axis_index("ec")
    me = ex * 2 + em
    partner = (section, ex, em, 1 - ep, ec)
    sibling = (section, ex, em, ep, 1 - ec)

    def peer(g):
        return (section, g // 2, g % 2, ep, ec)

    barrier = pltpu.get_barrier_semaphore()
    for d in range(1, groups):
        pl.semaphore_signal(barrier, inc=1, device_id=peer((me + d) % groups), device_id_type=MESH_IDS)
    pl.semaphore_signal(barrier, inc=1, device_id=partner, device_id_type=MESH_IDS)
    pl.semaphore_signal(barrier, inc=1, device_id=sibling, device_id_type=MESH_IDS)
    pl.semaphore_wait(barrier, groups + 1)

    def first_copy(s, g, target):
        return pltpu.make_async_remote_copy(
            src_ref=sends[s].at[g],
            dst_ref=rows[s].at[ec, 0, me],
            send_sem=first_send.at[s, g],
            recv_sem=first_recv.at[s, me],
            device_id=target,
            device_id_type=MESH_IDS,
        )

    def arrived(s, g):
        return pltpu.make_async_remote_copy(
            src_ref=sends[s].at[g],
            dst_ref=rows[s].at[ec, 0, g],
            send_sem=first_send.at[s, g],
            recv_sem=first_recv.at[s, g],
            device_id=peer(g),
            device_id_type=MESH_IDS,
        )

    def relay(s, q, g, target, recv, send, slot):
        return pltpu.make_async_remote_copy(
            src_ref=rows[s].at[ec, q, g],
            dst_ref=rows[s].at[ec, slot, g],
            send_sem=send.at[s, q, g],
            recv_sem=recv.at[s, q, g],
            device_id=target,
            device_id_type=MESH_IDS,
        )

    local = []
    for s in range(streams):
        copy = pltpu.make_async_copy(sends[s].at[me], rows[s].at[ec, 0, me], first_recv.at[s, me])
        copy.start()
        local.append(copy)
    for d in range(1, groups):
        for s in range(streams):
            g = (me + d) % groups
            first_copy(s, g, peer(g)).start()
    outgoing = []
    for d in range(groups):
        for s in range(streams):
            g = (me + groups - d) % groups
            if d > 0:
                arrived(s, g).wait_recv()
            else:
                local[s].wait()
            for target, recv, send, slot in (
                (partner, pair_recv, pair_send, 1),
                (sibling, near_recv, near_send, 0),
            ):
                copy = relay(s, 0, g, target, recv, send, slot)
                copy.start()
                outgoing.append(copy)
    for d in range(groups):
        for s in range(streams):
            g = (me + groups - d) % groups
            relay(s, 0, g, partner, pair_recv, pair_send, 1).wait_recv()
            copy = relay(s, 1, g, sibling, near_recv, near_send, 1)
            copy.start()
            outgoing.append(copy)
    for s in range(streams):
        for q in range(2):
            for g in range(groups):
                pltpu.make_async_remote_copy(
                    src_ref=rows[s].at[1 - ec, q, g],
                    dst_ref=rows[s].at[1 - ec, q, g],
                    send_sem=near_send.at[s, q, g],
                    recv_sem=near_recv.at[s, q, g],
                    device_id=sibling,
                    device_id_type=MESH_IDS,
                ).wait_recv()
    for s in range(streams):
        for d in range(1, groups):
            g = (me + d) % groups
            first_copy(s, g, peer(g)).wait_send()
    for copy in outgoing:
        copy.wait_send()


def spread_to_holders(*sends):
    groups, capacity, features = sends[0].shape
    streams = len(sends)
    rows = jax.ShapeDtypeStruct((2, 2, groups, capacity, features), sends[0].dtype)
    any_spec = pl.BlockSpec(memory_space=pl.ANY)
    return pl.pallas_call(
        functools.partial(spread_kernel, groups),
        out_shape=[rows] * streams,
        in_specs=[any_spec] * streams,
        out_specs=[any_spec] * streams,
        scratch_shapes=[
            pltpu.SemaphoreType.DMA((streams, groups)),
            pltpu.SemaphoreType.DMA((streams, groups)),
            pltpu.SemaphoreType.DMA((streams, 2, groups)),
            pltpu.SemaphoreType.DMA((streams, 2, groups)),
            pltpu.SemaphoreType.DMA((streams, 2, groups)),
            pltpu.SemaphoreType.DMA((streams, 2, groups)),
        ],
        compiler_params=pltpu.CompilerParams(collective_id=0, has_side_effects=True),
    )(*sends)


def collect_kernel(groups, *refs):
    streams = len(refs) - 11
    parts = refs[:streams]
    back, near_land, other_buf, pair_land, summed = refs[streams : streams + 5]
    near_recv, near_send, swap_recv, swap_send, back_recv, back_send = refs[streams + 5 :]
    section = lax.axis_index("section")
    ex = lax.axis_index("ex")
    em = lax.axis_index("em")
    ep = lax.axis_index("ep")
    ec = lax.axis_index("ec")
    me = ex * 2 + em
    partner = (section, ex, em, 1 - ep, ec)
    sibling = (section, ex, em, ep, 1 - ec)

    def peer(g):
        return (section, g // 2, g % 2, ep, ec)

    barrier = pltpu.get_barrier_semaphore()
    for d in range(1, groups):
        pl.semaphore_signal(barrier, inc=1, device_id=peer((me + d) % groups), device_id_type=MESH_IDS)
    pl.semaphore_signal(barrier, inc=1, device_id=partner, device_id_type=MESH_IDS)
    pl.semaphore_signal(barrier, inc=1, device_id=sibling, device_id_type=MESH_IDS)
    pl.semaphore_wait(barrier, groups + 1)

    def near(s, q, g):
        return pltpu.make_async_remote_copy(
            src_ref=parts[s].at[1 - ec, q, g],
            dst_ref=near_land.at[s, q, g],
            send_sem=near_send.at[s, q, g],
            recv_sem=near_recv.at[s, q, g],
            device_id=sibling,
            device_id_type=MESH_IDS,
        )

    def swap(s, g):
        return pltpu.make_async_remote_copy(
            src_ref=other_buf.at[s, g],
            dst_ref=pair_land.at[s, g],
            send_sem=swap_send.at[s, g],
            recv_sem=swap_recv.at[s, g],
            device_id=partner,
            device_id_type=MESH_IDS,
        )

    def reply(s, g):
        return pltpu.make_async_remote_copy(
            src_ref=summed.at[s, g],
            dst_ref=back.at[s, me],
            send_sem=back_send.at[s, g],
            recv_sem=back_recv.at[s, me],
            device_id=peer(g),
            device_id_type=MESH_IDS,
        )

    def incoming(s, g):
        return pltpu.make_async_remote_copy(
            src_ref=summed.at[s, g],
            dst_ref=back.at[s, g],
            send_sem=back_send.at[s, g],
            recv_sem=back_recv.at[s, g],
            device_id=peer(g),
            device_id_type=MESH_IDS,
        )

    for q in (1, 0):
        for d in range(1, groups + 1):
            for s in range(streams):
                near(s, q, (me + d) % groups).start()
    for d in range(1, groups + 1):
        for s in range(streams):
            g = (me + d) % groups
            near(s, 1, g).wait_recv()
            other_buf[s, g] = (
                parts[s][ec, 1, g].astype(jnp.float32) + near_land[s, 1, g].astype(jnp.float32)
            ).astype(other_buf.dtype)
            swap(s, g).start()
    local = []
    for d in range(1, groups + 1):
        for s in range(streams):
            g = (me + d) % groups
            near(s, 0, g).wait_recv()
            swap(s, g).wait_recv()
            pair = parts[s][ec, 0, g].astype(jnp.float32) + near_land[s, 0, g].astype(jnp.float32)
            summed[s, g] = (pair + pair_land[s, g].astype(jnp.float32)).astype(summed.dtype)
            if d < groups:
                reply(s, g).start()
            else:
                copy = pltpu.make_async_copy(summed.at[s, g], back.at[s, me], back_recv.at[s, me])
                copy.start()
                local.append(copy)
    for s in range(streams):
        local[s].wait()
        for d in range(1, groups):
            incoming(s, (me + d) % groups).wait_recv()
    for s in range(streams):
        for d in range(1, groups + 1):
            g = (me + d) % groups
            swap(s, g).wait_send()
            near(s, 0, g).wait_send()
            near(s, 1, g).wait_send()
        for d in range(1, groups):
            reply(s, (me + d) % groups).wait_send()


def collect_from_holders(*parts):
    streams = len(parts)
    _, _, groups, capacity, features = parts[0].shape
    block = (streams, groups, capacity, features)
    any_spec = pl.BlockSpec(memory_space=pl.ANY)
    back = pl.pallas_call(
        functools.partial(collect_kernel, groups),
        out_shape=jax.ShapeDtypeStruct(block, jnp.bfloat16),
        in_specs=[pl.BlockSpec(memory_space=pltpu.VMEM)] * streams,
        out_specs=any_spec,
        scratch_shapes=[
            pltpu.VMEM((streams, 2, groups, capacity, features), jnp.bfloat16),
            pltpu.VMEM(block, jnp.bfloat16),
            pltpu.VMEM(block, jnp.bfloat16),
            pltpu.VMEM(block, jnp.bfloat16),
            pltpu.SemaphoreType.DMA((streams, 2, groups)),
            pltpu.SemaphoreType.DMA((streams, 2, groups)),
            pltpu.SemaphoreType.DMA((streams, groups)),
            pltpu.SemaphoreType.DMA((streams, groups)),
            pltpu.SemaphoreType.DMA((streams, groups)),
            pltpu.SemaphoreType.DMA((streams, groups)),
        ],
        compiler_params=pltpu.CompilerParams(
            collective_id=1, has_side_effects=True, vmem_limit_bytes=60 * 1024 * 1024
        ),
    )(*parts)
    return [back[s] for s in range(streams)]


def body(
    embedded,
    forward_held,
    forward_route,
    forward_weight,
    loss_cotangent,
    backward_held,
    backward_route,
    backward_weight,
    saved_gate,
    saved_up,
    gate_weight,
    up_weight,
    down_weight,
    steering,
):
    section_count = lax.axis_size("section")
    section_index = lax.axis_index("section")
    group_count = lax.axis_size(GROUP)
    holder_count = lax.axis_size(HOLDERS)
    local_hidden = gate_weight.shape[2]
    expert_count = group_count
    device_count = group_count * holder_count
    capacity = saved_gate.shape[1] // device_count
    feature_count = embedded.shape[1]
    rows_shape = (device_count * capacity, feature_count)
    arriving = shifted(forward_held, "section", 1)[0]
    forward_in = jnp.where(section_index == 0, embedded, arriving)
    returning = shifted(backward_held, "section", -1)[0]
    backward_in = jnp.where(section_index == section_count - 1, loss_cotangent, returning)
    direction = steering[0]
    unit_dir = direction / jnp.sqrt(jnp.sum(direction * direction) + 1e-06)
    weights = (gate_weight[0], up_weight[0], down_weight[0])

    forward_layout = dispatch_layout(forward_route[0, :, 0], expert_count, capacity)
    forward_send = jnp.dot(forward_layout, forward_in, preferred_element_type=jnp.float32).astype(
        jnp.bfloat16
    )

    backward_dy = backward_in.astype(jnp.float32)
    along_dir = jnp.sum(backward_dy * unit_dir[None, :], axis=1)
    sent_rows = (
        backward_weight[0][:, None] * (backward_dy - along_dir[:, None] * unit_dir[None, :])
    ).astype(jnp.bfloat16)
    backward_layout = dispatch_layout(backward_route[0, :, 0], expert_count, capacity)
    backward_send = jnp.dot(backward_layout, sent_rows, preferred_element_type=jnp.float32).astype(
        jnp.bfloat16
    )
    forward_rows, backward_rows = spread_to_holders(
        forward_send.reshape(expert_count, capacity, feature_count),
        backward_send.reshape(expert_count, capacity, feature_count),
    )

    flip = lax.axis_index("ep") == 1

    def reorder(saved):
        grouped = saved[0].reshape(group_count, 2, 2, capacity, local_hidden).transpose(2, 1, 0, 3, 4)
        grouped = jnp.where(flip, grouped[:, ::-1], grouped)
        return grouped.reshape(device_count * capacity, local_hidden)

    forward_part = expert_forward(forward_rows.reshape(rows_shape), weights)
    backward_part = expert_backward(
        backward_rows.reshape(rows_shape), reorder(saved_gate), reorder(saved_up), weights
    )
    forward_back, backward_back = collect_from_holders(
        forward_part.reshape(2, 2, group_count, capacity, feature_count),
        backward_part.reshape(2, 2, group_count, capacity, feature_count),
    )
    forward_back = forward_back.reshape(expert_count * capacity, feature_count)
    backward_back = backward_back.reshape(expert_count * capacity, feature_count)

    contract = (((0,), (0,)), ((), ()))
    picked = lax.dot_general(forward_layout, forward_back, contract, preferred_element_type=jnp.float32)
    mixed_rows = forward_weight[0][:, None] * picked
    coefficient = jnp.sum(mixed_rows * unit_dir[None, :], axis=1)
    forward_out = (
        forward_in.astype(jnp.float32) + mixed_rows - coefficient[:, None] * unit_dir[None, :]
    ).astype(jnp.bfloat16)
    returned = lax.dot_general(
        backward_layout, backward_back, contract, preferred_element_type=jnp.float32
    )
    backward_out = (backward_dy + returned).astype(jnp.bfloat16)
    return (forward_out[None], coefficient[None], backward_out[None])


def solution(mesh):
    sections = mesh.shape["section"]
    experts = mesh.shape["expert"]
    fine = Mesh(
        np.asarray(mesh.devices).reshape(sections, experts // 8, 2, 2, 2),
        ("section",) + EXPERT_AXES,
    )
    E = EXPERT_AXES
    in_specs = (
        P(E, None),
        P("section", E, None),
        P("section", E, None),
        P("section", E),
        P(E, None),
        P("section", E, None),
        P("section", E, None),
        P("section", E),
        P("section", None, E),
        P("section", None, E),
        P("section", None, E),
        P("section", None, E),
        P("section", E, None),
        P("section", None),
    )
    out_specs = (P("section", E, None), P("section", E), P("section", E, None))
    return jax.shard_map(body, mesh=fine, in_specs=in_specs, out_specs=out_specs, check_vma=False)
```

```python
import functools

import jax
import jax.numpy as jnp
import numpy as np
from jax import lax
from jax.experimental import pallas as pl
from jax.experimental.pallas import tpu as pltpu
from jax.sharding import Mesh
from jax.sharding import PartitionSpec as P

H = 1024
EXPERT_AXES = ("ex", "em", "ep", "ec")
GROUP = ("ex", "em")
HOLDERS = ("ep", "ec")
MESH_IDS = pl.DeviceIdType.MESH


def shifted(value, axis, by):
    devices = lax.axis_size(axis)
    pairs = [(i, i + by) for i in range(devices) if 0 <= i + by < devices]
    return lax.ppermute(value, axis, pairs)


def dispatch_layout(expert_ids, expert_count, capacity):
    onehot = (expert_ids[:, None] == jnp.arange(expert_count, dtype=jnp.int32)[None, :]).astype(
        jnp.int32
    )
    earlier = jnp.cumsum(onehot, axis=0) - onehot
    position = jnp.sum(earlier * onehot, axis=1)
    target = expert_ids * capacity + position
    return (
        jnp.arange(expert_count * capacity, dtype=jnp.int32)[:, None] == target[None, :]
    ).astype(jnp.bfloat16)


def expert_forward(slot_rows, weights):
    gate_cols, up_cols, down_rows = weights
    both_pre = jnp.dot(
        slot_rows, jnp.concatenate([gate_cols, up_cols], axis=1), preferred_element_type=jnp.float32
    )
    gate_pre, up_pre = jnp.split(both_pre, 2, axis=1)
    hidden = lax.optimization_barrier((jax.nn.silu(gate_pre) * up_pre).astype(jnp.bfloat16))
    return jnp.dot(hidden, down_rows, preferred_element_type=jnp.float32).astype(jnp.bfloat16)


def expert_backward(slot_rows, gate_saved, up_saved, weights):
    gate_cols, up_cols, down_rows = weights
    contract = (((1,), (1,)), ((), ()))
    grad_hidden = lax.dot_general(
        slot_rows, down_rows, contract, preferred_element_type=jnp.float32
    )
    gate_pre = gate_saved.astype(jnp.float32)
    up_pre = up_saved.astype(jnp.float32)
    sigmoid_gate = jax.nn.sigmoid(gate_pre)
    grad_gate = (
        grad_hidden * up_pre * sigmoid_gate * (1.0 + gate_pre * (1.0 - sigmoid_gate))
    ).astype(jnp.bfloat16)
    grad_up = (grad_hidden * gate_pre * sigmoid_gate).astype(jnp.bfloat16)
    grad_gate, grad_up = lax.optimization_barrier((grad_gate, grad_up))
    grads = jnp.concatenate([grad_gate, grad_up], axis=1)
    both_cols = jnp.concatenate([gate_cols, up_cols], axis=1)
    grad_part = lax.dot_general(grads, both_cols, contract, preferred_element_type=jnp.float32)
    return grad_part.astype(jnp.bfloat16)


def swap_pair(value):
    return lax.ppermute(value, "ep", [(0, 1), (1, 0)])


def spread_kernel(groups, *refs):
    streams = (len(refs) - 6) // 2
    sends = refs[:streams]
    rows = refs[streams : 2 * streams]
    first_recv, first_send, pair_recv, pair_send, near_recv, near_send = refs[2 * streams : 2 * streams + 6]
    section = lax.axis_index("section")
    ex = lax.axis_index("ex")
    em = lax.axis_index("em")
    ep = lax.axis_index("ep")
    ec = lax.axis_index("ec")
    me = ex * 2 + em
    partner = (section, ex, em, 1 - ep, ec)
    sibling = (section, ex, em, ep, 1 - ec)

    def peer(g):
        return (section, g // 2, g % 2, ep, ec)

    barrier = pltpu.get_barrier_semaphore()
    for d in range(1, groups):
        pl.semaphore_signal(barrier, inc=1, device_id=peer((me + d) % groups), device_id_type=MESH_IDS)
    pl.semaphore_signal(barrier, inc=1, device_id=partner, device_id_type=MESH_IDS)
    pl.semaphore_signal(barrier, inc=1, device_id=sibling, device_id_type=MESH_IDS)
    pl.semaphore_wait(barrier, groups + 1)

    def first_copy(s, g, target):
        return pltpu.make_async_remote_copy(
            src_ref=sends[s].at[g],
            dst_ref=rows[s].at[ec, 0, me],
            send_sem=first_send.at[s, g],
            recv_sem=first_recv.at[s, me],
            device_id=target,
            device_id_type=MESH_IDS,
        )

    def arrived(s, g):
        return pltpu.make_async_remote_copy(
            src_ref=sends[s].at[g],
            dst_ref=rows[s].at[ec, 0, g],
            send_sem=first_send.at[s, g],
            recv_sem=first_recv.at[s, g],
            device_id=peer(g),
            device_id_type=MESH_IDS,
        )

    def relay(s, q, g, target, recv, send, slot):
        return pltpu.make_async_remote_copy(
            src_ref=rows[s].at[ec, q, g],
            dst_ref=rows[s].at[ec, slot, g],
            send_sem=send.at[s, q, g],
            recv_sem=recv.at[s, q, g],
            device_id=target,
            device_id_type=MESH_IDS,
        )

    local = []
    for s in range(streams):
        copy = pltpu.make_async_copy(sends[s].at[me], rows[s].at[ec, 0, me], first_recv.at[s, me])
        copy.start()
        local.append(copy)
    for d in range(1, groups):
        for s in range(streams):
            g = (me + d) % groups
            first_copy(s, g, peer(g)).start()
    outgoing = []
    for d in range(groups):
        for s in range(streams):
            g = (me + groups - d) % groups
            if d > 0:
                arrived(s, g).wait_recv()
            else:
                local[s].wait()
            for target, recv, send, slot in (
                (partner, pair_recv, pair_send, 1),
                (sibling, near_recv, near_send, 0),
            ):
                copy = relay(s, 0, g, target, recv, send, slot)
                copy.start()
                outgoing.append(copy)
    for d in range(groups):
        for s in range(streams):
            g = (me + groups - d) % groups
            relay(s, 0, g, partner, pair_recv, pair_send, 1).wait_recv()
            copy = relay(s, 1, g, sibling, near_recv, near_send, 1)
            copy.start()
            outgoing.append(copy)
    for s in range(streams):
        for q in range(2):
            for g in range(groups):
                pltpu.make_async_remote_copy(
                    src_ref=rows[s].at[1 - ec, q, g],
                    dst_ref=rows[s].at[1 - ec, q, g],
                    send_sem=near_send.at[s, q, g],
                    recv_sem=near_recv.at[s, q, g],
                    device_id=sibling,
                    device_id_type=MESH_IDS,
                ).wait_recv()
    for s in range(streams):
        for d in range(1, groups):
            g = (me + d) % groups
            first_copy(s, g, peer(g)).wait_send()
    for copy in outgoing:
        copy.wait_send()


def spread_to_holders(*sends):
    groups, capacity, features = sends[0].shape
    streams = len(sends)
    rows = jax.ShapeDtypeStruct((2, 2, groups, capacity, features), sends[0].dtype)
    any_spec = pl.BlockSpec(memory_space=pl.ANY)
    return pl.pallas_call(
        functools.partial(spread_kernel, groups),
        out_shape=[rows] * streams,
        in_specs=[any_spec] * streams,
        out_specs=[any_spec] * streams,
        scratch_shapes=[
            pltpu.SemaphoreType.DMA((streams, groups)),
            pltpu.SemaphoreType.DMA((streams, groups)),
            pltpu.SemaphoreType.DMA((streams, 2, groups)),
            pltpu.SemaphoreType.DMA((streams, 2, groups)),
            pltpu.SemaphoreType.DMA((streams, 2, groups)),
            pltpu.SemaphoreType.DMA((streams, 2, groups)),
        ],
        compiler_params=pltpu.CompilerParams(collective_id=0, has_side_effects=True),
    )(*sends)


def collect_kernel(groups, *refs):
    streams = len(refs) - 11
    parts = refs[:streams]
    back, near_land, other_buf, pair_land, summed = refs[streams : streams + 5]
    near_recv, near_send, swap_recv, swap_send, back_recv, back_send = refs[streams + 5 :]
    section = lax.axis_index("section")
    ex = lax.axis_index("ex")
    em = lax.axis_index("em")
    ep = lax.axis_index("ep")
    ec = lax.axis_index("ec")
    me = ex * 2 + em
    partner = (section, ex, em, 1 - ep, ec)
    sibling = (section, ex, em, ep, 1 - ec)

    def peer(g):
        return (section, g // 2, g % 2, ep, ec)

    barrier = pltpu.get_barrier_semaphore()
    for d in range(1, groups):
        pl.semaphore_signal(barrier, inc=1, device_id=peer((me + d) % groups), device_id_type=MESH_IDS)
    pl.semaphore_signal(barrier, inc=1, device_id=partner, device_id_type=MESH_IDS)
    pl.semaphore_signal(barrier, inc=1, device_id=sibling, device_id_type=MESH_IDS)
    pl.semaphore_wait(barrier, groups + 1)

    def near(s, q, g):
        return pltpu.make_async_remote_copy(
            src_ref=parts[s].at[1 - ec, q, g],
            dst_ref=near_land.at[s, q, g],
            send_sem=near_send.at[s, q, g],
            recv_sem=near_recv.at[s, q, g],
            device_id=sibling,
            device_id_type=MESH_IDS,
        )

    def swap(s, g):
        return pltpu.make_async_remote_copy(
            src_ref=other_buf.at[s, g],
            dst_ref=pair_land.at[s, g],
            send_sem=swap_send.at[s, g],
            recv_sem=swap_recv.at[s, g],
            device_id=partner,
            device_id_type=MESH_IDS,
        )

    def reply(s, g):
        return pltpu.make_async_remote_copy(
            src_ref=summed.at[s, g],
            dst_ref=back.at[s, me],
            send_sem=back_send.at[s, g],
            recv_sem=back_recv.at[s, me],
            device_id=peer(g),
            device_id_type=MESH_IDS,
        )

    def incoming(s, g):
        return pltpu.make_async_remote_copy(
            src_ref=summed.at[s, g],
            dst_ref=back.at[s, g],
            send_sem=back_send.at[s, g],
            recv_sem=back_recv.at[s, g],
            device_id=peer(g),
            device_id_type=MESH_IDS,
        )

    for q in (1, 0):
        for d in range(1, groups + 1):
            for s in range(streams):
                near(s, q, (me + d) % groups).start()
    for d in range(1, groups + 1):
        for s in range(streams):
            g = (me + d) % groups
            near(s, 1, g).wait_recv()
            other_buf[s, g] = (
                parts[s][ec, 1, g].astype(jnp.float32) + near_land[s, 1, g].astype(jnp.float32)
            ).astype(other_buf.dtype)
            swap(s, g).start()
    local = []
    for d in range(1, groups + 1):
        for s in range(streams):
            g = (me + d) % groups
            near(s, 0, g).wait_recv()
            swap(s, g).wait_recv()
            pair = parts[s][ec, 0, g].astype(jnp.float32) + near_land[s, 0, g].astype(jnp.float32)
            summed[s, g] = (pair + pair_land[s, g].astype(jnp.float32)).astype(summed.dtype)
            if d < groups:
                reply(s, g).start()
            else:
                copy = pltpu.make_async_copy(summed.at[s, g], back.at[s, me], back_recv.at[s, me])
                copy.start()
                local.append(copy)
    for s in range(streams):
        local[s].wait()
        for d in range(1, groups):
            incoming(s, (me + d) % groups).wait_recv()
    for s in range(streams):
        for d in range(1, groups + 1):
            g = (me + d) % groups
            swap(s, g).wait_send()
            near(s, 0, g).wait_send()
            near(s, 1, g).wait_send()
        for d in range(1, groups):
            reply(s, (me + d) % groups).wait_send()


def collect_from_holders(*parts):
    streams = len(parts)
    _, _, groups, capacity, features = parts[0].shape
    block = (streams, groups, capacity, features)
    any_spec = pl.BlockSpec(memory_space=pl.ANY)
    back = pl.pallas_call(
        functools.partial(collect_kernel, groups),
        out_shape=jax.ShapeDtypeStruct(block, jnp.bfloat16),
        in_specs=[pl.BlockSpec(memory_space=pltpu.VMEM)] * streams,
        out_specs=any_spec,
        scratch_shapes=[
            pltpu.VMEM((streams, 2, groups, capacity, features), jnp.bfloat16),
            pltpu.VMEM(block, jnp.bfloat16),
            pltpu.VMEM(block, jnp.bfloat16),
            pltpu.VMEM(block, jnp.bfloat16),
            pltpu.SemaphoreType.DMA((streams, 2, groups)),
            pltpu.SemaphoreType.DMA((streams, 2, groups)),
            pltpu.SemaphoreType.DMA((streams, groups)),
            pltpu.SemaphoreType.DMA((streams, groups)),
            pltpu.SemaphoreType.DMA((streams, groups)),
            pltpu.SemaphoreType.DMA((streams, groups)),
        ],
        compiler_params=pltpu.CompilerParams(
            collective_id=1, has_side_effects=True, vmem_limit_bytes=60 * 1024 * 1024
        ),
    )(*parts)
    return [back[s] for s in range(streams)]


def body(
    embedded,
    forward_held,
    forward_route,
    forward_weight,
    loss_cotangent,
    backward_held,
    backward_route,
    backward_weight,
    saved_gate,
    saved_up,
    gate_weight,
    up_weight,
    down_weight,
    steering,
):
    section_count = lax.axis_size("section")
    section_index = lax.axis_index("section")
    group_count = lax.axis_size(GROUP)
    holder_count = lax.axis_size(HOLDERS)
    local_hidden = gate_weight.shape[2]
    expert_count = group_count
    device_count = group_count * holder_count
    capacity = saved_gate.shape[1] // device_count
    feature_count = embedded.shape[1]
    rows_shape = (device_count * capacity, feature_count)
    arriving = shifted(forward_held, "section", 1)[0]
    forward_in = jnp.where(section_index == 0, embedded, arriving)
    returning = shifted(backward_held, "section", -1)[0]
    backward_in = jnp.where(section_index == section_count - 1, loss_cotangent, returning)
    direction = steering[0]
    unit_dir = direction / jnp.sqrt(jnp.sum(direction * direction) + 1e-06)
    weights = (gate_weight[0], up_weight[0], down_weight[0])

    forward_layout = dispatch_layout(forward_route[0, :, 0], expert_count, capacity)
    forward_send = jnp.dot(forward_layout, forward_in, preferred_element_type=jnp.float32).astype(
        jnp.bfloat16
    )

    backward_dy = backward_in.astype(jnp.float32)
    along_dir = jnp.sum(backward_dy * unit_dir[None, :], axis=1)
    sent_rows = (
        backward_weight[0][:, None] * (backward_dy - along_dir[:, None] * unit_dir[None, :])
    ).astype(jnp.bfloat16)
    backward_layout = dispatch_layout(backward_route[0, :, 0], expert_count, capacity)
    backward_send = jnp.dot(backward_layout, sent_rows, preferred_element_type=jnp.float32).astype(
        jnp.bfloat16
    )
    forward_rows, backward_rows = spread_to_holders(
        forward_send.reshape(expert_count, capacity, feature_count),
        backward_send.reshape(expert_count, capacity, feature_count),
    )

    flip = lax.axis_index("ep") == 1

    def reorder(saved):
        grouped = saved[0].reshape(group_count, 2, 2, capacity, local_hidden).transpose(2, 1, 0, 3, 4)
        grouped = jnp.where(flip, grouped[:, ::-1], grouped)
        return grouped.reshape(device_count * capacity, local_hidden)

    forward_part = expert_forward(forward_rows.reshape(rows_shape), weights)
    backward_part = expert_backward(
        backward_rows.reshape(rows_shape), reorder(saved_gate), reorder(saved_up), weights
    )
    forward_back, backward_back = collect_from_holders(
        forward_part.reshape(2, 2, group_count, capacity, feature_count),
        backward_part.reshape(2, 2, group_count, capacity, feature_count),
    )
    forward_back = forward_back.reshape(expert_count * capacity, feature_count)
    backward_back = backward_back.reshape(expert_count * capacity, feature_count)

    contract = (((0,), (0,)), ((), ()))
    picked = lax.dot_general(forward_layout, forward_back, contract, preferred_element_type=jnp.float32)
    mixed_rows = forward_weight[0][:, None] * picked
    coefficient = jnp.sum(mixed_rows * unit_dir[None, :], axis=1)
    forward_out = (
        forward_in.astype(jnp.float32) + mixed_rows - coefficient[:, None] * unit_dir[None, :]
    ).astype(jnp.bfloat16)
    returned = lax.dot_general(
        backward_layout, backward_back, contract, preferred_element_type=jnp.float32
    )
    backward_out = (backward_dy + returned).astype(jnp.bfloat16)
    return (forward_out[None], coefficient[None], backward_out[None])


def solution(mesh):
    sections = mesh.shape["section"]
    experts = mesh.shape["expert"]
    fine = Mesh(
        np.asarray(mesh.devices).reshape(sections, experts // 8, 2, 2, 2),
        ("section",) + EXPERT_AXES,
    )
    E = EXPERT_AXES
    in_specs = (
        P(E, None),
        P("section", E, None),
        P("section", E, None),
        P("section", E),
        P(E, None),
        P("section", E, None),
        P("section", E, None),
        P("section", E),
        P("section", None, E),
        P("section", None, E),
        P("section", None, E),
        P("section", None, E),
        P("section", E, None),
        P("section", None),
    )
    out_specs = (P("section", E, None), P("section", E), P("section", E, None))
    return jax.shard_map(body, mesh=fine, in_specs=in_specs, out_specs=out_specs, check_vma=False)
```

```python
import functools

import jax
import jax.numpy as jnp
import numpy as np
from jax import lax
from jax.experimental import pallas as pl
from jax.experimental.pallas import tpu as pltpu
from jax.sharding import Mesh
from jax.sharding import PartitionSpec as P

H = 1024
EXPERT_AXES = ("ex", "em", "ep", "ec")
GROUP = ("ex", "em")
HOLDERS = ("ep", "ec")
MESH_IDS = pl.DeviceIdType.MESH


def shifted(value, axis, by):
    devices = lax.axis_size(axis)
    pairs = [(i, i + by) for i in range(devices) if 0 <= i + by < devices]
    return lax.ppermute(value, axis, pairs)


def dispatch_layout(expert_ids, expert_count, capacity):
    onehot = (expert_ids[:, None] == jnp.arange(expert_count, dtype=jnp.int32)[None, :]).astype(
        jnp.int32
    )
    earlier = jnp.cumsum(onehot, axis=0) - onehot
    position = jnp.sum(earlier * onehot, axis=1)
    target = expert_ids * capacity + position
    return (
        jnp.arange(expert_count * capacity, dtype=jnp.int32)[:, None] == target[None, :]
    ).astype(jnp.bfloat16)


def gather_slots(expert_ids, expert_count, capacity, tokens):
    onehot = (expert_ids[:, None] == jnp.arange(expert_count, dtype=jnp.int32)[None, :]).astype(
        jnp.int32
    )
    earlier = jnp.cumsum(onehot, axis=0) - onehot
    position = jnp.sum(earlier * onehot, axis=1)
    target = expert_ids * capacity + position
    count = tokens.shape[0]
    slot_token = jnp.full((expert_count * capacity,), count, jnp.int32).at[target].set(
        jnp.arange(count, dtype=jnp.int32)
    )
    padded = jnp.concatenate([tokens, jnp.zeros((1, tokens.shape[1]), tokens.dtype)], axis=0)
    return padded[slot_token]


def expert_forward(slot_rows, weights):
    gate_cols, up_cols, down_rows = weights
    gate_pre = jnp.dot(slot_rows, gate_cols, preferred_element_type=jnp.float32)
    up_pre = jnp.dot(slot_rows, up_cols, preferred_element_type=jnp.float32)
    hidden = lax.optimization_barrier((jax.nn.silu(gate_pre) * up_pre).astype(jnp.bfloat16))
    return jnp.dot(hidden, down_rows, preferred_element_type=jnp.float32).astype(jnp.bfloat16)


def expert_backward(slot_rows, gate_saved, up_saved, weights):
    gate_cols, up_cols, down_rows = weights
    contract = (((1,), (1,)), ((), ()))
    grad_hidden = lax.dot_general(
        slot_rows, down_rows, contract, preferred_element_type=jnp.float32
    )
    gate_pre = gate_saved.astype(jnp.float32)
    up_pre = up_saved.astype(jnp.float32)
    sigmoid_gate = jax.nn.sigmoid(gate_pre)
    grad_gate = (
        grad_hidden * up_pre * sigmoid_gate * (1.0 + gate_pre * (1.0 - sigmoid_gate))
    ).astype(jnp.bfloat16)
    grad_up = (grad_hidden * gate_pre * sigmoid_gate).astype(jnp.bfloat16)
    grad_gate, grad_up = lax.optimization_barrier((grad_gate, grad_up))
    grads = jnp.concatenate([grad_gate, grad_up], axis=1)
    both_cols = jnp.concatenate([gate_cols, up_cols], axis=1)
    grad_part = lax.dot_general(grads, both_cols, contract, preferred_element_type=jnp.float32)
    return grad_part.astype(jnp.bfloat16)


def swap_pair(value):
    return lax.ppermute(value, "ep", [(0, 1), (1, 0)])


def spread_kernel(groups, *refs):
    streams = (len(refs) - 6) // 2
    sends = refs[:streams]
    rows = refs[streams : 2 * streams]
    first_recv, first_send, pair_recv, pair_send, near_recv, near_send = refs[2 * streams : 2 * streams + 6]
    section = lax.axis_index("section")
    ex = lax.axis_index("ex")
    em = lax.axis_index("em")
    ep = lax.axis_index("ep")
    ec = lax.axis_index("ec")
    me = ex * 2 + em
    partner = (section, ex, em, 1 - ep, ec)
    sibling = (section, ex, em, ep, 1 - ec)

    def peer(g):
        return (section, g // 2, g % 2, ep, ec)

    barrier = pltpu.get_barrier_semaphore()
    for d in range(1, groups):
        pl.semaphore_signal(barrier, inc=1, device_id=peer((me + d) % groups), device_id_type=MESH_IDS)
    pl.semaphore_signal(barrier, inc=1, device_id=partner, device_id_type=MESH_IDS)
    pl.semaphore_signal(barrier, inc=1, device_id=sibling, device_id_type=MESH_IDS)
    pl.semaphore_wait(barrier, groups + 1)

    def first_copy(s, g, target):
        return pltpu.make_async_remote_copy(
            src_ref=sends[s].at[g],
            dst_ref=rows[s].at[ec, 0, me],
            send_sem=first_send.at[s, g],
            recv_sem=first_recv.at[s, me],
            device_id=target,
            device_id_type=MESH_IDS,
        )

    def arrived(s, g):
        return pltpu.make_async_remote_copy(
            src_ref=sends[s].at[g],
            dst_ref=rows[s].at[ec, 0, g],
            send_sem=first_send.at[s, g],
            recv_sem=first_recv.at[s, g],
            device_id=peer(g),
            device_id_type=MESH_IDS,
        )

    def relay(s, q, g, target, recv, send, slot):
        return pltpu.make_async_remote_copy(
            src_ref=rows[s].at[ec, q, g],
            dst_ref=rows[s].at[ec, slot, g],
            send_sem=send.at[s, q, g],
            recv_sem=recv.at[s, q, g],
            device_id=target,
            device_id_type=MESH_IDS,
        )

    local = []
    for s in range(streams):
        copy = pltpu.make_async_copy(sends[s].at[me], rows[s].at[ec, 0, me], first_recv.at[s, me])
        copy.start()
        local.append(copy)
    for d in range(1, groups):
        for s in range(streams):
            g = (me + d) % groups
            first_copy(s, g, peer(g)).start()
    outgoing = []
    for d in range(groups):
        for s in range(streams):
            g = (me + groups - d) % groups
            if d > 0:
                arrived(s, g).wait_recv()
            else:
                local[s].wait()
            for target, recv, send, slot in (
                (partner, pair_recv, pair_send, 1),
                (sibling, near_recv, near_send, 0),
            ):
                copy = relay(s, 0, g, target, recv, send, slot)
                copy.start()
                outgoing.append(copy)
    for d in range(groups):
        for s in range(streams):
            g = (me + groups - d) % groups
            relay(s, 0, g, partner, pair_recv, pair_send, 1).wait_recv()
            copy = relay(s, 1, g, sibling, near_recv, near_send, 1)
            copy.start()
            outgoing.append(copy)
    for s in range(streams):
        for q in range(2):
            for g in range(groups):
                pltpu.make_async_remote_copy(
                    src_ref=rows[s].at[1 - ec, q, g],
                    dst_ref=rows[s].at[1 - ec, q, g],
                    send_sem=near_send.at[s, q, g],
                    recv_sem=near_recv.at[s, q, g],
                    device_id=sibling,
                    device_id_type=MESH_IDS,
                ).wait_recv()
    for s in range(streams):
        for d in range(1, groups):
            g = (me + d) % groups
            first_copy(s, g, peer(g)).wait_send()
    for copy in outgoing:
        copy.wait_send()


def spread_to_holders(*sends):
    groups, capacity, features = sends[0].shape
    streams = len(sends)
    rows = jax.ShapeDtypeStruct((2, 2, groups, capacity, features), sends[0].dtype)
    any_spec = pl.BlockSpec(memory_space=pl.ANY)
    return pl.pallas_call(
        functools.partial(spread_kernel, groups),
        out_shape=[rows] * streams,
        in_specs=[any_spec] * streams,
        out_specs=[any_spec] * streams,
        scratch_shapes=[
            pltpu.SemaphoreType.DMA((streams, groups)),
            pltpu.SemaphoreType.DMA((streams, groups)),
            pltpu.SemaphoreType.DMA((streams, 2, groups)),
            pltpu.SemaphoreType.DMA((streams, 2, groups)),
            pltpu.SemaphoreType.DMA((streams, 2, groups)),
            pltpu.SemaphoreType.DMA((streams, 2, groups)),
        ],
        compiler_params=pltpu.CompilerParams(collective_id=0, has_side_effects=True),
    )(*sends)


def collect_kernel(groups, *refs):
    streams = len(refs) - 11
    parts = refs[:streams]
    back, near_land, other_buf, pair_land, summed = refs[streams : streams + 5]
    near_recv, near_send, swap_recv, swap_send, back_recv, back_send = refs[streams + 5 :]
    section = lax.axis_index("section")
    ex = lax.axis_index("ex")
    em = lax.axis_index("em")
    ep = lax.axis_index("ep")
    ec = lax.axis_index("ec")
    me = ex * 2 + em
    partner = (section, ex, em, 1 - ep, ec)
    sibling = (section, ex, em, ep, 1 - ec)

    def peer(g):
        return (section, g // 2, g % 2, ep, ec)

    barrier = pltpu.get_barrier_semaphore()
    for d in range(1, groups):
        pl.semaphore_signal(barrier, inc=1, device_id=peer((me + d) % groups), device_id_type=MESH_IDS)
    pl.semaphore_signal(barrier, inc=1, device_id=partner, device_id_type=MESH_IDS)
    pl.semaphore_signal(barrier, inc=1, device_id=sibling, device_id_type=MESH_IDS)
    pl.semaphore_wait(barrier, groups + 1)

    def near(s, q, g):
        return pltpu.make_async_remote_copy(
            src_ref=parts[s].at[1 - ec, q, g],
            dst_ref=near_land.at[s, q, g],
            send_sem=near_send.at[s, q, g],
            recv_sem=near_recv.at[s, q, g],
            device_id=sibling,
            device_id_type=MESH_IDS,
        )

    def swap(s, g):
        return pltpu.make_async_remote_copy(
            src_ref=other_buf.at[s, g],
            dst_ref=pair_land.at[s, g],
            send_sem=swap_send.at[s, g],
            recv_sem=swap_recv.at[s, g],
            device_id=partner,
            device_id_type=MESH_IDS,
        )

    def reply(s, g):
        return pltpu.make_async_remote_copy(
            src_ref=summed.at[s, g],
            dst_ref=back.at[s, me],
            send_sem=back_send.at[s, g],
            recv_sem=back_recv.at[s, me],
            device_id=peer(g),
            device_id_type=MESH_IDS,
        )

    def incoming(s, g):
        return pltpu.make_async_remote_copy(
            src_ref=summed.at[s, g],
            dst_ref=back.at[s, g],
            send_sem=back_send.at[s, g],
            recv_sem=back_recv.at[s, g],
            device_id=peer(g),
            device_id_type=MESH_IDS,
        )

    for q in (1, 0):
        for d in range(1, groups + 1):
            for s in range(streams):
                near(s, q, (me + d) % groups).start()
    for d in range(1, groups + 1):
        for s in range(streams):
            g = (me + d) % groups
            near(s, 1, g).wait_recv()
            other_buf[s, g] = (
                parts[s][ec, 1, g].astype(jnp.float32) + near_land[s, 1, g].astype(jnp.float32)
            ).astype(other_buf.dtype)
            swap(s, g).start()
    local = []
    for d in range(1, groups + 1):
        for s in range(streams):
            g = (me + d) % groups
            near(s, 0, g).wait_recv()
            swap(s, g).wait_recv()
            pair = parts[s][ec, 0, g].astype(jnp.float32) + near_land[s, 0, g].astype(jnp.float32)
            summed[s, g] = (pair + pair_land[s, g].astype(jnp.float32)).astype(summed.dtype)
            if d < groups:
                reply(s, g).start()
            else:
                copy = pltpu.make_async_copy(summed.at[s, g], back.at[s, me], back_recv.at[s, me])
                copy.start()
                local.append(copy)
    for s in range(streams):
        local[s].wait()
        for d in range(1, groups):
            incoming(s, (me + d) % groups).wait_recv()
    for s in range(streams):
        for d in range(1, groups + 1):
            g = (me + d) % groups
            swap(s, g).wait_send()
            near(s, 0, g).wait_send()
            near(s, 1, g).wait_send()
        for d in range(1, groups):
            reply(s, (me + d) % groups).wait_send()


def collect_from_holders(*parts):
    streams = len(parts)
    _, _, groups, capacity, features = parts[0].shape
    block = (streams, groups, capacity, features)
    any_spec = pl.BlockSpec(memory_space=pl.ANY)
    back = pl.pallas_call(
        functools.partial(collect_kernel, groups),
        out_shape=jax.ShapeDtypeStruct(block, jnp.bfloat16),
        in_specs=[pl.BlockSpec(memory_space=pltpu.VMEM)] * streams,
        out_specs=any_spec,
        scratch_shapes=[
            pltpu.VMEM((streams, 2, groups, capacity, features), jnp.bfloat16),
            pltpu.VMEM(block, jnp.bfloat16),
            pltpu.VMEM(block, jnp.bfloat16),
            pltpu.VMEM(block, jnp.bfloat16),
            pltpu.SemaphoreType.DMA((streams, 2, groups)),
            pltpu.SemaphoreType.DMA((streams, 2, groups)),
            pltpu.SemaphoreType.DMA((streams, groups)),
            pltpu.SemaphoreType.DMA((streams, groups)),
            pltpu.SemaphoreType.DMA((streams, groups)),
            pltpu.SemaphoreType.DMA((streams, groups)),
        ],
        compiler_params=pltpu.CompilerParams(
            collective_id=1, has_side_effects=True, vmem_limit_bytes=60 * 1024 * 1024
        ),
    )(*parts)
    return [back[s] for s in range(streams)]


def body(
    embedded,
    forward_held,
    forward_route,
    forward_weight,
    loss_cotangent,
    backward_held,
    backward_route,
    backward_weight,
    saved_gate,
    saved_up,
    gate_weight,
    up_weight,
    down_weight,
    steering,
):
    section_count = lax.axis_size("section")
    section_index = lax.axis_index("section")
    group_count = lax.axis_size(GROUP)
    holder_count = lax.axis_size(HOLDERS)
    local_hidden = gate_weight.shape[2]
    expert_count = group_count
    device_count = group_count * holder_count
    capacity = saved_gate.shape[1] // device_count
    feature_count = embedded.shape[1]
    rows_shape = (device_count * capacity, feature_count)
    arriving = shifted(forward_held, "section", 1)[0]
    forward_in = jnp.where(section_index == 0, embedded, arriving)
    returning = shifted(backward_held, "section", -1)[0]
    backward_in = jnp.where(section_index == section_count - 1, loss_cotangent, returning)
    direction = steering[0]
    unit_dir = direction / jnp.sqrt(jnp.sum(direction * direction) + 1e-06)
    weights = (gate_weight[0], up_weight[0], down_weight[0])

    forward_layout = dispatch_layout(forward_route[0, :, 0], expert_count, capacity)
    forward_send = gather_slots(forward_route[0, :, 0], expert_count, capacity, forward_in)

    backward_dy = backward_in.astype(jnp.float32)
    along_dir = jnp.sum(backward_dy * unit_dir[None, :], axis=1)
    sent_rows = (
        backward_weight[0][:, None] * (backward_dy - along_dir[:, None] * unit_dir[None, :])
    ).astype(jnp.bfloat16)
    backward_layout = dispatch_layout(backward_route[0, :, 0], expert_count, capacity)
    backward_send = gather_slots(backward_route[0, :, 0], expert_count, capacity, sent_rows)
    forward_rows, backward_rows = spread_to_holders(
        forward_send.reshape(expert_count, capacity, feature_count),
        backward_send.reshape(expert_count, capacity, feature_count),
    )

    flip = lax.axis_index("ep") == 1

    def reorder(saved):
        grouped = saved[0].reshape(group_count, 2, 2, capacity, local_hidden).transpose(2, 1, 0, 3, 4)
        grouped = jnp.where(flip, grouped[:, ::-1], grouped)
        return grouped.reshape(device_count * capacity, local_hidden)

    forward_part = expert_forward(forward_rows.reshape(rows_shape), weights)
    backward_part = expert_backward(
        backward_rows.reshape(rows_shape), reorder(saved_gate), reorder(saved_up), weights
    )
    forward_back, backward_back = collect_from_holders(
        forward_part.reshape(2, 2, group_count, capacity, feature_count),
        backward_part.reshape(2, 2, group_count, capacity, feature_count),
    )
    forward_back = forward_back.reshape(expert_count * capacity, feature_count)
    backward_back = backward_back.reshape(expert_count * capacity, feature_count)

    contract = (((0,), (0,)), ((), ()))
    picked = lax.dot_general(forward_layout, forward_back, contract, preferred_element_type=jnp.float32)
    mixed_rows = forward_weight[0][:, None] * picked
    coefficient = jnp.sum(mixed_rows * unit_dir[None, :], axis=1)
    forward_out = (
        forward_in.astype(jnp.float32) + mixed_rows - coefficient[:, None] * unit_dir[None, :]
    ).astype(jnp.bfloat16)
    returned = lax.dot_general(
        backward_layout, backward_back, contract, preferred_element_type=jnp.float32
    )
    backward_out = (backward_dy + returned).astype(jnp.bfloat16)
    return (forward_out[None], coefficient[None], backward_out[None])


def solution(mesh):
    sections = mesh.shape["section"]
    experts = mesh.shape["expert"]
    fine = Mesh(
        np.asarray(mesh.devices).reshape(sections, experts // 8, 2, 2, 2),
        ("section",) + EXPERT_AXES,
    )
    E = EXPERT_AXES
    in_specs = (
        P(E, None),
        P("section", E, None),
        P("section", E, None),
        P("section", E),
        P(E, None),
        P("section", E, None),
        P("section", E, None),
        P("section", E),
        P("section", None, E),
        P("section", None, E),
        P("section", None, E),
        P("section", None, E),
        P("section", E, None),
        P("section", None),
    )
    out_specs = (P("section", E, None), P("section", E), P("section", E, None))
    return jax.shard_map(body, mesh=fine, in_specs=in_specs, out_specs=out_specs, check_vma=False)
```

```python
import functools

import jax
import jax.numpy as jnp
import numpy as np
from jax import lax
from jax.experimental import pallas as pl
from jax.experimental.pallas import tpu as pltpu
from jax.sharding import Mesh
from jax.sharding import PartitionSpec as P

H = 1024
EXPERT_AXES = ("ex", "em", "ep", "ec")
GROUP = ("ex", "em")
HOLDERS = ("ep", "ec")
MESH_IDS = pl.DeviceIdType.MESH


def shifted(value, axis, by):
    devices = lax.axis_size(axis)
    pairs = [(i, i + by) for i in range(devices) if 0 <= i + by < devices]
    return lax.ppermute(value, axis, pairs)


def dispatch_layout(expert_ids, expert_count, capacity):
    onehot = (expert_ids[:, None] == jnp.arange(expert_count, dtype=jnp.int32)[None, :]).astype(
        jnp.int32
    )
    earlier = jnp.cumsum(onehot, axis=0) - onehot
    position = jnp.sum(earlier * onehot, axis=1)
    target = expert_ids * capacity + position
    return (
        jnp.arange(expert_count * capacity, dtype=jnp.int32)[:, None] == target[None, :]
    ).astype(jnp.bfloat16)


def expert_forward(slot_rows, weights):
    gate_cols, up_cols, down_rows = weights
    gate_pre = jnp.dot(slot_rows, gate_cols, preferred_element_type=jnp.float32)
    up_pre = jnp.dot(slot_rows, up_cols, preferred_element_type=jnp.float32)
    hidden = lax.optimization_barrier((jax.nn.silu(gate_pre) * up_pre).astype(jnp.bfloat16))
    return jnp.dot(hidden, down_rows, preferred_element_type=jnp.float32).astype(jnp.bfloat16)


def expert_backward(slot_rows, gate_saved, up_saved, weights):
    gate_cols, up_cols, down_rows = weights
    contract = (((1,), (1,)), ((), ()))
    grad_hidden = lax.optimization_barrier(
        lax.dot_general(slot_rows, down_rows, contract, preferred_element_type=jnp.float32)
    )
    gate_pre = gate_saved.astype(jnp.float32)
    up_pre = up_saved.astype(jnp.float32)
    sigmoid_gate = jax.nn.sigmoid(gate_pre)
    grad_gate = (
        grad_hidden * up_pre * sigmoid_gate * (1.0 + gate_pre * (1.0 - sigmoid_gate))
    ).astype(jnp.bfloat16)
    grad_up = (grad_hidden * gate_pre * sigmoid_gate).astype(jnp.bfloat16)
    grad_gate, grad_up = lax.optimization_barrier((grad_gate, grad_up))
    grads = jnp.concatenate([grad_gate, grad_up], axis=1)
    both_cols = jnp.concatenate([gate_cols, up_cols], axis=1)
    grad_part = lax.dot_general(grads, both_cols, contract, preferred_element_type=jnp.float32)
    return grad_part.astype(jnp.bfloat16)


def swap_pair(value):
    return lax.ppermute(value, "ep", [(0, 1), (1, 0)])


def spread_kernel(groups, *refs):
    streams = (len(refs) - 6) // 2
    sends = refs[:streams]
    rows = refs[streams : 2 * streams]
    first_recv, first_send, pair_recv, pair_send, near_recv, near_send = refs[2 * streams : 2 * streams + 6]
    section = lax.axis_index("section")
    ex = lax.axis_index("ex")
    em = lax.axis_index("em")
    ep = lax.axis_index("ep")
    ec = lax.axis_index("ec")
    me = ex * 2 + em
    partner = (section, ex, em, 1 - ep, ec)
    sibling = (section, ex, em, ep, 1 - ec)

    def peer(g):
        return (section, g // 2, g % 2, ep, ec)

    barrier = pltpu.get_barrier_semaphore()
    for d in range(1, groups):
        pl.semaphore_signal(barrier, inc=1, device_id=peer((me + d) % groups), device_id_type=MESH_IDS)
    pl.semaphore_signal(barrier, inc=1, device_id=partner, device_id_type=MESH_IDS)
    pl.semaphore_signal(barrier, inc=1, device_id=sibling, device_id_type=MESH_IDS)
    pl.semaphore_wait(barrier, groups + 1)

    def first_copy(s, g, target):
        return pltpu.make_async_remote_copy(
            src_ref=sends[s].at[g],
            dst_ref=rows[s].at[ec, 0, me],
            send_sem=first_send.at[s, g],
            recv_sem=first_recv.at[s, me],
            device_id=target,
            device_id_type=MESH_IDS,
        )

    def arrived(s, g):
        return pltpu.make_async_remote_copy(
            src_ref=sends[s].at[g],
            dst_ref=rows[s].at[ec, 0, g],
            send_sem=first_send.at[s, g],
            recv_sem=first_recv.at[s, g],
            device_id=peer(g),
            device_id_type=MESH_IDS,
        )

    def relay(s, q, g, target, recv, send, slot):
        return pltpu.make_async_remote_copy(
            src_ref=rows[s].at[ec, q, g],
            dst_ref=rows[s].at[ec, slot, g],
            send_sem=send.at[s, q, g],
            recv_sem=recv.at[s, q, g],
            device_id=target,
            device_id_type=MESH_IDS,
        )

    local = []
    for s in range(streams):
        copy = pltpu.make_async_copy(sends[s].at[me], rows[s].at[ec, 0, me], first_recv.at[s, me])
        copy.start()
        local.append(copy)
    for d in range(1, groups):
        for s in range(streams):
            g = (me + d) % groups
            first_copy(s, g, peer(g)).start()
    outgoing = []
    for d in range(groups):
        for s in range(streams):
            g = (me + groups - d) % groups
            if d > 0:
                arrived(s, g).wait_recv()
            else:
                local[s].wait()
            for target, recv, send, slot in (
                (partner, pair_recv, pair_send, 1),
                (sibling, near_recv, near_send, 0),
            ):
                copy = relay(s, 0, g, target, recv, send, slot)
                copy.start()
                outgoing.append(copy)
    for d in range(groups):
        for s in range(streams):
            g = (me + groups - d) % groups
            relay(s, 0, g, partner, pair_recv, pair_send, 1).wait_recv()
            copy = relay(s, 1, g, sibling, near_recv, near_send, 1)
            copy.start()
            outgoing.append(copy)
    for s in range(streams):
        for q in range(2):
            for g in range(groups):
                pltpu.make_async_remote_copy(
                    src_ref=rows[s].at[1 - ec, q, g],
                    dst_ref=rows[s].at[1 - ec, q, g],
                    send_sem=near_send.at[s, q, g],
                    recv_sem=near_recv.at[s, q, g],
                    device_id=sibling,
                    device_id_type=MESH_IDS,
                ).wait_recv()
    for s in range(streams):
        for d in range(1, groups):
            g = (me + d) % groups
            first_copy(s, g, peer(g)).wait_send()
    for copy in outgoing:
        copy.wait_send()


def spread_to_holders(*sends):
    groups, capacity, features = sends[0].shape
    streams = len(sends)
    rows = jax.ShapeDtypeStruct((2, 2, groups, capacity, features), sends[0].dtype)
    any_spec = pl.BlockSpec(memory_space=pl.ANY)
    return pl.pallas_call(
        functools.partial(spread_kernel, groups),
        out_shape=[rows] * streams,
        in_specs=[any_spec] * streams,
        out_specs=[any_spec] * streams,
        scratch_shapes=[
            pltpu.SemaphoreType.DMA((streams, groups)),
            pltpu.SemaphoreType.DMA((streams, groups)),
            pltpu.SemaphoreType.DMA((streams, 2, groups)),
            pltpu.SemaphoreType.DMA((streams, 2, groups)),
            pltpu.SemaphoreType.DMA((streams, 2, groups)),
            pltpu.SemaphoreType.DMA((streams, 2, groups)),
        ],
        compiler_params=pltpu.CompilerParams(collective_id=0, has_side_effects=True),
    )(*sends)


def collect_kernel(groups, *refs):
    streams = len(refs) - 11
    parts = refs[:streams]
    back, near_land, other_buf, pair_land, summed = refs[streams : streams + 5]
    near_recv, near_send, swap_recv, swap_send, back_recv, back_send = refs[streams + 5 :]
    section = lax.axis_index("section")
    ex = lax.axis_index("ex")
    em = lax.axis_index("em")
    ep = lax.axis_index("ep")
    ec = lax.axis_index("ec")
    me = ex * 2 + em
    partner = (section, ex, em, 1 - ep, ec)
    sibling = (section, ex, em, ep, 1 - ec)

    def peer(g):
        return (section, g // 2, g % 2, ep, ec)

    barrier = pltpu.get_barrier_semaphore()
    for d in range(1, groups):
        pl.semaphore_signal(barrier, inc=1, device_id=peer((me + d) % groups), device_id_type=MESH_IDS)
    pl.semaphore_signal(barrier, inc=1, device_id=partner, device_id_type=MESH_IDS)
    pl.semaphore_signal(barrier, inc=1, device_id=sibling, device_id_type=MESH_IDS)
    pl.semaphore_wait(barrier, groups + 1)

    def near(s, q, g):
        return pltpu.make_async_remote_copy(
            src_ref=parts[s].at[1 - ec, q, g],
            dst_ref=near_land.at[s, q, g],
            send_sem=near_send.at[s, q, g],
            recv_sem=near_recv.at[s, q, g],
            device_id=sibling,
            device_id_type=MESH_IDS,
        )

    def swap(s, g):
        return pltpu.make_async_remote_copy(
            src_ref=other_buf.at[s, g],
            dst_ref=pair_land.at[s, g],
            send_sem=swap_send.at[s, g],
            recv_sem=swap_recv.at[s, g],
            device_id=partner,
            device_id_type=MESH_IDS,
        )

    def reply(s, g):
        return pltpu.make_async_remote_copy(
            src_ref=summed.at[s, g],
            dst_ref=back.at[s, me],
            send_sem=back_send.at[s, g],
            recv_sem=back_recv.at[s, me],
            device_id=peer(g),
            device_id_type=MESH_IDS,
        )

    def incoming(s, g):
        return pltpu.make_async_remote_copy(
            src_ref=summed.at[s, g],
            dst_ref=back.at[s, g],
            send_sem=back_send.at[s, g],
            recv_sem=back_recv.at[s, g],
            device_id=peer(g),
            device_id_type=MESH_IDS,
        )

    for q in (1, 0):
        for d in range(1, groups + 1):
            for s in range(streams):
                near(s, q, (me + d) % groups).start()
    for d in range(1, groups + 1):
        for s in range(streams):
            g = (me + d) % groups
            near(s, 1, g).wait_recv()
            other_buf[s, g] = (
                parts[s][ec, 1, g].astype(jnp.float32) + near_land[s, 1, g].astype(jnp.float32)
            ).astype(other_buf.dtype)
            swap(s, g).start()
    local = []
    for d in range(1, groups + 1):
        for s in range(streams):
            g = (me + d) % groups
            near(s, 0, g).wait_recv()
            swap(s, g).wait_recv()
            pair = parts[s][ec, 0, g].astype(jnp.float32) + near_land[s, 0, g].astype(jnp.float32)
            summed[s, g] = (pair + pair_land[s, g].astype(jnp.float32)).astype(summed.dtype)
            if d < groups:
                reply(s, g).start()
            else:
                copy = pltpu.make_async_copy(summed.at[s, g], back.at[s, me], back_recv.at[s, me])
                copy.start()
                local.append(copy)
    for s in range(streams):
        local[s].wait()
        for d in range(1, groups):
            incoming(s, (me + d) % groups).wait_recv()
    for s in range(streams):
        for d in range(1, groups + 1):
            g = (me + d) % groups
            swap(s, g).wait_send()
            near(s, 0, g).wait_send()
            near(s, 1, g).wait_send()
        for d in range(1, groups):
            reply(s, (me + d) % groups).wait_send()


def collect_from_holders(*parts):
    streams = len(parts)
    _, _, groups, capacity, features = parts[0].shape
    block = (streams, groups, capacity, features)
    any_spec = pl.BlockSpec(memory_space=pl.ANY)
    back = pl.pallas_call(
        functools.partial(collect_kernel, groups),
        out_shape=jax.ShapeDtypeStruct(block, jnp.bfloat16),
        in_specs=[pl.BlockSpec(memory_space=pltpu.VMEM)] * streams,
        out_specs=any_spec,
        scratch_shapes=[
            pltpu.VMEM((streams, 2, groups, capacity, features), jnp.bfloat16),
            pltpu.VMEM(block, jnp.bfloat16),
            pltpu.VMEM(block, jnp.bfloat16),
            pltpu.VMEM(block, jnp.bfloat16),
            pltpu.SemaphoreType.DMA((streams, 2, groups)),
            pltpu.SemaphoreType.DMA((streams, 2, groups)),
            pltpu.SemaphoreType.DMA((streams, groups)),
            pltpu.SemaphoreType.DMA((streams, groups)),
            pltpu.SemaphoreType.DMA((streams, groups)),
            pltpu.SemaphoreType.DMA((streams, groups)),
        ],
        compiler_params=pltpu.CompilerParams(
            collective_id=1, has_side_effects=True, vmem_limit_bytes=60 * 1024 * 1024
        ),
    )(*parts)
    return [back[s] for s in range(streams)]


def body(
    embedded,
    forward_held,
    forward_route,
    forward_weight,
    loss_cotangent,
    backward_held,
    backward_route,
    backward_weight,
    saved_gate,
    saved_up,
    gate_weight,
    up_weight,
    down_weight,
    steering,
):
    section_count = lax.axis_size("section")
    section_index = lax.axis_index("section")
    group_count = lax.axis_size(GROUP)
    holder_count = lax.axis_size(HOLDERS)
    local_hidden = gate_weight.shape[2]
    expert_count = group_count
    device_count = group_count * holder_count
    capacity = saved_gate.shape[1] // device_count
    feature_count = embedded.shape[1]
    rows_shape = (device_count * capacity, feature_count)
    arriving = shifted(forward_held, "section", 1)[0]
    forward_in = jnp.where(section_index == 0, embedded, arriving)
    returning = shifted(backward_held, "section", -1)[0]
    backward_in = jnp.where(section_index == section_count - 1, loss_cotangent, returning)
    direction = steering[0]
    unit_dir = direction / jnp.sqrt(jnp.sum(direction * direction) + 1e-06)
    weights = (gate_weight[0], up_weight[0], down_weight[0])

    forward_layout = dispatch_layout(forward_route[0, :, 0], expert_count, capacity)
    forward_send = jnp.dot(forward_layout, forward_in, preferred_element_type=jnp.float32).astype(
        jnp.bfloat16
    )

    backward_dy = backward_in.astype(jnp.float32)
    along_dir = jnp.sum(backward_dy * unit_dir[None, :], axis=1)
    sent_rows = (
        backward_weight[0][:, None] * (backward_dy - along_dir[:, None] * unit_dir[None, :])
    ).astype(jnp.bfloat16)
    backward_layout = dispatch_layout(backward_route[0, :, 0], expert_count, capacity)
    backward_send = jnp.dot(backward_layout, sent_rows, preferred_element_type=jnp.float32).astype(
        jnp.bfloat16
    )
    forward_rows, backward_rows = spread_to_holders(
        forward_send.reshape(expert_count, capacity, feature_count),
        backward_send.reshape(expert_count, capacity, feature_count),
    )

    flip = lax.axis_index("ep") == 1

    def reorder(saved):
        grouped = saved[0].reshape(group_count, 2, 2, capacity, local_hidden).transpose(2, 1, 0, 3, 4)
        grouped = jnp.where(flip, grouped[:, ::-1], grouped)
        return grouped.reshape(device_count * capacity, local_hidden)

    forward_part = expert_forward(forward_rows.reshape(rows_shape), weights)
    backward_part = expert_backward(
        backward_rows.reshape(rows_shape), reorder(saved_gate), reorder(saved_up), weights
    )
    forward_back, backward_back = collect_from_holders(
        forward_part.reshape(2, 2, group_count, capacity, feature_count),
        backward_part.reshape(2, 2, group_count, capacity, feature_count),
    )
    forward_back = forward_back.reshape(expert_count * capacity, feature_count)
    backward_back = backward_back.reshape(expert_count * capacity, feature_count)

    contract = (((0,), (0,)), ((), ()))
    picked = lax.dot_general(forward_layout, forward_back, contract, preferred_element_type=jnp.float32)
    mixed_rows = forward_weight[0][:, None] * picked
    coefficient = jnp.sum(mixed_rows * unit_dir[None, :], axis=1)
    forward_out = (
        forward_in.astype(jnp.float32) + mixed_rows - coefficient[:, None] * unit_dir[None, :]
    ).astype(jnp.bfloat16)
    returned = lax.dot_general(
        backward_layout, backward_back, contract, preferred_element_type=jnp.float32
    )
    backward_out = (backward_dy + returned).astype(jnp.bfloat16)
    return (forward_out[None], coefficient[None], backward_out[None])


def solution(mesh):
    sections = mesh.shape["section"]
    experts = mesh.shape["expert"]
    fine = Mesh(
        np.asarray(mesh.devices).reshape(sections, experts // 8, 2, 2, 2),
        ("section",) + EXPERT_AXES,
    )
    E = EXPERT_AXES
    in_specs = (
        P(E, None),
        P("section", E, None),
        P("section", E, None),
        P("section", E),
        P(E, None),
        P("section", E, None),
        P("section", E, None),
        P("section", E),
        P("section", None, E),
        P("section", None, E),
        P("section", None, E),
        P("section", None, E),
        P("section", E, None),
        P("section", None),
    )
    out_specs = (P("section", E, None), P("section", E), P("section", E, None))
    return jax.shard_map(body, mesh=fine, in_specs=in_specs, out_specs=out_specs, check_vma=False)
```
